32 devices in a mesh: dp: 8 (over y, x, core), tensor: 4 (over z).
Axes of the slice: x: 2, y: 2, z: 4, core: 2. Of those that a mesh axis runs over, the one named last changes fastest.
Arguments:
- tokens: bfloat16 [24576, 1536], P(('dp', 'tensor')), may hold values from -6 to 6
- query_weight: bfloat16 [1536, 1536], P('dp', 'tensor'), may hold values from -0.15625 to 0.15625
- key_weight: bfloat16 [1536, 1536], P('dp', 'tensor'), may hold values from -0.15625 to 0.15625
- value_weight: bfloat16 [1536, 1536], P('dp', 'tensor'), may hold values from -0.15625 to 0.15625
- gate_weight: bfloat16 [1536, 1536], P('dp', 'tensor'), may hold values from -0.15625 to 0.15625
- output_weight: bfloat16 [1536, 1536], P('tensor', 'dp'), may hold values from -1 to 1
- memory_in: bfloat16 [1536, 6144], P('dp', 'tensor'), may hold values from -0.15625 to 0.15625
- memory_out: bfloat16 [6144, 1536], P('tensor', 'dp'), may hold values from -0.078125 to 0.078125
- swiglu_gate: bfloat16 [1536, 4096], P('dp', 'tensor'), may hold values from -0.15625 to 0.15625
- swiglu_up: bfloat16 [1536, 4096], P('dp', 'tensor'), may hold values from -0.15625 to 0.15625
- swiglu_down: bfloat16 [4096, 1536], P('tensor', 'dp'), may hold values from -0.09375 to 0.09375
- conv_query: float32 [4, 1536], P(None, 'tensor'), may hold values from -3 to 3
- conv_key: float32 [4, 1536], P(None, 'tensor'), may hold values from -3 to 3
- conv_value: float32 [4, 1536], P(None, 'tensor'), may hold values from -3 to 3
- persist_key: float32 [64, 1536], P(None, 'tensor'), may hold values from -5 to 5
- persist_value: float32 [64, 1536], P(None, 'tensor'), may hold values from -5 to 5
- momentum: float32 [16], P('tensor'), may hold values from 0.3 to 0.9
- step_size: float32 [16], P('tensor'), may hold values from 0.03 to 0.15
- decay_rate: float32 [16], P('tensor'), may hold values from 0.02 to 0.3
- norm_attn: float32 [1536], replicated, may hold values from 0.5 to 1.5
- norm_swiglu: float32 [1536], replicated, may hold values from 0.5 to 1.5
- seq_lengths: int32 [8, 2], P('dp'), may hold values from 768 to 1536, as said below
- deal_order: int32 [8, 24], P('dp'), may hold values from 0 to 23, each once within a row
- cotangent: bfloat16 [24576, 1536], P(('dp', 'tensor')), may hold values from -6 to 6
Outputs:
- layer_out: bfloat16 [24576, 1536], P(('dp', 'tensor'))
- grad_tokens: float32 [24576, 1536], P(('dp', 'tensor'))
- grad_query: float32 [1536, 1536], P('dp', 'tensor')
- grad_key: float32 [1536, 1536], P('dp', 'tensor')
- grad_value: float32 [1536, 1536], P('dp', 'tensor')
- grad_gate: float32 [1536, 1536], P('dp', 'tensor')
- grad_output: float32 [1536, 1536], P('tensor', 'dp')
- grad_memory_in: float32 [1536, 6144], P('dp', 'tensor')
- grad_memory_out: float32 [6144, 1536], P('tensor', 'dp')
- grad_swiglu_gate: float32 [1536, 4096], P('dp', 'tensor')
- grad_swiglu_up: float32 [1536, 4096], P('dp', 'tensor')
- grad_swiglu_down: float32 [4096, 1536], P('tensor', 'dp')
- grad_conv_query: float32 [4, 1536], P(None, 'tensor')
- grad_conv_key: float32 [4, 1536], P(None, 'tensor')
- grad_conv_value: float32 [4, 1536], P(None, 'tensor')
- grad_persist_key: float32 [64, 1536], P(None, 'tensor')
- grad_persist_value: float32 [64, 1536], P(None, 'tensor')
- grad_momentum: float32 [16], P('tensor')
- grad_step_size: float32 [16], P('tensor')
- grad_decay_rate: float32 [16], P('tensor')
- grad_norm_attn: float32 [1536], replicated
- grad_norm_swiglu: float32 [1536], replicated
The draws below stay inside these ranges and needn't reach their ends.
Inputs may be any that keep to these rules, and one draw needn't show every extreme that they name: `seq_lengths`: row g gives the 2 live lengths of group g's slots; they sum to 2304 and one is exactly 1536. `deal_order`: each row is a permutation of the 24 blocks of its group.
All inputs are finite; a program needn't handle non-finite values.
Results may differ from the reference program's by a relative error of at most 0.019.
Values may be sent and summed in bfloat16 or wider, within the bound.
No kernel may reach another device: no remote copies, remote signals or barrier semaphores. Data moves between devices by JAX's collectives and lax.ppermute only.
A program may use at most 384 MiB of HBM per device.

```python
import math
import jax
import jax.numpy as jnp
from jax import lax

D = 1536
H = 16
DH = 96
MEMH = 6144
FFH = 4096
NP = 64
CH = 512
KC = 4
SLOT = 1536
BLK = 128
SEQ_GRP = 2
NCH = 3
NBG = 24
TOKENS = 24576
N_DP = 8


def draw_seq_lengths(key, part):
    half_slot = SLOT // 2

    def one_row(row_key):
        weight_key, order_key = jax.random.split(row_key)
        shares = jax.random.randint(weight_key, (SEQ_GRP - 1,), 1, 17)
        deficits = shares * half_slot // jnp.sum(shares)
        deficits = deficits.at[0].add(half_slot - jnp.sum(deficits))
        lengths = jnp.concatenate([jnp.full((1,), SLOT, jnp.int32), (SLOT - deficits).astype(jnp.int32)])
        return jax.random.permutation(order_key, lengths)
    return jax.vmap(one_row)(jax.random.split(key, N_DP))


def steps_of(own_key, extent, shards, smallest, largest):
    level, own = 1.0, jax.random.fold_in(own_key, 6)
    for axis_at, parts in shards:
        steps = jnp.exp(jax.random.uniform(jax.random.fold_in(own, axis_at), (parts,), jnp.float32, smallest / len(shards), largest / len(shards)))
        level = level * jnp.repeat(steps, extent[axis_at] // parts).reshape([-1 if axis == axis_at else 1 for axis in range(len(extent))])
    return level


def normal_values(stream_key, extent, spread, reach, cuts=(), kind=jnp.bfloat16):
    array = spread * jax.random.normal(stream_key, extent, jnp.float32)
    if cuts:
        array = array * steps_of(stream_key, extent, cuts, -0.22, 0.18)
    return jnp.clip(array, -reach, reach).astype(kind)


def setup_inputs(seed: int = 0) -> dict:
    streams_of = jax.random.split(jax.random.key(seed), 25)
    return {
        "tokens": normal_values(streams_of[0], (TOKENS, D), 1.0, 6.0, ((0, 32),)),
        "query_weight": normal_values(streams_of[1], (D, D), D ** -0.5, 0.15625, ((0, 8), (1, 4))),
        "key_weight": normal_values(streams_of[2], (D, D), D ** -0.5, 0.15625, ((0, 8), (1, 4))),
        "value_weight": normal_values(streams_of[3], (D, D), D ** -0.5, 0.15625, ((0, 8), (1, 4))),
        "gate_weight": normal_values(streams_of[4], (D, D), D ** -0.5, 0.15625, ((0, 8), (1, 4))),
        "output_weight": normal_values(streams_of[5], (D, D), (D // 48) ** -0.5, 1.0, ((0, 4), (1, 8))),
        "memory_in": normal_values(streams_of[6], (D, MEMH), D ** -0.5, 0.15625, ((0, 8), (1, 4))),
        "memory_out": normal_values(streams_of[7], (MEMH, D), MEMH ** -0.5, 0.078125, ((0, 4), (1, 8))),
        "swiglu_gate": normal_values(streams_of[8], (D, FFH), D ** -0.5, 0.15625, ((0, 8), (1, 4))),
        "swiglu_up": normal_values(streams_of[9], (D, FFH), D ** -0.5, 0.15625, ((0, 8), (1, 4))),
        "swiglu_down": normal_values(streams_of[10], (FFH, D), FFH ** -0.5, 0.09375, ((0, 4), (1, 8))),
        "conv_query": normal_values(streams_of[11], (KC, D), 0.6, 3.0, ((1, 4),), jnp.float32),
        "conv_key": normal_values(streams_of[12], (KC, D), 0.6, 3.0, ((1, 4),), jnp.float32),
        "conv_value": normal_values(streams_of[13], (KC, D), 0.6, 3.0, ((1, 4),), jnp.float32),
        "persist_key": normal_values(streams_of[14], (NP, D), 1.0, 5.0, ((1, 4),), jnp.float32),
        "persist_value": normal_values(streams_of[15], (NP, D), 1.0, 5.0, ((1, 4),), jnp.float32),
        "momentum": jnp.clip(jnp.exp(math.log(0.9) - 1.0986122 * jax.random.uniform(streams_of[16], (H,), jnp.float32) ** steps_of(streams_of[16], (H,), ((0, 4),), -0.2, 0.2)), 0.3, 0.9),
        "step_size": jnp.clip(jnp.exp(math.log(0.15) - 1.609438 * jax.random.uniform(streams_of[17], (H,), jnp.float32) ** steps_of(streams_of[17], (H,), ((0, 4),), -0.2, 0.2)), 0.03, 0.15),
        "decay_rate": jnp.clip(jnp.exp(math.log(0.3) - 2.7080503 * jax.random.uniform(streams_of[18], (H,), jnp.float32) ** steps_of(streams_of[18], (H,), ((0, 4),), -0.2, 0.2)), 0.02, 0.3),
        "norm_attn": jnp.clip(1.0 + 0.1 * jax.random.normal(streams_of[19], (D,), jnp.float32), 0.5, 1.5),
        "norm_swiglu": jnp.clip(1.0 + 0.1 * jax.random.normal(streams_of[20], (D,), jnp.float32), 0.5, 1.5),
        "seq_lengths": draw_seq_lengths(jax.random.fold_in(streams_of[24], 71), 0),
        "deal_order": jax.vmap(lambda own: jax.random.permutation(own, NBG))(jax.random.split(streams_of[22], N_DP)).reshape((N_DP, NBG)).astype(jnp.int32),
        "cotangent": normal_values(streams_of[23], (TOKENS, D), 1.0, 6.0, ((0, 32),)),
    }


EPS = 1e-06
HIGH = lax.Precision.HIGHEST
MASKED = -1e+30

@jax.custom_vjp
def low(v):
    return lax.optimization_barrier(v.astype(jnp.bfloat16)).astype(jnp.float32)

@jax.custom_vjp
def low_back(v):
    return v

def low_keep(v):
    return (low(v), None)

def low_pass(kept, grad):
    return (grad,)

def back_keep(v):
    return (v, None)

def back_low(kept, grad):
    return (low(grad),)
low.defvjp(low_keep, low_pass)
low_back.defvjp(back_keep, back_low)

def matmul(first_op, second_op):
    return jnp.dot(first_op, second_op, precision=HIGH)

def rms_rows(values, gain):
    inv_rms = lax.rsqrt(lax.optimization_barrier(jnp.mean(values * values, axis=-1, keepdims=True)) + EPS)
    return values * inv_rms * gain

def head_norm(values):
    return values * lax.rsqrt(lax.optimization_barrier(jnp.mean(values * values, axis=-1, keepdims=True)) + EPS)

def causal_conv(values, kernel):
    feat_width = values.shape[-1]
    by_slot = values.reshape(SEQ_GRP, SLOT, feat_width)
    padded = jnp.pad(by_slot, ((0, 0), (KC - 1, 0), (0, 0)))
    summed = jnp.zeros_like(by_slot)
    for offset in range(KC):
        summed = summed + kernel[offset] * padded[:, KC - 1 - offset:KC - 1 - offset + SLOT]
    return summed.reshape(-1, feat_width)

def block_reorder(rows_in, block_order):
    feat_width = rows_in.shape[-1]
    blocks = rows_in.reshape(-1, BLK, feat_width)
    return jnp.take(blocks, block_order, axis=0).reshape(-1, feat_width)

def group_live(lengths_row):
    positions = jnp.arange(SEQ_GRP * SLOT, dtype=jnp.int32)
    per_slot = (positions // SLOT)[:, None] == jnp.arange(SEQ_GRP, dtype=jnp.int32)[None, :]
    length_of = lax.optimization_barrier(jnp.sum(jnp.where(per_slot, lengths_row[None, :], 0), axis=1))
    return (positions % SLOT < length_of).astype(jnp.float32)

def key_mask(live_blk):
    rows_idx = jnp.arange(CH, dtype=jnp.int32)
    causal = (rows_idx[None, :] <= rows_idx[:, None]) & (live_blk[None, :] > 0.5)
    return jnp.concatenate([jnp.ones((CH, NP), dtype=bool), causal], axis=1)

def memory_chain(query_heads, key_heads, value_heads, live_rows, momentum, step_size, decay_rate):
    heads_here = query_heads.shape[1]
    unit_scale = DH ** (-0.5)
    query_c = (query_heads * unit_scale).reshape(SEQ_GRP, NCH, CH, heads_here, DH)
    key_c = (key_heads * unit_scale).reshape(SEQ_GRP, NCH, CH, heads_here, DH)
    value_c = value_heads.reshape(SEQ_GRP, NCH, CH, heads_here, DH)
    live_c = live_rows.reshape(SEQ_GRP, NCH, CH)
    memory = jnp.zeros((SEQ_GRP, heads_here, DH, DH), jnp.float32)
    surprise = jnp.zeros((SEQ_GRP, heads_here, DH, DH), jnp.float32)
    mom_b = momentum[None, :, None, None]
    step_b = step_size[None, :, None, None]
    decay_b = decay_rate[None, :, None, None]
    read_list = []
    for span_idx in range(NCH):
        read_list.append(jnp.einsum('shij,schj->schi', memory, query_c[:, span_idx], precision=HIGH))
        if span_idx < NCH - 1:
            keys_now = key_c[:, span_idx]
            errors = (jnp.einsum('shij,schj->schi', memory, keys_now, precision=HIGH) - value_c[:, span_idx]) * live_c[:, span_idx][:, :, None, None]
            update = jnp.einsum('schi,schj->shij', errors, keys_now, precision=HIGH)
            surprise = mom_b * surprise - step_b * update
            memory = (1.0 - decay_b) * memory + surprise
    return jnp.stack(read_list, axis=1).reshape(-1, heads_here, DH)

def attend_block(block_in, persist_keys, persist_vals):
    queries, keys_blk, vals_blk, live_blk = block_in
    all_keys = jnp.concatenate([persist_keys, keys_blk], axis=0)
    all_vals = jnp.concatenate([persist_vals, vals_blk], axis=0)
    scores = low_back(jnp.einsum('qhd,khd->hqk', queries, all_keys, precision=HIGH) * DH ** (-0.5))
    scores = jnp.where(key_mask(live_blk)[None], scores, MASKED)
    row_max = lax.optimization_barrier(jnp.max(scores, axis=-1, keepdims=True))
    shifted = jnp.exp(scores - row_max)
    probs = low(shifted / lax.optimization_barrier(jnp.sum(shifted, axis=-1, keepdims=True)))
    return low_back(jnp.einsum('hqk,khd->qhd', probs, all_vals, precision=HIGH))

def group_layer(tokens_g, lengths_g, deal_g, weights):
    query_weight, key_weight, value_weight, gate_weight, output_weight, memory_in, memory_out, swiglu_gate, swiglu_up, swiglu_down, conv_query, conv_key, conv_value, persist_key, persist_value, momentum, step_size, decay_rate, norm_attn, norm_swiglu = weights
    ordered = block_reorder(tokens_g, jnp.argsort(deal_g))
    live_rows = group_live(lengths_g)
    normed = low(rms_rows(ordered, norm_attn))
    query_pre = low_back(matmul(normed, query_weight))
    key_pre = low_back(matmul(normed, key_weight))
    value_pre = low_back(matmul(normed, value_weight))
    gate_pre = low_back(matmul(normed, gate_weight))
    query_heads = low(head_norm(causal_conv(query_pre, conv_query).reshape(-1, H, DH)))
    key_heads = low(head_norm(causal_conv(key_pre, conv_key).reshape(-1, H, DH)))
    value_heads = low(causal_conv(value_pre, conv_value).reshape(-1, H, DH))
    persist_keys = low(head_norm(persist_key.reshape(NP, H, DH)))
    persist_vals = low(persist_value.reshape(NP, H, DH))
    read_rows = memory_chain(query_heads, key_heads, value_heads, live_rows, momentum, step_size, decay_rate)
    block_count = SEQ_GRP * NCH
    block_fn = jax.checkpoint(lambda block_in: attend_block(block_in, persist_keys, persist_vals))
    attended = lax.map(block_fn, (query_heads.reshape(block_count, CH, H, DH), key_heads.reshape(block_count, CH, H, DH), value_heads.reshape(block_count, CH, H, DH), live_rows.reshape(block_count, CH)))
    combined = low((attended.reshape(-1, H, DH) + read_rows).reshape(-1, D) * jax.nn.sigmoid(gate_pre))
    mem_hidden = low(jax.nn.silu(low_back(matmul(normed, memory_in))))
    branch = low_back(matmul(combined, output_weight) + matmul(mem_hidden, memory_out))
    mid_rows = ordered + live_rows[:, None] * branch
    swiglu_in = low(rms_rows(mid_rows, norm_swiglu))
    sw_gate = low_back(matmul(swiglu_in, swiglu_gate))
    sw_up = low_back(matmul(swiglu_in, swiglu_up))
    hidden = low(jax.nn.silu(sw_gate) * sw_up)
    swiglu_out = low_back(matmul(hidden, swiglu_down))
    out_rows = mid_rows + live_rows[:, None] * swiglu_out
    return block_reorder(out_rows, deal_g)

def reference(tokens, query_weight, key_weight, value_weight, gate_weight, output_weight, memory_in, memory_out, swiglu_gate, swiglu_up, swiglu_down, conv_query, conv_key, conv_value, persist_key, persist_value, momentum, step_size, decay_rate, norm_attn, norm_swiglu, seq_lengths, deal_order, cotangent):
    params = tuple((weight.astype(jnp.float32) for weight in (query_weight, key_weight, value_weight, gate_weight, output_weight, memory_in, memory_out, swiglu_gate, swiglu_up, swiglu_down, conv_query, conv_key, conv_value, persist_key, persist_value, momentum, step_size, decay_rate, norm_attn, norm_swiglu)))

    def forward(token_rows, weights):
        grouped = token_rows.reshape(N_DP, SEQ_GRP * SLOT, D)
        layer_fn = jax.checkpoint(group_layer)

        def one_group(carry, inputs):
            return (carry, layer_fn(inputs[0], inputs[1], inputs[2], weights))
        carry_out, outputs = lax.scan(one_group, jnp.zeros((), jnp.float32), (grouped, seq_lengths, deal_order))
        return outputs.reshape(-1, D)
    result, pullback = jax.vjp(forward, tokens.astype(jnp.float32), params)
    grad_rows, grad_params = pullback(cotangent.astype(jnp.float32))
    return (result.astype(jnp.bfloat16), grad_rows) + tuple(grad_params)
```

```python
import functools

import jax
import jax.numpy as jnp
from jax import lax
from jax.experimental import pallas as pl
from jax.experimental.pallas import tpu as pltpu
from jax.sharding import PartitionSpec as P

DH = 96
HP = 128
NP = 64
CH = 512
KC = 4
SLOT = 1536
SHORT = 768
LIVE = SLOT + SHORT
BLK = 128
SUB = 256
NSUB = LIVE // SUB
LONG_SUBS = SLOT // SUB
SLOT_BLKS = SLOT // BLK
SHORT_BLKS = SHORT // BLK
PAD_ROWS = LIVE + 24
EPS = 1e-06
KAPPA = DH ** (-0.5)
VMEM = 56 * 1024 * 1024

F32 = jnp.float32
BF16 = jnp.bfloat16


def dot_nn(a, b):
    return lax.dot_general(a, b, (((1,), (0,)), ((), ())), preferred_element_type=F32)


def dot_nt(a, b):
    return lax.dot_general(a, b, (((1,), (1,)), ((), ())), preferred_element_type=F32)


def dot_tn(a, b):
    return lax.dot_general(a, b, (((0,), (0,)), ((), ())), preferred_element_type=F32)


def gather_kernel(count, rows, normed, idx_ref, *refs):
    ins, rest = refs[:count], refs[count:]
    out = rest[-1]
    for i in range(count):
        block = ins[i][...]
        if normed:
            wide = block.astype(F32)
            inv = lax.rsqrt(jnp.mean(wide * wide, axis=-1, keepdims=True) + EPS)
            block = (wide * inv * rest[0][...]).astype(BF16)
        out[pl.ds(i * rows, rows), :] = block


def gather_rows(source, index, rows, count, gain=None):
    width = source.shape[1]
    steps = index.shape[0] // count
    in_specs = [
        pl.BlockSpec((rows, width), functools.partial(lambda j, i, idx: (idx[i * count + j], 0), j))
        for j in range(count)
    ]
    args = [source] * count
    if gain is not None:
        in_specs.append(pl.BlockSpec((1, width), lambda i, idx: (0, 0)))
        args.append(gain[None, :])
    return pl.pallas_call(
        functools.partial(gather_kernel, count, rows, gain is not None),
        grid_spec=pltpu.PrefetchScalarGridSpec(
            num_scalar_prefetch=1,
            grid=(steps,),
            in_specs=in_specs,
            out_specs=pl.BlockSpec((count * rows, width), lambda i, idx: (i, 0)),
        ),
        out_shape=jax.ShapeDtypeStruct((index.shape[0] * rows, width), source.dtype),
        compiler_params=pltpu.CompilerParams(vmem_limit_bytes=VMEM),
        name="gather_rows",
    )(index, *args)


def pad_base(step):
    return pl.multiple_of(8 + SUB * step + jnp.where(step >= LONG_SUBS, 8, 0), 8)


def load_padded(offs, chunk, src_ref, pad_ref):
    zero = jnp.zeros((8, HP), F32)
    pad_ref[0:8, :] = zero
    pad_ref[8 + SLOT : 16 + SLOT, :] = zero
    pad_ref[16 + LIVE : 24 + LIVE, :] = zero
    piece = 32
    for q in range(LIVE // chunk):
        start = q * chunk
        for first in range(0, chunk, piece):
            row = start + first
            pad_ref[pl.ds(8 + row + (8 if row >= SLOT else 0), piece), :] = src_ref[
                pl.ds(pl.multiple_of(offs[q] + first, piece), piece), :
            ].astype(F32)


def load_natural(offs, chunk, src_ref, dst_ref):
    for q in range(LIVE // chunk):
        dst_ref[pl.ds(q * chunk, chunk), :] = src_ref[
            pl.ds(pl.multiple_of(offs[q], 32), chunk), :
        ].astype(dst_ref.dtype)


def store_rel(offs, chunk, src_ref, dst_ref):
    for q in range(LIVE // chunk):
        dst_ref[pl.ds(pl.multiple_of(offs[q], 32), chunk), :] = src_ref[
            pl.ds(q * chunk, chunk), :
        ].astype(dst_ref.dtype)


def conv_rows(pad_ref, taps, base):
    window = pad_ref[pl.ds(pl.multiple_of(base - 8, 8), SUB + 8), :]
    total = taps[0:1, :] * window[8:, :]
    for j in range(1, KC):
        total = total + taps[j : j + 1, :] * window[8 - j : 8 - j + SUB, :]
    return total


def inv_head(values):
    return lax.rsqrt(jnp.sum(values * values, axis=-1, keepdims=True) * (1.0 / DH) + EPS)


def head_back(values, inv, grad):
    normed = values * inv
    return inv * (grad - normed * (jnp.sum(grad * normed, axis=-1, keepdims=True) * (1.0 / DH)))


def with_ones(values):
    lane = lax.broadcasted_iota(jnp.int32, values.shape, 1)
    return jnp.where(lane == DH, 1.0, values.astype(F32)).astype(BF16)


def causal(shape):
    return lax.broadcasted_iota(jnp.int32, shape, 1) <= lax.broadcasted_iota(jnp.int32, shape, 0)


def split2(values):
    high = values.astype(BF16)
    return high, (values - high.astype(F32)).astype(BF16)


def forward_kernel(
    chunk,
    offs,
    mom_ref,
    step_ref,
    decay_ref,
    qp_ref,
    kp_ref,
    vp_ref,
    gp_ref,
    cq_ref,
    ck_ref,
    cv_ref,
    pk_ref,
    pv_ref,
    o_ref,
    a_ref,
    state_ref,
    qpad,
    kpad,
    vpad,
    q_s,
    k_s,
    v_s,
    r_s,
    g_s,
):
    head = pl.program_id(0)
    load_padded(offs, chunk, qp_ref, qpad)
    load_padded(offs, chunk, kp_ref, kpad)
    load_padded(offs, chunk, vp_ref, vpad)
    load_natural(offs, chunk, gp_ref, g_s)
    taps_q, taps_k, taps_v = cq_ref[...], ck_ref[...], cv_ref[...]

    def prepare(step, carry):
        base = pad_base(step)
        rows = pl.ds(pl.multiple_of(step * SUB, SUB), SUB)
        qc = conv_rows(qpad, taps_q, base)
        q_s[rows, :] = (qc * inv_head(qc)).astype(BF16)
        kc = conv_rows(kpad, taps_k, base)
        k_s[rows, :] = (kc * inv_head(kc)).astype(BF16)
        v_s[rows, :] = conv_rows(vpad, taps_v, base).astype(BF16)
        return carry

    lax.fori_loop(0, NSUB, prepare, 0)
    pkv = pk_ref[...]
    pk = (pkv * inv_head(pkv)).astype(BF16)
    pv1 = with_ones(pv_ref[...])

    mom, eta, decay = mom_ref[head], step_ref[head], decay_ref[head]

    def span(first, size=CH):
        return slice(first, first + size)

    def read(memory, rows):
        high, low = split2(memory * KAPPA)
        return dot_nt(q_s[rows, :], high) + dot_nt(q_s[rows, :], low)

    long0, long1, long2 = span(0), span(CH), span(2 * CH)
    short0, short1 = span(SLOT), span(SLOT + CH, SHORT - CH)
    update0 = dot_tn(v_s[long0, :], k_s[long0, :]) * (-KAPPA)
    mem1 = update0 * (-eta)
    high, low = split2(mem1 * KAPPA)
    err1 = dot_nt(k_s[long1, :], high) + dot_nt(k_s[long1, :], low) - v_s[long1, :].astype(F32)
    err_high, err_low = split2(err1)
    update1 = (dot_tn(err_high, k_s[long1, :]) + dot_tn(err_low, k_s[long1, :])) * KAPPA
    sur2 = mom * mem1 - eta * update1
    mem2 = (1.0 - decay) * mem1 + sur2
    update_s = dot_tn(v_s[short0, :], k_s[short0, :]) * (-KAPPA)
    mem_s = update_s * (-eta)
    state_ref[0, 0] = mem1
    state_ref[0, 1] = mem2
    state_ref[0, 2] = mem_s
    state_ref[0, 3] = update0
    state_ref[0, 4] = update1
    state_ref[0, 5] = update_s
    r_s[long0, :] = jnp.zeros((CH, HP), F32)
    r_s[long1, :] = read(mem1, long1)
    r_s[long2, :] = read(mem2, long2)
    r_s[short0, :] = jnp.zeros((CH, HP), F32)
    r_s[short1, :] = read(mem_s, short1)

    lane = lax.broadcasted_iota(jnp.int32, (SUB, HP), 1)

    def finish(rows, acc):
        inv = 1.0 / acc[:, DH : DH + 1]
        att = acc * inv
        a_ref[rows, :] = jnp.where(lane == DH, inv, att)
        comb = jnp.where(lane >= DH, 0.0, att) + r_s[rows, :]
        g_s[rows, :] = comb * jax.nn.sigmoid(g_s[rows, :])

    def own_part(q, rows):
        e_d = jnp.where(causal((SUB, SUB)), jnp.exp(dot_nt(q, k_s[rows, :]) * KAPPA), 0.0)
        e_p = jnp.exp(dot_nt(q, pk) * KAPPA)
        return dot_nn(e_d.astype(BF16), with_ones(v_s[rows, :])) + dot_nn(e_p.astype(BF16), pv1)

    def pair(step, carry):
        rows0 = pl.ds(pl.multiple_of(step * CH, SUB), SUB)
        rows1 = pl.ds(pl.multiple_of(step * CH + SUB, SUB), SUB)
        finish(rows0, own_part(q_s[rows0, :], rows0))
        q = q_s[rows1, :]
        e_o = jnp.exp(dot_nt(q, k_s[rows0, :]) * KAPPA)
        finish(rows1, own_part(q, rows1) + dot_nn(e_o.astype(BF16), with_ones(v_s[rows0, :])))
        return carry

    lax.fori_loop(0, LIVE // CH, pair, 0)
    tail = pl.ds(LIVE - SUB, SUB)
    finish(tail, own_part(q_s[tail, :], tail))
    store_rel(offs, chunk, g_s, o_ref)


def head_col(part, heads):
    return pl.BlockSpec((LIVE, HP), lambda h, offs: (0, part * heads + h))


def attention_forward(offs, rates, wide, convs, persists, heads, chunk):
    smem = pl.BlockSpec(memory_space=pltpu.SMEM)
    col = lambda rows: pl.BlockSpec((rows, HP), lambda h, offs: (0, h))
    return pl.pallas_call(
        functools.partial(forward_kernel, chunk),
        grid_spec=pltpu.PrefetchScalarGridSpec(
            num_scalar_prefetch=1,
            grid=(heads,),
            in_specs=[smem] * 3
            + [head_col(i, heads) for i in range(4)]
            + [col(KC)] * 3
            + [col(NP)] * 2,
            out_specs=[
                col(LIVE),
                col(LIVE),
                pl.BlockSpec((1, 6, HP, HP), lambda h, offs: (h, 0, 0, 0)),
            ],
            scratch_shapes=[pltpu.VMEM((PAD_ROWS, HP), F32)] * 3
            + [pltpu.VMEM((LIVE, HP), BF16)] * 3
            + [pltpu.VMEM((LIVE, HP), F32)] * 2,
        ),
        out_shape=[
            jax.ShapeDtypeStruct((LIVE, heads * HP), BF16),
            jax.ShapeDtypeStruct((LIVE, heads * HP), F32),
            jax.ShapeDtypeStruct((heads, 6, HP, HP), F32),
        ],
        compiler_params=pltpu.CompilerParams(vmem_limit_bytes=VMEM),
        name="attention_forward",
    )(offs, *rates, wide, wide, wide, wide, *convs, *persists)


def backward_kernel(
    chunk,
    offs,
    mom_ref,
    step_ref,
    decay_ref,
    qp_ref,
    kp_ref,
    vp_ref,
    gp_ref,
    do_ref,
    a_ref,
    state_ref,
    cq_ref,
    ck_ref,
    cv_ref,
    pk_ref,
    pv_ref,
    dq_ref,
    dk_ref,
    dv_ref,
    dg_ref,
    gcq_ref,
    gck_ref,
    gcv_ref,
    gpk_ref,
    gpv_ref,
    rate_ref,
    qpad,
    kpad,
    vpad,
    gq_s,
    gk_s,
    gv_s,
    q_s,
    k_s,
    v_s,
    da_s,
    dr_s,
    d_s,
    t_s,
    gpk_s,
    gpv_s,
):
    head = pl.program_id(0)
    load_padded(offs, chunk, qp_ref, qpad)
    load_padded(offs, chunk, kp_ref, kpad)
    load_padded(offs, chunk, vp_ref, vpad)
    load_natural(offs, chunk, do_ref, dr_s)
    load_natural(offs, chunk, gp_ref, d_s)
    taps_q, taps_k, taps_v = cq_ref[...], ck_ref[...], cv_ref[...]
    zero8 = jnp.zeros((8, HP), F32)
    for pad in (gq_s, gk_s, gv_s):
        pad[0:8, :] = zero8
        pad[8 + SLOT : 16 + SLOT, :] = zero8
        pad[16 + LIVE : 24 + LIVE, :] = zero8
    lane = lax.broadcasted_iota(jnp.int32, (SUB, HP), 1)

    def prepare(step, carry):
        base = pad_base(step)
        rows = pl.ds(pl.multiple_of(step * SUB, SUB), SUB)
        qc = conv_rows(qpad, taps_q, base)
        q_s[rows, :] = (qc * inv_head(qc)).astype(BF16)
        kc = conv_rows(kpad, taps_k, base)
        k_s[rows, :] = (kc * inv_head(kc)).astype(BF16)
        v_s[rows, :] = conv_rows(vpad, taps_v, base).astype(BF16)
        return carry

    lax.fori_loop(0, NSUB, prepare, 0)
    pkv = pk_ref[...]
    pk_inv = inv_head(pkv)
    pk = (pkv * pk_inv).astype(BF16)
    pv = pv_ref[...].astype(BF16)
    mom, eta, decay = mom_ref[head], step_ref[head], decay_ref[head]
    mem1, mem2, mem_s = state_ref[0, 0], state_ref[0, 1], state_ref[0, 2]
    update0, update1, update_s = state_ref[0, 3], state_ref[0, 4], state_ref[0, 5]

    def scaled(memory):
        return split2(memory * KAPPA)

    def two_nt(x, pieces):
        return dot_nt(x, pieces[0]) + dot_nt(x, pieces[1])

    def two_nn(x, pieces):
        return dot_nn(x, pieces[0]) + dot_nn(x, pieces[1])

    km1, km2, kms = scaled(mem1), scaled(mem2), scaled(mem_s)

    def gates(first, size, memory):
        for start in range(first, first + size, SUB):
            rows = slice(start, start + SUB)
            grad = dr_s[rows, :]
            sig = jax.nn.sigmoid(d_s[rows, :])
            att = a_ref[rows, :]
            comb = jnp.where(lane >= DH, 0.0, att)
            if memory is not None:
                comb = comb + two_nt(q_s[rows, :], memory)
            through = grad * sig
            t_s[rows, :] = (through * comb * (1.0 - sig)).astype(BF16)
            dr_s[rows, :] = through
            low = through.astype(BF16)
            da_s[rows, :] = low
            row_dot = jnp.sum(low.astype(F32) * att, axis=-1, keepdims=True)
            d_s[rows, :] = jnp.where(lane == 0, att[:, DH : DH + 1], row_dot)

    gates(0, CH, None)
    gates(CH, CH, km1)
    gates(2 * CH, CH, km2)
    gates(SLOT, CH, None)
    gates(SLOT + CH, SHORT - CH, kms)
    store_rel(offs, chunk, t_s, dg_ref)

    def span(first, size=CH):
        return slice(first, first + size)

    long0, long1, long2 = span(0), span(CH), span(2 * CH)
    short0, short1 = span(SLOT), span(SLOT + CH, SHORT - CH)

    def padded(rows):
        shift = 16 if rows.start >= SLOT else 8
        return slice(rows.start + shift, rows.stop + shift)

    def outer(left, right):
        high, low = split2(left)
        return dot_tn(high, right) + dot_tn(low, right)

    zero_span = jnp.zeros((CH, HP), F32)

    def reads_back(rows, pieces):
        gq_s[padded(rows), :] = two_nn(dr_s[rows, :].astype(BF16), pieces)

    def zero_out(pad, rows):
        pad[padded(rows), :] = jnp.zeros((rows.stop - rows.start, HP), F32)

    def row_sum(values):
        return jnp.sum(values, axis=0, keepdims=True)

    grad_mem2 = outer(dr_s[long2, :], q_s[long2, :]) * KAPPA
    reads_back(long2, km2)
    zero_out(gk_s, long2)
    zero_out(gv_s, long2)
    total2 = grad_mem2
    rate_decay = -row_sum(grad_mem2 * mem1)
    rate_mom = row_sum(total2 * mem1)
    rate_step = -row_sum(total2 * update1)
    grad_up = total2 * (-eta)
    k1 = k_s[long1, :]
    de1 = two_nt(k1, scaled(grad_up))
    err1 = two_nt(k1, km1) - v_s[long1, :].astype(F32)
    gk_s[padded(long1), :] = two_nn(err1.astype(BF16), scaled(grad_up)) + two_nn(
        de1.astype(BF16), km1
    )
    gv_s[padded(long1), :] = -de1
    grad_mem1 = (
        outer(dr_s[long1, :], q_s[long1, :]) * KAPPA
        + (1.0 - decay) * grad_mem2
        + outer(de1, k1) * KAPPA
    )
    reads_back(long1, km1)
    total1 = grad_mem1 + mom * total2
    rate_step = rate_step - row_sum(total1 * update0)

    def first_span(rows, total):
        pieces = scaled(total * (-eta))
        gv_s[padded(rows), :] = -two_nt(k_s[rows, :], pieces)
        gk_s[padded(rows), :] = -two_nn(v_s[rows, :], pieces)
        gq_s[padded(rows), :] = zero_span

    first_span(long0, total1)
    grad_mem_s = outer(dr_s[short1, :], q_s[short1, :]) * KAPPA
    reads_back(short1, kms)
    zero_out(gk_s, short1)
    zero_out(gv_s, short1)
    rate_step = rate_step - row_sum(grad_mem_s * update_s)
    first_span(short0, grad_mem_s)
    rate_ref[...] = jnp.concatenate(
        [rate_mom, rate_step, rate_decay, jnp.zeros((5, HP), F32)], axis=0
    )

    gpk_s[...] = jnp.zeros((NP, HP), F32)
    gpv_s[...] = jnp.zeros((NP, HP), F32)

    def block(q, da, inv, row_dot, keys, vals, masked):
        prob = jnp.exp(dot_nt(q, keys) * KAPPA) * inv
        if masked:
            prob = jnp.where(causal(prob.shape), prob, 0.0)
        grad = dot_nt(da, vals)
        ds = (prob * (grad - row_dot) * KAPPA).astype(BF16)
        return dot_nn(ds, keys), dot_tn(ds, q), dot_tn(prob.astype(BF16), da)

    def one(rows, base, before=None, base_before=None):
        q, da = q_s[rows, :], da_s[rows, :]
        inv, row_dot = d_s[rows, 0:1], d_s[rows, 1:2]
        here = pl.ds(base, SUB)
        gq, gk, gv = block(q, da, inv, row_dot, k_s[rows, :], v_s[rows, :], True)
        gk_s[here, :] += gk
        gv_s[here, :] += gv
        pq, gpk, gpv = block(q, da, inv, row_dot, pk, pv, False)
        gpk_s[...] += gpk
        gpv_s[...] += gpv
        gq = gq + pq
        if before is not None:
            oq, ok, ov = block(q, da, inv, row_dot, k_s[before, :], v_s[before, :], False)
            there = pl.ds(base_before, SUB)
            gk_s[there, :] += ok
            gv_s[there, :] += ov
            gq = gq + oq
        gq_s[here, :] += gq

    def pair(step, carry):
        rows0 = pl.ds(pl.multiple_of(step * CH, SUB), SUB)
        rows1 = pl.ds(pl.multiple_of(step * CH + SUB, SUB), SUB)
        base0, base1 = pad_base(2 * step), pad_base(2 * step + 1)
        one(rows0, base0)
        one(rows1, base1, rows0, base0)
        return carry

    lax.fori_loop(0, LIVE // CH, pair, 0)
    one(pl.ds(LIVE - SUB, SUB), 16 + LIVE - SUB)
    gpv_ref[...] = gpv_s[...]
    gpk_ref[...] = head_back(pkv, pk_inv, gpk_s[...])

    def norms(step, carry):
        base = pad_base(step)
        here = pl.ds(base, SUB)
        qc = conv_rows(qpad, taps_q, base)
        gq_s[here, :] = head_back(qc, inv_head(qc), gq_s[here, :])
        kc = conv_rows(kpad, taps_k, base)
        gk_s[here, :] = head_back(kc, inv_head(kc), gk_s[here, :])
        return carry

    lax.fori_loop(0, NSUB, norms, 0)

    def conv_back(pre_ref, grad_ref, taps, out_ref, taps_ref):
        def body(step, carry):
            base = pad_base(step)
            rows = pl.ds(pl.multiple_of(step * SUB, SUB), SUB)
            after = grad_ref[pl.ds(base, SUB + 8), :]
            before = pre_ref[pl.ds(pl.multiple_of(base - 8, 8), SUB + 8), :]
            grad = after[:SUB, :]
            total = taps[0:1, :] * grad
            sums = [row_sum(grad * before[8:, :])]
            for j in range(1, KC):
                total = total + taps[j : j + 1, :] * after[j : j + SUB, :]
                sums.append(row_sum(grad * before[8 - j : 8 - j + SUB, :]))
            t_s[rows, :] = total.astype(BF16)
            return tuple(c + s for c, s in zip(carry, sums))

        sums = lax.fori_loop(0, NSUB, body, (jnp.zeros((1, HP), F32),) * KC)
        taps_ref[...] = jnp.concatenate(sums, axis=0)
        store_rel(offs, chunk, t_s, out_ref)

    conv_back(qpad, gq_s, taps_q, dq_ref, gcq_ref)
    conv_back(kpad, gk_s, taps_k, dk_ref, gck_ref)
    conv_back(vpad, gv_s, taps_v, dv_ref, gcv_ref)


def attention_backward(offs, rates, wide, grad_out, att, states, convs, persists, heads, chunk):
    smem = pl.BlockSpec(memory_space=pltpu.SMEM)
    col = lambda rows: pl.BlockSpec((rows, HP), lambda h, offs: (0, h))
    shape = lambda rows, dtype: jax.ShapeDtypeStruct((rows, heads * HP), dtype)
    return pl.pallas_call(
        functools.partial(backward_kernel, chunk),
        grid_spec=pltpu.PrefetchScalarGridSpec(
            num_scalar_prefetch=1,
            grid=(heads,),
            in_specs=[smem] * 3
            + [head_col(i, heads) for i in range(4)]
            + [col(LIVE)] * 2
            + [pl.BlockSpec((1, 6, HP, HP), lambda h, offs: (h, 0, 0, 0))]
            + [col(KC)] * 3
            + [col(NP)] * 2,
            out_specs=[col(LIVE)] * 4 + [col(KC)] * 3 + [col(NP)] * 2 + [col(8)],
            scratch_shapes=[pltpu.VMEM((PAD_ROWS, HP), F32)] * 6
            + [pltpu.VMEM((LIVE, HP), BF16)] * 4
            + [pltpu.VMEM((LIVE, HP), F32)] * 2
            + [pltpu.VMEM((LIVE, HP), BF16)]
            + [pltpu.VMEM((NP, HP), F32)] * 2,
        ),
        out_shape=[shape(LIVE, BF16)] * 4
        + [shape(KC, F32)] * 3
        + [shape(NP, F32)] * 2
        + [shape(8, F32)],
        compiler_params=pltpu.CompilerParams(vmem_limit_bytes=VMEM),
        name="attention_backward",
    )(offs, *rates, wide, wide, wide, wide, grad_out, att, states, *convs, *persists)


def silu_grad(values):
    sigmoid_v = jax.nn.sigmoid(values)
    return sigmoid_v * (1.0 + values * (1.0 - sigmoid_v))


def rms_backward(values, inv_rms, gain, grad_out):
    scaled = grad_out * gain
    grad_in = inv_rms * (
        scaled - values * inv_rms * inv_rms * jnp.mean(scaled * values, axis=-1, keepdims=True)
    )
    return grad_in, jnp.sum(grad_out * values * inv_rms, axis=0)


def pad_heads(values):
    rows, cols = values.shape
    split = values.reshape(rows, cols // DH, DH)
    return jnp.pad(split, ((0, 0), (0, 0), (0, HP - DH))).reshape(rows, -1)


def cut_heads(values):
    rows, cols = values.shape
    return values.reshape(rows, cols // HP, HP)[:, :, :DH].reshape(rows, -1)


class Team:
    def __init__(self, n_dp, n_tensor):
        self.n_dp, self.n_tensor = n_dp, n_tensor
        self.half = half = n_tensor // 2
        p, t = lax.axis_index("dp"), lax.axis_index("tensor")
        self.t = t
        self.core = p % 2
        self.side = t // half
        self.place = t % half
        self.same = self.core == self.side
        self.core_swap = [(i, i ^ 1) for i in range(n_dp)]
        lin = lambda c, k, h, z: (2 * k + c) * n_tensor + z + h * half
        quads = [(k, z) for k in range(n_dp // 2) for z in range(half)]
        self.diag, self.cycle, self.cycle_back = [], [], []
        for k, z in quads:
            d00, d01, d10, d11 = lin(0, k, 0, z), lin(0, k, 1, z), lin(1, k, 0, z), lin(1, k, 1, z)
            self.diag += [(d10, d01), (d01, d10)]
            self.cycle += [(d00, d01), (d11, d10), (d10, d00), (d01, d11)]
        self.cycle_back = [(b, a) for a, b in self.cycle]
        self.parity = [list(range(c, n_dp, 2)) for c in range(2)]
        self.chunk = LIVE // n_tensor

    def swap(self, values):
        return lax.ppermute(values, "dp", self.core_swap)

    def rotate(self, values, by):
        half = self.half
        return lax.ppermute(
            values,
            "tensor",
            [(t, (t // half) * half + (t + by) % half) for t in range(self.n_tensor)],
        )

    def across(self, values):
        return lax.ppermute(values, ("dp", "tensor"), self.diag)

    def gather(self, own):
        pieces = []
        for s in range(self.half):
            piece = own if s == 0 else self.rotate(own, s)
            pieces += [piece, self.swap(piece)]
        return jnp.concatenate(pieces, axis=0)

    def scatter(self, partial):
        size = self.chunk
        total = None
        for s in reversed(range(self.half)):
            keep = partial[2 * s * size : (2 * s + 1) * size]
            send = partial[(2 * s + 1) * size : (2 * s + 2) * size]
            chip = keep.astype(F32) + self.swap(send).astype(F32)
            if s:
                chip = self.rotate(chip.astype(BF16), self.half - s).astype(F32)
            total = chip if total is None else total + chip
        return total

    def fetch_weights(self, block):
        first_in = lax.ppermute(block, ("dp", "tensor"), self.cycle)
        second_in = lax.ppermute(block, ("dp", "tensor"), self.diag)
        first = jnp.where(self.same, block, first_in)
        second = jnp.where(self.same, first_in, second_in)
        low = jnp.where(self.core == 0, first, second)
        high = jnp.where(self.core == 0, second, first)
        both = jnp.concatenate([low, high], axis=0)
        return lax.all_gather(both, "dp", axis=0, tiled=True, axis_index_groups=self.parity)

    def reduce_weights(self, grad):
        both = lax.psum_scatter(
            grad, "dp", scatter_dimension=0, tiled=True, axis_index_groups=self.parity
        )
        rows = both.shape[0] // 2
        low, high = both[:rows], both[rows:]
        of_core = jnp.where(self.core == 0, low, high)
        of_other = jnp.where(self.core == 0, high, low)
        first_in = lax.ppermute(
            jnp.where(self.same, of_other, of_core), ("dp", "tensor"), self.cycle_back
        )
        second_in = lax.ppermute(of_other, ("dp", "tensor"), self.diag)
        return first_in.astype(F32) + jnp.where(self.same, of_core, second_in).astype(F32)


def per_device(
    n_dp,
    n_tensor,
    tokens,
    query_weight,
    key_weight,
    value_weight,
    gate_weight,
    output_weight,
    memory_in,
    memory_out,
    swiglu_gate,
    swiglu_up,
    swiglu_down,
    conv_query,
    conv_key,
    conv_value,
    persist_key,
    persist_value,
    momentum,
    step_size,
    decay_rate,
    norm_attn,
    norm_swiglu,
    seq_lengths,
    deal_order,
    cotangent,
):
    team = Team(n_dp, n_tensor)
    half, core, side, place, same, chunk = (
        team.half,
        team.core,
        team.side,
        team.place,
        team.same,
        team.chunk,
    )
    own_rows = tokens.shape[0]
    own_blks = own_rows // BLK
    head_feats = query_weight.shape[1]
    heads = head_feats // DH
    grain = next(g for g in (128, 64, 32) if chunk % g == 0)
    per_blk, per_chunk = BLK // grain, chunk // grain

    tables = jnp.concatenate([deal_order[0], seq_lengths[0]])
    other_tables = team.swap(tables)
    group_tables = jnp.where(same, tables, other_tables)
    n_blks = deal_order.shape[1]
    deal = group_tables[:n_blks]
    long_slot = jnp.where(group_tables[n_blks] == SLOT, 0, 1)

    small = jnp.concatenate(
        [
            conv_query,
            conv_key,
            conv_value,
            persist_key,
            persist_value,
        ],
        axis=0,
    )
    rates = jnp.stack([momentum, step_size, decay_rate])
    flip = [(t, (t + half) % n_tensor) for t in range(n_tensor)]
    small = jnp.where(same, small, lax.ppermute(small, "tensor", flip))
    rates = jnp.where(same, rates, lax.ppermute(rates, "tensor", flip))
    small = pad_heads(small)
    convs = [small[KC * i : KC * (i + 1)] for i in range(3)]
    persists = [small[3 * KC + NP * i : 3 * KC + NP * (i + 1)] for i in range(2)]
    rates = [rates[0], rates[1], rates[2]]

    rows_in = jnp.where(same, tokens, team.across(tokens))
    cots_in = jnp.where(same, cotangent, team.across(cotangent))

    def index_of(rel):
        part, within = rel // per_chunk, rel % per_chunk
        turn, cross = part // 2, part % 2
        natural = (place - turn) % half + ((core + cross) % 2) * half
        compact = natural * per_chunk + within
        blk, sub = compact // per_blk, compact % per_blk
        in_long = blk < SLOT_BLKS
        nat_blk = jnp.where(
            in_long, long_slot * SLOT_BLKS + blk, (1 - long_slot) * SLOT_BLKS + blk - SLOT_BLKS
        )
        match = (deal[None, :] == nat_blk[:, None]).astype(jnp.int32)
        dealt = jnp.sum(match * jnp.arange(n_blks, dtype=jnp.int32)[None, :], axis=1)
        shard, blk_in = dealt // own_blks, dealt % own_blks
        owner_core, owner_place = shard // half, shard % half
        piece = 2 * ((place - owner_place) % half) + (owner_core != core).astype(jnp.int32)
        return ((piece * own_blks + blk_in) * per_blk + sub).astype(jnp.int32)

    n_sub = LIVE // grain
    gather_index = index_of(jnp.arange(n_sub, dtype=jnp.int32))
    count = n_sub // 9
    own_index = gather_index[:per_chunk]

    offs_at = jnp.arange(n_tensor, dtype=jnp.int32)
    offs = (
        (
            2 * ((place - offs_at % half) % half) + (offs_at // half != core).astype(jnp.int32)
        )
        * chunk
    ).astype(jnp.int32)

    heads_w = team.fetch_weights(
        jnp.concatenate(
            [query_weight, key_weight, value_weight, gate_weight, output_weight.T], axis=1
        )
    )
    x_all = team.gather(rows_in)
    min_w = team.fetch_weights(memory_in)
    mout_w = team.fetch_weights(memory_out.T)
    c_all = team.gather(cots_in)
    gu_w = team.fetch_weights(jnp.concatenate([swiglu_gate, swiglu_up], axis=1))
    down_w = team.fetch_weights(swiglu_down.T)

    heads_w = pad_heads(heads_w)
    wide_feats = 4 * heads * HP
    qkvg_w, out_w = heads_w[:, :wide_feats], heads_w[:, wide_feats:]

    normed = gather_rows(x_all, gather_index, grain, count, norm_attn)
    x_own = gather_rows(x_all, own_index, grain, per_chunk // 3).astype(F32)
    inv_first = lax.rsqrt(jnp.mean(x_own * x_own, axis=-1, keepdims=True) + EPS)

    wide = dot_nn(normed, qkvg_w)
    o_low, att, states = attention_forward(offs, rates, wide, convs, persists, heads, chunk)
    mem_pre = dot_nn(normed, min_w).astype(BF16)
    mem_hidden = jax.nn.silu(mem_pre.astype(F32)).astype(BF16)
    branch = (dot_nt(o_low, out_w) + dot_nt(mem_hidden, mout_w)).astype(BF16)
    mid_own = x_own + team.scatter(branch)
    inv_second = lax.rsqrt(jnp.mean(mid_own * mid_own, axis=-1, keepdims=True) + EPS)
    swiglu_in = team.gather((mid_own * inv_second * norm_swiglu).astype(BF16))

    cot_low = gather_rows(c_all, gather_index, grain, count)
    cot_own = cot_low[:chunk].astype(F32)
    ff = swiglu_gate.shape[1]
    gate_up = dot_nn(swiglu_in, gu_w)
    gate_pre, up_pre = gate_up[:, :ff], gate_up[:, ff:]
    gate_act = jax.nn.silu(gate_pre)
    hidden = (gate_act * up_pre).astype(BF16)
    grad_hidden = dot_nn(cot_low, down_w)
    grad_gate_up = jnp.concatenate(
        [
            (grad_hidden * up_pre * silu_grad(gate_pre)).astype(BF16),
            (grad_hidden * gate_act).astype(BF16),
        ],
        axis=1,
    )
    grad_mid_norm = team.scatter(dot_nt(grad_gate_up, gu_w).astype(BF16))
    swiglu_out = team.scatter(dot_nt(hidden, down_w).astype(BF16))
    y_own = (mid_own + swiglu_out).astype(BF16)
    grad_gu = team.reduce_weights(dot_tn(swiglu_in, grad_gate_up).astype(BF16))
    grad_down = team.reduce_weights(dot_tn(cot_low, hidden).astype(BF16))

    grad_second, gain_second = rms_backward(mid_own, inv_second, norm_swiglu, grad_mid_norm)
    grad_mid = cot_own + grad_second
    branch_cot = team.gather(grad_mid.astype(BF16))

    grad_out = dot_nn(branch_cot, out_w)
    grad_mem = (dot_nn(branch_cot, mout_w) * silu_grad(mem_pre.astype(F32))).astype(BF16)
    back = attention_backward(
        offs, rates, wide, grad_out, att, states, convs, persists, heads, chunk
    )
    grad_wide = jnp.concatenate(back[:4], axis=1)
    grad_normed = team.scatter(
        (dot_nt(grad_wide, qkvg_w) + dot_nt(grad_mem, min_w)).astype(BF16)
    )
    grad_mout = team.reduce_weights(dot_tn(branch_cot, mem_hidden).astype(BF16))
    grad_min = team.reduce_weights(dot_tn(normed, grad_mem).astype(BF16))
    grad_heads = team.reduce_weights(
        cut_heads(
            jnp.concatenate(
                [dot_tn(normed, grad_wide).astype(BF16), dot_tn(branch_cot, o_low).astype(BF16)],
                axis=1,
            )
        )
    )
    grad_first, gain_first = rms_backward(x_own, inv_first, norm_attn, grad_normed)
    rows_grad_own = (grad_mid + grad_first).astype(BF16)

    want = jnp.arange(own_blks * per_blk, dtype=jnp.int32)
    shard = jnp.where(same, team.t, (team.t + half) % n_tensor)
    nat_blk = deal[shard * own_blks + want // per_blk]
    in_long = nat_blk // SLOT_BLKS == long_slot
    blk = jnp.where(in_long, nat_blk % SLOT_BLKS, SLOT_BLKS + nat_blk % SLOT_BLKS)
    compact = jnp.minimum(blk, LIVE // BLK - 1) * per_blk + want % per_blk
    natural, within = compact // per_chunk, compact % per_chunk
    part = 2 * ((place - natural % half) % half) + (natural // half != core).astype(jnp.int32)
    back_index = (part * per_chunk + within).astype(jnp.int32)

    own_deal = lax.dynamic_slice_in_dim(deal_order[0], team.t * own_blks, own_blks)
    own_len = jnp.where(own_deal // SLOT_BLKS == 0, seq_lengths[0, 0], seq_lengths[0, 1])
    live_blk = (own_deal % SLOT_BLKS) * BLK < own_len
    live = jnp.broadcast_to(live_blk[:, None], (own_blks, BLK)).reshape(own_rows, 1)

    def send_back(values):
        built = gather_rows(team.gather(values), back_index, grain, 4)
        return jnp.where(same, built, team.across(built))

    layer_out = jnp.where(live, send_back(y_own), tokens)
    grad_tokens = jnp.where(live, send_back(rows_grad_own), cotangent).astype(F32)

    small_back = jnp.concatenate(back[4:], axis=0).astype(BF16)
    summed = lax.psum(small_back.astype(F32), "dp", axis_index_groups=team.parity)
    summed = summed + lax.ppermute(summed, "tensor", flip)
    summed = jnp.where(same, summed, team.swap(summed))
    base = 3 * KC + 2 * NP
    taps = cut_heads(summed[:base])
    rate_rows = jnp.sum(summed[base : base + 3].reshape(3, heads, HP), axis=-1)
    gain_attn, gain_swiglu = lax.psum((gain_first, gain_second), ("dp", "tensor"))

    f = head_feats
    return (
        layer_out,
        grad_tokens,
        grad_heads[:, :f],
        grad_heads[:, f : 2 * f],
        grad_heads[:, 2 * f : 3 * f],
        grad_heads[:, 3 * f : 4 * f],
        grad_heads[:, 4 * f :].T,
        grad_min,
        grad_mout.T,
        grad_gu[:, :ff],
        grad_gu[:, ff:],
        grad_down.T,
        taps[:KC],
        taps[KC : 2 * KC],
        taps[2 * KC : 3 * KC],
        taps[3 * KC : 3 * KC + NP],
        taps[3 * KC + NP :],
        rate_rows[0],
        rate_rows[1],
        rate_rows[2],
        gain_attn,
        gain_swiglu,
    )


def solution(mesh):
    rows = P(("dp", "tensor"), None)
    cols_w, rows_w = P("dp", "tensor"), P("tensor", "dp")
    feats, rate = P(None, "tensor"), P("tensor")
    weights = (cols_w,) * 4 + (rows_w, cols_w, rows_w, cols_w, cols_w, rows_w)
    smalls = (feats,) * 5 + (rate,) * 3
    return jax.shard_map(
        functools.partial(per_device, mesh.shape["dp"], mesh.shape["tensor"]),
        mesh=mesh,
        in_specs=(rows,) + weights + smalls + (P(), P(), P("dp", None), P("dp", None), rows),
        out_specs=(rows, rows) + weights + smalls + (P(), P()),
        check_vma=False,
    )
```

```python
import functools

import jax
import jax.numpy as jnp
from jax import lax
from jax.experimental import pallas as pl
from jax.experimental.layout import Layout, with_layout_constraint
from jax.experimental.pallas import tpu as pltpu
from jax.sharding import PartitionSpec as P

DH = 96
HP = 128
NP = 64
CH = 512
KC = 4
SLOT = 1536
SHORT = 768
LIVE = SLOT + SHORT
BLK = 128
SUB = 256
NSUB = LIVE // SUB
LONG_SUBS = SLOT // SUB
SLOT_BLKS = SLOT // BLK
SHORT_BLKS = SHORT // BLK
PAD_ROWS = LIVE + 24
EPS = 1e-06
KAPPA = DH ** (-0.5)
VMEM = 56 * 1024 * 1024

F32 = jnp.float32
BF16 = jnp.bfloat16


def dot_nn(a, b):
    return lax.dot_general(a, b, (((1,), (0,)), ((), ())), preferred_element_type=F32)


def dot_nt(a, b):
    return lax.dot_general(a, b, (((1,), (1,)), ((), ())), preferred_element_type=F32)


def dot_tn(a, b):
    return lax.dot_general(a, b, (((0,), (0,)), ((), ())), preferred_element_type=F32)


STEP = 3


def gather_kernel(sources, rows, own_steps, normed, idx_ref, *refs):
    ins, refs = refs[:sources], refs[sources:]
    if normed:
        gain_ref, refs = refs[0], refs[1:]
    out_ref, buf, sem = refs[0], refs[-2], refs[-1]
    step, steps = pl.program_id(0), pl.num_programs(0)
    per_source = ins[0].shape[0] // rows

    def copy(source, first, slot, j):
        return pltpu.make_async_copy(
            source.at[pl.ds(first, rows)], buf.at[slot, pl.ds(j * rows, rows)], sem.at[slot, j]
        )

    def fetch(at, slot):
        for j in range(STEP):
            block = idx_ref[at * STEP + j]
            first = pl.multiple_of((block % per_source) * rows, rows)
            for i in range(sources):

                @pl.when(block // per_source == i)
                def _(i=i, first=first, j=j):
                    copy(ins[i], first, slot, j).start()

    slot = step % 2

    @pl.when(step == 0)
    def _():
        fetch(0, 0)

    @pl.when(step + 1 < steps)
    def _():
        fetch(step + 1, 1 - slot)

    for j in range(STEP):
        copy(ins[0], 0, slot, j).wait()
    block = buf[slot]
    if own_steps:

        @pl.when(step < own_steps)
        def _():
            refs[1][...] = block

    if normed:
        wide = block.astype(F32)
        inv = lax.rsqrt(jnp.mean(wide * wide, axis=-1, keepdims=True) + EPS)
        block = (wide * inv * gain_ref[...]).astype(BF16)
    out_ref[...] = block


def gather_rows(sources, index, rows, gain=None, own_steps=0):
    width, dtype = sources[0].shape[1], sources[0].dtype
    in_specs = [pl.BlockSpec(memory_space=pl.ANY)] * len(sources)
    args = list(sources)
    size = STEP * rows
    if gain is not None:
        in_specs.append(pl.BlockSpec((1, width), lambda i, idx: (0, 0)))
        args.append(gain[None, :])
    out_specs = [pl.BlockSpec((size, width), lambda i, idx: (i, 0))]
    out_shape = [jax.ShapeDtypeStruct((index.shape[0] * rows, width), dtype)]
    if own_steps:
        out_specs.append(
            pl.BlockSpec((size, width), lambda i, idx: (jnp.minimum(i, own_steps - 1), 0))
        )
        out_shape.append(jax.ShapeDtypeStruct((own_steps * size, width), dtype))
    out = pl.pallas_call(
        functools.partial(gather_kernel, len(sources), rows, own_steps, gain is not None),
        grid_spec=pltpu.PrefetchScalarGridSpec(
            num_scalar_prefetch=1,
            grid=(index.shape[0] // STEP,),
            in_specs=in_specs,
            out_specs=out_specs,
            scratch_shapes=[
                pltpu.VMEM((2, size, width), dtype),
                pltpu.SemaphoreType.DMA((2, STEP)),
            ],
        ),
        out_shape=out_shape,
        compiler_params=pltpu.CompilerParams(vmem_limit_bytes=VMEM),
        name="gather_rows",
    )(index, *args)
    return out if own_steps else out[0]


def cut_kernel(groups, in_ref, out_ref):
    width = out_ref.shape[2]
    for g in range(groups):
        out_ref[g, :, :] = in_ref[:DH, g * width : (g + 1) * width]


def cut_columns(values, groups):
    rows, width = values.shape
    return pl.pallas_call(
        functools.partial(cut_kernel, groups),
        grid=(rows // HP,),
        in_specs=[pl.BlockSpec((HP, width), lambda i: (i, 0))],
        out_specs=pl.BlockSpec((groups, DH, width // groups), lambda i: (0, i, 0)),
        out_shape=jax.ShapeDtypeStruct((groups, rows // HP * DH, width // groups), values.dtype),
        compiler_params=pltpu.CompilerParams(vmem_limit_bytes=VMEM),
        name="cut_columns",
    )(values).reshape(-1, width // groups)


def pad_base(step):
    return pl.multiple_of(8 + SUB * step + jnp.where(step >= LONG_SUBS, 8, 0), 8)


def load_padded(offs, chunk, src_ref, pad_ref):
    zero = jnp.zeros((8, HP), F32)
    pad_ref[0:8, :] = zero
    pad_ref[8 + SLOT : 16 + SLOT, :] = zero
    pad_ref[16 + LIVE : 24 + LIVE, :] = zero
    piece = 32
    for q in range(LIVE // chunk):
        start = q * chunk
        for first in range(0, chunk, piece):
            row = start + first
            pad_ref[pl.ds(8 + row + (8 if row >= SLOT else 0), piece), :] = src_ref[
                pl.ds(pl.multiple_of(offs[q] + first, piece), piece), :
            ].astype(F32)


def load_natural(offs, chunk, src_ref, dst_ref):
    for q in range(LIVE // chunk):
        dst_ref[pl.ds(q * chunk, chunk), :] = src_ref[
            pl.ds(pl.multiple_of(offs[q], 32), chunk), :
        ].astype(dst_ref.dtype)


def store_rel(offs, chunk, src_ref, dst_ref):
    for q in range(LIVE // chunk):
        dst_ref[pl.ds(pl.multiple_of(offs[q], 32), chunk), :] = src_ref[
            pl.ds(q * chunk, chunk), :
        ].astype(dst_ref.dtype)


def conv_rows(pad_ref, taps, base):
    window = pad_ref[pl.ds(pl.multiple_of(base - 8, 8), SUB + 8), :]
    total = taps[0:1, :] * window[8:, :]
    for j in range(1, KC):
        total = total + taps[j : j + 1, :] * window[8 - j : 8 - j + SUB, :]
    return total


def inv_head(values):
    return lax.rsqrt(jnp.sum(values * values, axis=-1, keepdims=True) * (1.0 / DH) + EPS)


def head_back(values, inv, grad):
    normed = values * inv
    return inv * (grad - normed * (jnp.sum(grad * normed, axis=-1, keepdims=True) * (1.0 / DH)))


def with_ones(values):
    lane = lax.broadcasted_iota(jnp.int32, values.shape, 1)
    return jnp.where(lane == DH, 1.0, values.astype(F32)).astype(BF16)


def causal(shape):
    return lax.broadcasted_iota(jnp.int32, shape, 1) <= lax.broadcasted_iota(jnp.int32, shape, 0)


def split2(values):
    high = values.astype(BF16)
    return high, (values - high.astype(F32)).astype(BF16)


def forward_kernel(
    chunk,
    offs,
    mom_ref,
    step_ref,
    decay_ref,
    qp_ref,
    kp_ref,
    vp_ref,
    gp_ref,
    cq_ref,
    ck_ref,
    cv_ref,
    pk_ref,
    pv_ref,
    o_ref,
    a_ref,
    state_ref,
    qpad,
    kpad,
    vpad,
    q_s,
    k_s,
    v_s,
    r_s,
    g_s,
):
    head = pl.program_id(0)
    load_padded(offs, chunk, qp_ref, qpad)
    load_padded(offs, chunk, kp_ref, kpad)
    load_padded(offs, chunk, vp_ref, vpad)
    load_natural(offs, chunk, gp_ref, g_s)
    taps_q, taps_k, taps_v = cq_ref[...], ck_ref[...], cv_ref[...]

    def prepare(step, carry):
        base = pad_base(step)
        rows = pl.ds(pl.multiple_of(step * SUB, SUB), SUB)
        qc = conv_rows(qpad, taps_q, base)
        q_s[rows, :] = (qc * inv_head(qc)).astype(BF16)
        kc = conv_rows(kpad, taps_k, base)
        k_s[rows, :] = (kc * inv_head(kc)).astype(BF16)
        v_s[rows, :] = conv_rows(vpad, taps_v, base).astype(BF16)
        return carry

    lax.fori_loop(0, NSUB, prepare, 0)
    pkv = pk_ref[...]
    pk = (pkv * inv_head(pkv)).astype(BF16)
    pv1 = with_ones(pv_ref[...])

    mom, eta, decay = mom_ref[head], step_ref[head], decay_ref[head]

    def span(first, size=CH):
        return slice(first, first + size)

    def read(memory, rows):
        high, low = split2(memory * KAPPA)
        return dot_nt(q_s[rows, :], high) + dot_nt(q_s[rows, :], low)

    long0, long1, long2 = span(0), span(CH), span(2 * CH)
    short0, short1 = span(SLOT), span(SLOT + CH, SHORT - CH)
    update0 = dot_tn(v_s[long0, :], k_s[long0, :]) * (-KAPPA)
    mem1 = update0 * (-eta)
    high, low = split2(mem1 * KAPPA)
    err1 = dot_nt(k_s[long1, :], high) + dot_nt(k_s[long1, :], low) - v_s[long1, :].astype(F32)
    err_high, err_low = split2(err1)
    update1 = (dot_tn(err_high, k_s[long1, :]) + dot_tn(err_low, k_s[long1, :])) * KAPPA
    sur2 = mom * mem1 - eta * update1
    mem2 = (1.0 - decay) * mem1 + sur2
    update_s = dot_tn(v_s[short0, :], k_s[short0, :]) * (-KAPPA)
    mem_s = update_s * (-eta)
    state_ref[0, 0] = mem1
    state_ref[0, 1] = mem2
    state_ref[0, 2] = mem_s
    state_ref[0, 3] = update0
    state_ref[0, 4] = update1
    state_ref[0, 5] = update_s
    r_s[long0, :] = jnp.zeros((CH, HP), F32)
    r_s[long1, :] = read(mem1, long1)
    r_s[long2, :] = read(mem2, long2)
    r_s[short0, :] = jnp.zeros((CH, HP), F32)
    r_s[short1, :] = read(mem_s, short1)

    lane = lax.broadcasted_iota(jnp.int32, (SUB, HP), 1)

    def finish(rows, acc):
        inv = 1.0 / acc[:, DH : DH + 1]
        att = acc * inv
        a_ref[rows, :] = jnp.where(lane == DH, inv, att)
        comb = jnp.where(lane >= DH, 0.0, att) + r_s[rows, :]
        g_s[rows, :] = comb * jax.nn.sigmoid(g_s[rows, :])

    def own_part(q, rows):
        e_d = jnp.where(causal((SUB, SUB)), jnp.exp(dot_nt(q, k_s[rows, :]) * KAPPA), 0.0)
        e_p = jnp.exp(dot_nt(q, pk) * KAPPA)
        return dot_nn(e_d.astype(BF16), with_ones(v_s[rows, :])) + dot_nn(e_p.astype(BF16), pv1)

    def pair(step, carry):
        rows0 = pl.ds(pl.multiple_of(step * CH, SUB), SUB)
        rows1 = pl.ds(pl.multiple_of(step * CH + SUB, SUB), SUB)
        finish(rows0, own_part(q_s[rows0, :], rows0))
        q = q_s[rows1, :]
        e_o = jnp.exp(dot_nt(q, k_s[rows0, :]) * KAPPA)
        finish(rows1, own_part(q, rows1) + dot_nn(e_o.astype(BF16), with_ones(v_s[rows0, :])))
        return carry

    lax.fori_loop(0, LIVE // CH, pair, 0)
    tail = pl.ds(LIVE - SUB, SUB)
    finish(tail, own_part(q_s[tail, :], tail))
    store_rel(offs, chunk, g_s, o_ref)


def head_col(part, heads, first=0):
    return pl.BlockSpec((LIVE, HP), lambda h, offs: (0, part * heads + first + h))


def attention_forward(offs, rates, wide, convs, persists, heads, chunk):
    smem = pl.BlockSpec(memory_space=pltpu.SMEM)
    col = lambda rows: pl.BlockSpec((rows, HP), lambda h, offs: (0, h))
    return pl.pallas_call(
        functools.partial(forward_kernel, chunk),
        grid_spec=pltpu.PrefetchScalarGridSpec(
            num_scalar_prefetch=1,
            grid=(heads,),
            in_specs=[smem] * 3
            + [head_col(i, heads) for i in range(4)]
            + [col(KC)] * 3
            + [col(NP)] * 2,
            out_specs=[
                col(LIVE),
                col(LIVE),
                pl.BlockSpec((1, 6, HP, HP), lambda h, offs: (h, 0, 0, 0)),
            ],
            scratch_shapes=[pltpu.VMEM((PAD_ROWS, HP), F32)] * 3
            + [pltpu.VMEM((LIVE, HP), BF16)] * 3
            + [pltpu.VMEM((LIVE, HP), F32)] * 2,
        ),
        out_shape=[
            jax.ShapeDtypeStruct((LIVE, heads * HP), BF16),
            jax.ShapeDtypeStruct((LIVE, heads * HP), F32),
            jax.ShapeDtypeStruct((heads, 6, HP, HP), F32),
        ],
        compiler_params=pltpu.CompilerParams(vmem_limit_bytes=VMEM),
        name="attention_forward",
    )(offs, *rates, wide, wide, wide, wide, *convs, *persists)


def backward_kernel(
    chunk,
    first_head,
    offs,
    mom_ref,
    step_ref,
    decay_ref,
    qp_ref,
    kp_ref,
    vp_ref,
    gp_ref,
    do_ref,
    a_ref,
    state_ref,
    cq_ref,
    ck_ref,
    cv_ref,
    pk_ref,
    pv_ref,
    dq_ref,
    dk_ref,
    dv_ref,
    dg_ref,
    gcq_ref,
    gck_ref,
    gcv_ref,
    gpk_ref,
    gpv_ref,
    rate_ref,
    qpad,
    kpad,
    vpad,
    gq_s,
    gk_s,
    gv_s,
    q_s,
    k_s,
    v_s,
    da_s,
    dr_s,
    d_s,
    t_s,
    gpk_s,
    gpv_s,
):
    head = pl.program_id(0) + first_head
    load_padded(offs, chunk, qp_ref, qpad)
    load_padded(offs, chunk, kp_ref, kpad)
    load_padded(offs, chunk, vp_ref, vpad)
    load_natural(offs, chunk, do_ref, dr_s)
    load_natural(offs, chunk, gp_ref, d_s)
    taps_q, taps_k, taps_v = cq_ref[...], ck_ref[...], cv_ref[...]
    zero8 = jnp.zeros((8, HP), F32)
    for pad in (gq_s, gk_s, gv_s):
        pad[0:8, :] = zero8
        pad[8 + SLOT : 16 + SLOT, :] = zero8
        pad[16 + LIVE : 24 + LIVE, :] = zero8
    lane = lax.broadcasted_iota(jnp.int32, (SUB, HP), 1)

    def prepare(step, carry):
        base = pad_base(step)
        rows = pl.ds(pl.multiple_of(step * SUB, SUB), SUB)
        qc = conv_rows(qpad, taps_q, base)
        q_s[rows, :] = (qc * inv_head(qc)).astype(BF16)
        kc = conv_rows(kpad, taps_k, base)
        k_s[rows, :] = (kc * inv_head(kc)).astype(BF16)
        v_s[rows, :] = conv_rows(vpad, taps_v, base).astype(BF16)
        return carry

    lax.fori_loop(0, NSUB, prepare, 0)
    pkv = pk_ref[...]
    pk_inv = inv_head(pkv)
    pk = (pkv * pk_inv).astype(BF16)
    pv = pv_ref[...].astype(BF16)
    mom, eta, decay = mom_ref[head], step_ref[head], decay_ref[head]
    mem1, mem2, mem_s = state_ref[0, 0], state_ref[0, 1], state_ref[0, 2]
    update0, update1, update_s = state_ref[0, 3], state_ref[0, 4], state_ref[0, 5]

    def scaled(memory):
        return split2(memory * KAPPA)

    def two_nt(x, pieces):
        return dot_nt(x, pieces[0]) + dot_nt(x, pieces[1])

    def two_nn(x, pieces):
        return dot_nn(x, pieces[0]) + dot_nn(x, pieces[1])

    km1, km2, kms = scaled(mem1), scaled(mem2), scaled(mem_s)

    def gates(first, size, memory):
        for start in range(first, first + size, SUB):
            rows = slice(start, start + SUB)
            grad = dr_s[rows, :]
            sig = jax.nn.sigmoid(d_s[rows, :])
            att = a_ref[rows, :]
            comb = jnp.where(lane >= DH, 0.0, att)
            if memory is not None:
                comb = comb + two_nt(q_s[rows, :], memory)
            through = grad * sig
            t_s[rows, :] = (through * comb * (1.0 - sig)).astype(BF16)
            dr_s[rows, :] = through
            low = through.astype(BF16)
            da_s[rows, :] = low
            row_dot = jnp.sum(low.astype(F32) * att, axis=-1, keepdims=True)
            d_s[rows, :] = jnp.where(lane == 0, att[:, DH : DH + 1], row_dot)

    gates(0, CH, None)
    gates(CH, CH, km1)
    gates(2 * CH, CH, km2)
    gates(SLOT, CH, None)
    gates(SLOT + CH, SHORT - CH, kms)
    store_rel(offs, chunk, t_s, dg_ref)

    def span(first, size=CH):
        return slice(first, first + size)

    long0, long1, long2 = span(0), span(CH), span(2 * CH)
    short0, short1 = span(SLOT), span(SLOT + CH, SHORT - CH)

    def padded(rows):
        shift = 16 if rows.start >= SLOT else 8
        return slice(rows.start + shift, rows.stop + shift)

    def outer(left, right):
        high, low = split2(left)
        return dot_tn(high, right) + dot_tn(low, right)

    zero_span = jnp.zeros((CH, HP), F32)

    def reads_back(rows, pieces):
        gq_s[padded(rows), :] = two_nn(dr_s[rows, :].astype(BF16), pieces)

    def zero_out(pad, rows):
        pad[padded(rows), :] = jnp.zeros((rows.stop - rows.start, HP), F32)

    def row_sum(values):
        return jnp.sum(values, axis=0, keepdims=True)

    grad_mem2 = outer(dr_s[long2, :], q_s[long2, :]) * KAPPA
    reads_back(long2, km2)
    zero_out(gk_s, long2)
    zero_out(gv_s, long2)
    total2 = grad_mem2
    rate_decay = -row_sum(grad_mem2 * mem1)
    rate_mom = row_sum(total2 * mem1)
    rate_step = -row_sum(total2 * update1)
    grad_up = total2 * (-eta)
    k1 = k_s[long1, :]
    de1 = two_nt(k1, scaled(grad_up))
    err1 = two_nt(k1, km1) - v_s[long1, :].astype(F32)
    gk_s[padded(long1), :] = two_nn(err1.astype(BF16), scaled(grad_up)) + two_nn(
        de1.astype(BF16), km1
    )
    gv_s[padded(long1), :] = -de1
    grad_mem1 = (
        outer(dr_s[long1, :], q_s[long1, :]) * KAPPA
        + (1.0 - decay) * grad_mem2
        + outer(de1, k1) * KAPPA
    )
    reads_back(long1, km1)
    total1 = grad_mem1 + mom * total2
    rate_step = rate_step - row_sum(total1 * update0)

    def first_span(rows, total):
        pieces = scaled(total * (-eta))
        gv_s[padded(rows), :] = -two_nt(k_s[rows, :], pieces)
        gk_s[padded(rows), :] = -two_nn(v_s[rows, :], pieces)
        gq_s[padded(rows), :] = zero_span

    first_span(long0, total1)
    grad_mem_s = outer(dr_s[short1, :], q_s[short1, :]) * KAPPA
    reads_back(short1, kms)
    zero_out(gk_s, short1)
    zero_out(gv_s, short1)
    rate_step = rate_step - row_sum(grad_mem_s * update_s)
    first_span(short0, grad_mem_s)
    rate_ref[...] = jnp.concatenate(
        [rate_mom, rate_step, rate_decay, jnp.zeros((5, HP), F32)], axis=0
    )

    gpk_s[...] = jnp.zeros((NP, HP), F32)
    gpv_s[...] = jnp.zeros((NP, HP), F32)

    def block(q, da, inv, row_dot, keys, vals, masked):
        prob = jnp.exp(dot_nt(q, keys) * KAPPA) * inv
        if masked:
            prob = jnp.where(causal(prob.shape), prob, 0.0)
        grad = dot_nt(da, vals)
        ds = (prob * (grad - row_dot) * KAPPA).astype(BF16)
        return dot_nn(ds, keys), dot_tn(ds, q), dot_tn(prob.astype(BF16), da)

    def one(rows, base, before=None, base_before=None):
        q, da = q_s[rows, :], da_s[rows, :]
        inv, row_dot = d_s[rows, 0:1], d_s[rows, 1:2]
        here = pl.ds(base, SUB)
        gq, gk, gv = block(q, da, inv, row_dot, k_s[rows, :], v_s[rows, :], True)
        gk_s[here, :] += gk
        gv_s[here, :] += gv
        pq, gpk, gpv = block(q, da, inv, row_dot, pk, pv, False)
        gpk_s[...] += gpk
        gpv_s[...] += gpv
        gq = gq + pq
        if before is not None:
            oq, ok, ov = block(q, da, inv, row_dot, k_s[before, :], v_s[before, :], False)
            there = pl.ds(base_before, SUB)
            gk_s[there, :] += ok
            gv_s[there, :] += ov
            gq = gq + oq
        gq_s[here, :] += gq

    def pair(step, carry):
        rows0 = pl.ds(pl.multiple_of(step * CH, SUB), SUB)
        rows1 = pl.ds(pl.multiple_of(step * CH + SUB, SUB), SUB)
        base0, base1 = pad_base(2 * step), pad_base(2 * step + 1)
        one(rows0, base0)
        one(rows1, base1, rows0, base0)
        return carry

    lax.fori_loop(0, LIVE // CH, pair, 0)
    one(pl.ds(LIVE - SUB, SUB), 16 + LIVE - SUB)
    gpv_ref[...] = gpv_s[...]
    gpk_ref[...] = head_back(pkv, pk_inv, gpk_s[...])

    def norms(step, carry):
        base = pad_base(step)
        here = pl.ds(base, SUB)
        qc = conv_rows(qpad, taps_q, base)
        gq_s[here, :] = head_back(qc, inv_head(qc), gq_s[here, :])
        kc = conv_rows(kpad, taps_k, base)
        gk_s[here, :] = head_back(kc, inv_head(kc), gk_s[here, :])
        return carry

    lax.fori_loop(0, NSUB, norms, 0)

    def conv_back(pre_ref, grad_ref, taps, out_ref, taps_ref):
        def body(step, carry):
            base = pad_base(step)
            rows = pl.ds(pl.multiple_of(step * SUB, SUB), SUB)
            after = grad_ref[pl.ds(base, SUB + 8), :]
            before = pre_ref[pl.ds(pl.multiple_of(base - 8, 8), SUB + 8), :]
            grad = after[:SUB, :]
            total = taps[0:1, :] * grad
            sums = [row_sum(grad * before[8:, :])]
            for j in range(1, KC):
                total = total + taps[j : j + 1, :] * after[j : j + SUB, :]
                sums.append(row_sum(grad * before[8 - j : 8 - j + SUB, :]))
            t_s[rows, :] = total.astype(BF16)
            return tuple(c + s for c, s in zip(carry, sums))

        sums = lax.fori_loop(0, NSUB, body, (jnp.zeros((1, HP), F32),) * KC)
        taps_ref[...] = jnp.concatenate(sums, axis=0)
        store_rel(offs, chunk, t_s, out_ref)

    conv_back(qpad, gq_s, taps_q, dq_ref, gcq_ref)
    conv_back(kpad, gk_s, taps_k, dk_ref, gck_ref)
    conv_back(vpad, gv_s, taps_v, dv_ref, gcv_ref)


def attention_backward(
    offs, rates, wide, grad_out, att, states, convs, persists, heads, chunk, first, some
):
    smem = pl.BlockSpec(memory_space=pltpu.SMEM)
    col = lambda rows: pl.BlockSpec((rows, HP), lambda h, offs: (0, h + first))
    out = lambda rows: pl.BlockSpec((rows, HP), lambda h, offs: (0, h))
    shape = lambda rows, dtype: jax.ShapeDtypeStruct((rows, some * HP), dtype)
    return pl.pallas_call(
        functools.partial(backward_kernel, chunk, first),
        grid_spec=pltpu.PrefetchScalarGridSpec(
            num_scalar_prefetch=1,
            grid=(some,),
            in_specs=[smem] * 3
            + [head_col(i, heads, first) for i in range(4)]
            + [col(LIVE)] * 2
            + [pl.BlockSpec((1, 6, HP, HP), lambda h, offs: (h + first, 0, 0, 0))]
            + [col(KC)] * 3
            + [col(NP)] * 2,
            out_specs=[out(LIVE)] * 4 + [out(KC)] * 3 + [out(NP)] * 2 + [out(8)],
            scratch_shapes=[pltpu.VMEM((PAD_ROWS, HP), F32)] * 6
            + [pltpu.VMEM((LIVE, HP), BF16)] * 4
            + [pltpu.VMEM((LIVE, HP), F32)] * 2
            + [pltpu.VMEM((LIVE, HP), BF16)]
            + [pltpu.VMEM((NP, HP), F32)] * 2,
        ),
        out_shape=[shape(LIVE, BF16)] * 4
        + [shape(KC, F32)] * 3
        + [shape(NP, F32)] * 2
        + [shape(8, F32)],
        compiler_params=pltpu.CompilerParams(vmem_limit_bytes=VMEM),
        name="attention_backward",
    )(offs, *rates, wide, wide, wide, wide, grad_out, att, states, *convs, *persists)


def silu_grad(values):
    sigmoid_v = jax.nn.sigmoid(values)
    return sigmoid_v * (1.0 + values * (1.0 - sigmoid_v))


def rms_backward(values, inv_rms, gain, grad_out):
    scaled = grad_out * gain
    grad_in = inv_rms * (
        scaled - values * inv_rms * inv_rms * jnp.mean(scaled * values, axis=-1, keepdims=True)
    )
    return grad_in, jnp.sum(grad_out * values * inv_rms, axis=0)


def pad_heads(values):
    rows, cols = values.shape
    split = values.reshape(rows, cols // DH, DH)
    return jnp.pad(split, ((0, 0), (0, 0), (0, HP - DH))).reshape(rows, -1)


def cut_heads(values):
    rows, cols = values.shape
    return values.reshape(rows, cols // HP, HP)[:, :, :DH].reshape(rows, -1)


def after(value, token):
    return lax.optimization_barrier((value, token))[0]


def plain(values):
    return with_layout_constraint(values, Layout(tuple(range(values.ndim))))


def tie(*values):
    return lax.optimization_barrier(values)


def interleave(first, second):
    return [v for pair in zip(first, second) for v in pair]


class Team:
    def __init__(self, n_dp, n_tensor):
        self.n_dp, self.n_tensor = n_dp, n_tensor
        self.half = half = n_tensor // 2
        p, t = lax.axis_index("dp"), lax.axis_index("tensor")
        self.t = t
        self.core = p % 2
        self.side = t // half
        self.place = t % half
        self.same = self.core == self.side
        self.core_swap = [(i, i ^ 1) for i in range(n_dp)]
        self.flips = [(t, (t + half) % n_tensor) for t in range(n_tensor)]
        self.parity = [list(range(c, n_dp, 2)) for c in range(2)]
        self.chunk = LIVE // n_tensor

    def swap(self, values):
        return lax.ppermute(values, "dp", self.core_swap)

    def flip(self, values):
        return lax.ppermute(values, "tensor", self.flips)

    def rotate(self, values, by):
        half = self.half
        return lax.ppermute(
            values,
            "tensor",
            [(t, (t // half) * half + (t + by) % half) for t in range(self.n_tensor)],
        )

    def sum_bits(self, values, axis, size, first=1):
        step = first
        while step < size:
            pairs = [(i, i ^ step) for i in range(size)]
            values = values + lax.ppermute(values, axis, pairs)
            step *= 2
        return values

    def by_core(self, mine, other):
        return jnp.concatenate(
            [jnp.where(self.core == 0, mine, other), jnp.where(self.core == 0, other, mine)], axis=0
        )

    def halves(self, values):
        size = values.shape[0] // 2
        low, high = values[:size], values[size:]
        return jnp.where(self.core == 0, low, high), jnp.where(self.core == 0, high, low)

    def share_out(self, rows):
        mine, give = self.halves(rows)
        got = self.swap(give)
        return jnp.where(self.same, mine, got), jnp.where(self.same, got, mine)

    def finish_home(self, own_side, back):
        mine = jnp.where(self.same, own_side, back)
        got = self.swap(jnp.where(self.same, back, own_side))
        return self.by_core(mine, got)

    def sort_blocks(self, block, flipped):
        return jnp.where(self.same, block, flipped), jnp.where(self.same, flipped, block)

    def gather_weights(self, mine, got):
        return lax.all_gather(
            self.by_core(mine, got), "dp", axis=0, tiled=True, axis_index_groups=self.parity
        )

    def scatter_weights(self, grad):
        return lax.psum_scatter(
            grad, "dp", scatter_dimension=0, tiled=True, axis_index_groups=self.parity
        )

    def scatter_first(self, partial):
        size = partial.shape[0] // (self.n_tensor - 2)
        out = []
        for s in range(1, self.half):
            keep = partial[(2 * s - 2) * size : (2 * s - 1) * size]
            send = partial[(2 * s - 1) * size : 2 * s * size]
            out.append((keep.astype(F32) + self.swap(send).astype(F32)).astype(BF16))
        return out

    def scatter_turn(self, sums):
        return [self.rotate(v, self.half - 1 - i) for i, v in enumerate(sums)]

    def scatter_last(self, partial, turned):
        size = partial.shape[0] // 2
        total = partial[:size].astype(F32) + self.swap(partial[size:]).astype(F32)
        for v in turned:
            total = total + v.astype(F32)
        return total

    def reduce_first(self, both, axis=0):
        low, high = jnp.split(both, 2, axis=axis)
        mine = jnp.where(self.core == 0, low, high)
        got = self.swap(jnp.where(self.core == 0, high, low))
        return jnp.where(self.same, mine, got), jnp.where(self.same, got, mine)


def per_device(
    n_dp,
    n_tensor,
    tokens,
    query_weight,
    key_weight,
    value_weight,
    gate_weight,
    output_weight,
    memory_in,
    memory_out,
    swiglu_gate,
    swiglu_up,
    swiglu_down,
    conv_query,
    conv_key,
    conv_value,
    persist_key,
    persist_value,
    momentum,
    step_size,
    decay_rate,
    norm_attn,
    norm_swiglu,
    seq_lengths,
    deal_order,
    cotangent,
):
    team = Team(n_dp, n_tensor)
    half, core, side, place, same, chunk = (
        team.half,
        team.core,
        team.side,
        team.place,
        team.same,
        team.chunk,
    )
    own_rows = tokens.shape[0]
    own_blks = own_rows // BLK
    half_rows = own_rows // 2
    head_feats = query_weight.shape[1]
    heads = head_feats // DH
    grain = next(g for g in (128, 64, 32) if chunk % g == 0)
    per_blk, per_chunk = BLK // grain, chunk // grain
    per_half = half_rows // grain

    tables = jnp.concatenate([deal_order[0], seq_lengths[0]])
    other_tables = team.swap(tables)
    group_tables = jnp.where(same, tables, other_tables)
    n_blks = deal_order.shape[1]
    deal = group_tables[:n_blks]
    long_slot = jnp.where(group_tables[n_blks] == SLOT, 0, 1)

    small = jnp.concatenate(
        [
            conv_query,
            conv_key,
            conv_value,
            persist_key,
            persist_value,
            jnp.pad(
                jnp.stack([momentum, step_size, decay_rate]), ((0, 0), (0, head_feats - heads))
            ),
        ],
        axis=0,
    )
    x_near, x_give = team.share_out(tokens)
    heads_block = jnp.concatenate(
        [query_weight, key_weight, value_weight, gate_weight, output_weight.T], axis=1
    )
    heads_sent = team.flip(heads_block)
    x_near, x_give, heads_sent = tie(x_near, x_give, heads_sent)
    taps_end, persist_end = 3 * KC, 3 * KC + 2 * NP
    def chunk_of(natural):
        return 2 * ((place - natural % half) % half) + (natural // half != core).astype(jnp.int32)

    def compact_of(rel):
        part, within = rel // per_chunk, rel % per_chunk
        natural = (place - part // 2) % half + ((core + part) % 2) * half
        return natural * per_chunk + within

    def dealt_of(rel):
        compact = compact_of(rel)
        blk, sub = compact // per_blk, compact % per_blk
        nat_blk = jnp.where(
            blk < SLOT_BLKS,
            long_slot * SLOT_BLKS + blk,
            (1 - long_slot) * SLOT_BLKS + blk - SLOT_BLKS,
        )
        match = (deal[None, :] == nat_blk[:, None]).astype(jnp.int32)
        dealt = jnp.sum(match * jnp.arange(n_blks, dtype=jnp.int32)[None, :], axis=1)
        shard, row = dealt // own_blks, (dealt % own_blks) * per_blk + sub
        which, within = row // per_half, row % per_half
        piece = (
            (shard // half != side).astype(jnp.int32) * 2 * half
            + 2 * ((place - shard % half) % half)
            + (which != core).astype(jnp.int32)
        )
        return (piece * per_half + within).astype(jnp.int32)

    def rel_of(shard, row):
        nat_blk = deal[shard * own_blks + row // per_blk]
        in_long = nat_blk // SLOT_BLKS == long_slot
        live_here = in_long | (nat_blk % SLOT_BLKS < SHORT_BLKS)
        blk = jnp.where(in_long, nat_blk % SLOT_BLKS, SLOT_BLKS + nat_blk % SLOT_BLKS)
        compact = jnp.minimum(blk, LIVE // BLK - 1) * per_blk + row % per_blk
        rel = chunk_of(compact // per_chunk) * per_chunk + compact % per_chunk
        return rel.astype(jnp.int32), live_here

    def half_index(side_of):
        steps = jnp.arange(n_tensor * per_half, dtype=jnp.int32)
        part, within = steps // per_half, steps % per_half
        shard = (place - part // 2) % half + side_of * half
        return rel_of(shard, ((core + part) % 2) * per_half + within)

    n_sub = LIVE // grain
    gather_index = dealt_of(jnp.arange(n_sub, dtype=jnp.int32))
    near_index, near_live = half_index(side)
    far_index, far_live = half_index(1 - side)
    offs = (chunk_of(jnp.arange(n_tensor, dtype=jnp.int32)) * chunk).astype(jnp.int32)

    def row_mask(live_sub):
        return jnp.broadcast_to(live_sub[:per_half, None], (per_half, grain)).reshape(half_rows, 1)

    near_mask, far_mask = row_mask(near_live), row_mask(far_live)

    near_rows = 2 * chunk
    turns = range(1, half)
    heads_mine, heads_give = team.sort_blocks(heads_block, heads_sent)
    heads_w = team.gather_weights(heads_mine, team.swap(heads_give))
    x_far = team.flip(x_give)
    near_turns = [team.rotate(x_near, s) for s in turns]
    x_near_other = team.swap(x_near)
    x_far, near_turns, x_near_other = tie(x_far, near_turns, x_near_other)

    far_turns = [team.rotate(x_far, s) for s in turns]
    x_far_other = team.swap(x_far)
    near_turns_other = [team.swap(v) for v in near_turns]
    min_sent = team.flip(after(memory_in, x_far))
    c_near, c_give = team.share_out(after(cotangent, x_far))
    far_turns, x_far_other, near_turns_other, min_sent, c_near, c_give = tie(
        far_turns, x_far_other, near_turns_other, min_sent, c_near, c_give
    )

    far_turns_other = [team.swap(v) for v in far_turns]
    min_mine, min_give = team.sort_blocks(memory_in, min_sent)
    min_got = team.swap(min_give)
    min_w = team.gather_weights(min_mine, min_got)
    mout_block, gu_block, down_block = after(
        (
            memory_out.T,
            jnp.concatenate([swiglu_gate, swiglu_up], axis=1),
            swiglu_down.T,
        ),
        far_turns,
    )
    normed, x_own = gather_rows(
        interleave([x_near] + near_turns, [x_near_other] + near_turns_other)
        + interleave([x_far] + far_turns, [x_far_other] + far_turns_other),
        gather_index,
        grain,
        norm_attn,
        per_chunk // STEP,
    )
    small_other = team.flip(after(small, normed))
    mout_sent = team.flip(after(mout_block, normed))
    c_turns = [team.rotate(after(c_near, normed), s) for s in turns]
    heads_w = pad_heads(heads_w)
    wide_feats = 4 * heads * HP
    qkvg_w, out_w = heads_w[:, :wide_feats], heads_w[:, wide_feats:]
    wide = dot_nn(normed, qkvg_w).astype(BF16)
    wide, normed, x_own, mout_sent, c_turns, small_other = tie(
        wide, normed, x_own, mout_sent, c_turns, small_other
    )
    small = jnp.where(same, small, small_other)
    rates = [small[persist_end + i, :heads] for i in range(3)]
    small = pad_heads(small[:persist_end])
    convs = [small[KC * i : KC * (i + 1)] for i in range(3)]
    persists = [small[taps_end + NP * i : taps_end + NP * (i + 1)] for i in range(2)]

    mout_mine, mout_give = team.sort_blocks(mout_block, mout_sent)
    mout_got = team.swap(mout_give)
    mout_w = team.gather_weights(mout_mine, mout_got)
    gu_sent = team.flip(after(gu_block, wide))
    o_low, att, states = attention_forward(
        offs, rates, wide, convs, persists, heads, chunk
    )
    o_low, gu_sent = tie(o_low, gu_sent)

    near, far = slice(0, near_rows), slice(near_rows, None)

    def memory_of(rows, token):
        pre = dot_nn(after(normed, token)[rows], min_w).astype(BF16)
        return pre, jax.nn.silu(pre.astype(F32)).astype(BF16)

    def branch_of(rows, mem):
        return (dot_nt(o_low[rows], out_w) + dot_nt(mem, mout_w)).astype(BF16)

    gu_mine, gu_give = team.sort_blocks(gu_block, gu_sent)
    gu_got = team.swap(gu_give)
    gu_w = team.gather_weights(gu_mine, gu_got)
    c_far = team.flip(after(c_give, o_low))
    mem_pre_far, mem_far = memory_of(far, o_low)
    branch_far = branch_of(far, mem_far)
    branch_far = team.scatter_first(branch_far)
    branch_far, mem_far, gu_got = tie(branch_far, mem_far, gu_got)

    branch_turned = team.scatter_turn(branch_far)
    mem_pre_near, mem_near = memory_of(near, branch_far)
    branch_near = branch_of(near, mem_near)
    branch_turned, branch_near, c_far = tie(branch_turned, branch_near, c_far)
    down_sent = team.flip(after(down_block, c_far))
    x_own = x_own.astype(F32)
    mid_own = x_own + team.scatter_last(branch_near, branch_turned)
    inv_second = lax.rsqrt(jnp.mean(mid_own * mid_own, axis=-1, keepdims=True) + EPS)
    sw_own = (mid_own * inv_second * norm_swiglu).astype(BF16)

    ff = swiglu_gate.shape[1]

    def gates_of(gate_up):
        return gate_up[:, :ff].astype(F32), gate_up[:, ff:].astype(F32)

    def hidden_of(gate_up):
        gate_pre, up_pre = gates_of(gate_up)
        return (jax.nn.silu(gate_pre) * up_pre).astype(BF16)

    def hidden_back(gate_up, grad_hidden):
        gate_pre, up_pre = gates_of(gate_up)
        return jnp.concatenate(
            [
                (grad_hidden * up_pre * silu_grad(gate_pre)).astype(BF16),
                (grad_hidden * jax.nn.silu(gate_pre)).astype(BF16),
            ],
            axis=1,
        )

    sw_turns = [team.rotate(sw_own, s) for s in turns]
    sw_near = jnp.concatenate([sw_own, team.swap(sw_own)], axis=0)
    pre_near = dot_nn(sw_near, gu_w).astype(BF16)
    hidden_near = hidden_of(pre_near)
    sw_turns, pre_near, hidden_near, mid_own, down_sent = tie(
        sw_turns, pre_near, hidden_near, mid_own, down_sent
    )

    down_mine, down_give = team.sort_blocks(down_block, down_sent)
    down_w = team.gather_weights(down_mine, team.swap(down_give))
    c_far_turns = [team.rotate(after(c_far, sw_own), s) for s in turns]
    c_others = [team.swap(after(v, sw_own)) for v in [c_near] + c_turns + [c_far]]
    sw_far = jnp.concatenate(interleave(sw_turns, [team.swap(v) for v in sw_turns]), axis=0)
    pre_far = dot_nn(sw_far, gu_w).astype(BF16)
    hidden_far = hidden_of(pre_far)
    sw_far, pre_far, hidden_far, c_far_turns, c_others = tie(
        sw_far, pre_far, hidden_far, c_far_turns, c_others
    )

    c_others += [team.swap(v) for v in c_far_turns]
    cot_low = gather_rows(
        interleave([c_near] + c_turns + [c_far] + c_far_turns, c_others), gather_index, grain
    )
    cot_parts = [cot_low[:near_rows], cot_low[near_rows:]]
    gu_far = hidden_back(pre_far, dot_nn(cot_parts[1], down_w))
    rows_far = dot_nt(gu_far, gu_w).astype(BF16)
    rows_far, gu_far, hidden_far, sw_far, cot_parts = tie(
        rows_far, gu_far, hidden_far, sw_far, cot_parts
    )

    gu_near = hidden_back(pre_near, dot_nn(cot_parts[0], down_w))
    rows_far = team.scatter_first(rows_far)
    rows_far, gu_near = tie(rows_far, gu_near)
    rows_turned = team.scatter_turn(rows_far)
    rows_near = dot_nt(gu_near, gu_w).astype(BF16)
    grad_gu = (dot_tn(sw_near, gu_near) + dot_tn(sw_far, gu_far)).astype(BF16)
    rows_turned, rows_near, grad_gu, cot_parts, hidden_near, hidden_far = tie(
        rows_turned, rows_near, grad_gu, cot_parts, hidden_near, hidden_far
    )

    grad_gu = team.scatter_weights(grad_gu)
    grad_mid_norm = team.scatter_last(rows_near, rows_turned)
    grad_second, gain_second = rms_backward(mid_own, inv_second, norm_swiglu, grad_mid_norm)
    dz_own = (cot_low[:chunk].astype(F32) + grad_second).astype(BF16)

    def mem_back(cot, pre):
        return (dot_nn(cot, mout_w) * silu_grad(pre.astype(F32))).astype(BF16)

    dz_turns = [team.rotate(dz_own, s) for s in turns]
    dz_near = jnp.concatenate([dz_own, team.swap(dz_own)], axis=0)
    back_near = mem_back(dz_near, mem_pre_near)
    out_near = dot_nn(dz_near, out_w).astype(BF16)
    feed_far = dot_nt(after(hidden_far, dz_own), down_w).astype(BF16)
    feed_near = dot_nt(after(hidden_near, dz_own), down_w).astype(BF16)
    grad_down = (
        dot_tn(cot_parts[0], after(hidden_near, dz_own)) + dot_tn(cot_parts[1], hidden_far)
    ).astype(BF16)
    dz_turns, back_near, out_near, feed_far, feed_near, grad_down, dz_near = tie(
        dz_turns, back_near, out_near, feed_far, feed_near, grad_down, dz_near
    )

    dz_far = jnp.concatenate(interleave(dz_turns, [team.swap(v) for v in dz_turns]), axis=0)
    feed_far = team.scatter_first(feed_far)
    dz_far, feed_far = tie(dz_far, feed_far)

    feed_turned = team.scatter_turn(feed_far)
    grad_down = team.scatter_weights(grad_down)
    dz_all = jnp.concatenate([dz_near, dz_far], axis=0)
    grad_out = jnp.concatenate([out_near, dot_nn(dz_far, out_w).astype(BF16)], axis=0)
    grad_mem = jnp.concatenate([back_near, mem_back(dz_far, mem_pre_far)], axis=0)
    grad_mout = (dot_tn(dz_near, mem_near) + dot_tn(dz_far, mem_far)).astype(BF16)
    grad_min = dot_tn(normed, grad_mem).astype(BF16)
    grad_owt = cut_columns(dot_tn(o_low, dz_all).astype(BF16), n_dp // 2)
    feed_turned, dz_all, grad_out, grad_mem, grad_mout, grad_min, grad_owt, grad_gu = tie(
        feed_turned, dz_all, grad_out, grad_mem, grad_mout, grad_min, grad_owt, grad_gu
    )

    half_heads = heads // 2

    def heads_back(first, token):
        return attention_backward(
            after(offs, token), rates, wide, grad_out, att, states, convs, persists, heads, chunk,
            first, half_heads,
        )

    gu_keep, gu_back = team.reduce_first(grad_gu)
    gu_back = team.flip(gu_back)
    grad_mout = team.scatter_weights(grad_mout)
    grad_min = team.scatter_weights(grad_min)
    y_own = (mid_own + team.scatter_last(feed_near, feed_turned)).astype(BF16)
    y_turns = [team.rotate(y_own, s) for s in turns]
    y_other = team.swap(y_own)
    back_low = heads_back(0, y_own)
    back_low, y_turns, y_other, gu_back, grad_down = tie(
        back_low, y_turns, y_other, gu_back, grad_down
    )

    down_keep, down_back = team.reduce_first(grad_down)
    down_back = team.flip(down_back)
    y_pieces = [y_own, y_other] + interleave(y_turns, [team.swap(v) for v in y_turns])
    y_near = gather_rows(y_pieces, near_index[:per_half], grain)
    y_far = gather_rows(y_pieces, far_index[:per_half], grain)
    y_back = team.flip(y_far)
    back_high = heads_back(half_heads, y_far)
    back_high, down_back, grad_mout = tie(back_high, down_back, grad_mout)

    grad_owt = team.scatter_weights(after(grad_owt, down_back))
    mout_keep, mout_back = team.reduce_first(grad_mout)
    mout_back = team.flip(mout_back)
    small_back = jnp.concatenate(
        [jnp.concatenate(pair, axis=1) for pair in zip(back_low[4:], back_high[4:])], axis=0
    )
    small_x = team.sum_bits(small_back, "dp", n_dp, 2)
    grad_wide = jnp.concatenate(
        [v for pair in zip(back_low[:4], back_high[:4]) for v in pair], axis=1
    )
    grad_normed = (dot_nt(grad_wide, qkvg_w) + dot_nt(grad_mem, min_w)).astype(BF16)
    far_part = gather_rows([grad_normed], far_index, grain)
    far_part, grad_normed, grad_wide, small_x, y_back, grad_min = tie(
        far_part, grad_normed, grad_wide, small_x, y_back, grad_min
    )

    def rows_grad(index, mask, x_half, summed):
        x_rows = x_half.astype(F32)
        inv_first = lax.rsqrt(jnp.mean(x_rows * x_rows, axis=-1, keepdims=True) + EPS)
        grad_first, gain_first = rms_backward(
            x_rows, inv_first, norm_attn, jnp.where(mask, summed, 0.0)
        )
        mid = gather_rows([dz_all], index[:per_half], grain).astype(F32)
        return (mid + grad_first).astype(BF16), gain_first

    split = 2 * half_rows
    far_sums = team.scatter_first(far_part[split:])
    min_keep, min_back = team.reduce_first(grad_min)
    near_part = gather_rows([grad_normed], near_index, grain)
    near_sums = team.scatter_first(near_part[split:])
    far_sums, near_sums, min_keep, min_back, near_part = tie(
        far_sums, near_sums, min_keep, min_back, near_part
    )

    far_turned = team.scatter_turn(far_sums)
    min_back = team.flip(min_back)
    small_flipped = team.flip(small_x)
    grad_heads = dot_tn(after(grad_wide, far_sums), normed).astype(BF16)
    grad_heads = cut_columns(grad_heads, n_dp // 2)
    y_rows = team.finish_home(y_near, y_back)
    far_turned, grad_heads, small_flipped, y_rows, mout_back, min_back = tie(
        far_turned, grad_heads, small_flipped, y_rows, mout_back, min_back
    )

    grad_heads = plain(team.scatter_weights(plain(grad_heads)))
    near_turned = team.scatter_turn(after(near_sums, far_turned))
    grad_far, gain_far = rows_grad(
        far_index, far_mask, x_far, team.scatter_last(far_part[:split], far_turned)
    )
    far_back = team.flip(grad_far)
    near_part = after(near_part, grad_far)
    grad_near, gain_near = rows_grad(
        near_index, near_mask, x_near, team.scatter_last(near_part[:split], near_turned)
    )
    owt_keep, owt_back = team.reduce_first(after(grad_owt, grad_near), -1)
    gains = team.sum_bits(jnp.stack([gain_far + gain_near, gain_second]), "dp", n_dp)
    summed = small_x + small_flipped
    summed = jnp.where(same, summed, team.swap(after(summed, grad_far)))
    total = lambda keep, back: keep.astype(F32) + back.astype(F32)
    grad_gu = total(gu_keep, gu_back)
    grad_down = total(down_keep, down_back)
    grad_mout = total(mout_keep, mout_back)
    grad_min = total(min_keep, min_back)
    grad_heads, grad_near, gains, summed, grad_gu, grad_down, grad_mout, grad_min = tie(
        grad_heads, grad_near, gains, summed, grad_gu, grad_down, grad_mout, grad_min
    )
    heads_keep, heads_other = team.reduce_first(grad_heads, -1)
    heads_other = team.flip(plain(heads_other))
    gains = team.sum_bits(gains, "tensor", n_tensor)
    owt_back = team.flip(owt_back)
    row_grads = team.finish_home(grad_near, far_back)
    grad_heads = total(heads_keep, heads_other)
    grad_owt = total(owt_keep, owt_back)

    own_deal = lax.dynamic_slice_in_dim(deal_order[0], team.t * own_blks, own_blks)
    own_len = jnp.where(own_deal // SLOT_BLKS == 0, seq_lengths[0, 0], seq_lengths[0, 1])
    live_blk = (own_deal % SLOT_BLKS) * BLK < own_len
    live = jnp.broadcast_to(live_blk[:, None], (own_blks, BLK)).reshape(own_rows, 1)

    layer_out = jnp.where(live, y_rows, tokens)
    grad_tokens = jnp.where(live, row_grads, cotangent).astype(F32)

    taps = cut_heads(summed[:persist_end])
    rate_rows = jnp.sum(summed[persist_end : persist_end + 3].reshape(3, heads, HP), axis=-1)

    f = head_feats
    return (
        layer_out,
        grad_tokens,
        grad_heads[:f].T,
        grad_heads[f : 2 * f].T,
        grad_heads[2 * f : 3 * f].T,
        grad_heads[3 * f : 4 * f].T,
        grad_owt,
        grad_min,
        grad_mout.T,
        grad_gu[:, :ff],
        grad_gu[:, ff:],
        grad_down.T,
        taps[:KC],
        taps[KC : 2 * KC],
        taps[2 * KC : 3 * KC],
        taps[3 * KC : 3 * KC + NP],
        taps[3 * KC + NP :],
        rate_rows[0],
        rate_rows[1],
        rate_rows[2],
        gains[0],
        gains[1],
    )


def solution(mesh):
    rows = P(("dp", "tensor"), None)
    cols_w, rows_w = P("dp", "tensor"), P("tensor", "dp")
    feats, rate = P(None, "tensor"), P("tensor")
    weights = (cols_w,) * 4 + (rows_w, cols_w, rows_w, cols_w, cols_w, rows_w)
    smalls = (feats,) * 5 + (rate,) * 3
    return jax.shard_map(
        functools.partial(per_device, mesh.shape["dp"], mesh.shape["tensor"]),
        mesh=mesh,
        in_specs=(rows,) + weights + smalls + (P(), P(), P("dp", None), P("dp", None), rows),
        out_specs=(rows, rows) + weights + smalls + (P(), P()),
        check_vma=False,
    )
```

```python
import functools

import jax
import jax.numpy as jnp
from jax import lax
from jax.experimental import pallas as pl
from jax.experimental.layout import Layout, with_layout_constraint
from jax.experimental.pallas import tpu as pltpu
from jax.sharding import PartitionSpec as P

DH = 96
HP = 128
NP = 64
CH = 512
KC = 4
SLOT = 1536
SHORT = 768
LIVE = SLOT + SHORT
BLK = 128
SUB = 256
NSUB = LIVE // SUB
LONG_SUBS = SLOT // SUB
SLOT_BLKS = SLOT // BLK
SHORT_BLKS = SHORT // BLK
PAD_ROWS = LIVE + 24
EPS = 1e-06
KAPPA = DH ** (-0.5)
VMEM = 56 * 1024 * 1024

F32 = jnp.float32
BF16 = jnp.bfloat16


def dot_nn(a, b):
    return lax.dot_general(a, b, (((1,), (0,)), ((), ())), preferred_element_type=F32)


def dot_nt(a, b):
    return lax.dot_general(a, b, (((1,), (1,)), ((), ())), preferred_element_type=F32)


def dot_tn(a, b):
    return lax.dot_general(a, b, (((0,), (0,)), ((), ())), preferred_element_type=F32)


STEP = 3


def gather_kernel(sources, rows, own_steps, normed, idx_ref, *refs):
    ins, refs = refs[:sources], refs[sources:]
    if normed:
        gain_ref, refs = refs[0], refs[1:]
    out_ref, buf, sem = refs[0], refs[-2], refs[-1]
    step, steps = pl.program_id(0), pl.num_programs(0)
    per_source = ins[0].shape[0] // rows

    def copy(source, first, slot, j):
        return pltpu.make_async_copy(
            source.at[pl.ds(first, rows)], buf.at[slot, pl.ds(j * rows, rows)], sem.at[slot, j]
        )

    def fetch(at, slot):
        for j in range(STEP):
            block = idx_ref[at * STEP + j]
            first = pl.multiple_of((block % per_source) * rows, rows)
            for i in range(sources):

                @pl.when(block // per_source == i)
                def _(i=i, first=first, j=j):
                    copy(ins[i], first, slot, j).start()

    slot = step % 2

    @pl.when(step == 0)
    def _():
        fetch(0, 0)

    @pl.when(step + 1 < steps)
    def _():
        fetch(step + 1, 1 - slot)

    for j in range(STEP):
        copy(ins[0], 0, slot, j).wait()
    block = buf[slot]
    if own_steps:

        @pl.when(step < own_steps)
        def _():
            refs[1][...] = block

    if normed:
        wide = block.astype(F32)
        inv = lax.rsqrt(jnp.mean(wide * wide, axis=-1, keepdims=True) + EPS)
        block = (wide * inv * gain_ref[...]).astype(BF16)
    out_ref[...] = block


def gather_rows(sources, index, rows, gain=None, own_steps=0):
    width, dtype = sources[0].shape[1], sources[0].dtype
    in_specs = [pl.BlockSpec(memory_space=pl.ANY)] * len(sources)
    args = list(sources)
    size = STEP * rows
    if gain is not None:
        in_specs.append(pl.BlockSpec((1, width), lambda i, idx: (0, 0)))
        args.append(gain[None, :])
    out_specs = [pl.BlockSpec((size, width), lambda i, idx: (i, 0))]
    out_shape = [jax.ShapeDtypeStruct((index.shape[0] * rows, width), dtype)]
    if own_steps:
        out_specs.append(
            pl.BlockSpec((size, width), lambda i, idx: (jnp.minimum(i, own_steps - 1), 0))
        )
        out_shape.append(jax.ShapeDtypeStruct((own_steps * size, width), dtype))
    out = pl.pallas_call(
        functools.partial(gather_kernel, len(sources), rows, own_steps, gain is not None),
        grid_spec=pltpu.PrefetchScalarGridSpec(
            num_scalar_prefetch=1,
            grid=(index.shape[0] // STEP,),
            in_specs=in_specs,
            out_specs=out_specs,
            scratch_shapes=[
                pltpu.VMEM((2, size, width), dtype),
                pltpu.SemaphoreType.DMA((2, STEP)),
            ],
        ),
        out_shape=out_shape,
        compiler_params=pltpu.CompilerParams(vmem_limit_bytes=VMEM),
        name="gather_rows",
    )(index, *args)
    return out if own_steps else out[0]


def cut_kernel(groups, in_ref, out_ref):
    width = out_ref.shape[2]
    for g in range(groups):
        out_ref[g, :, :] = in_ref[:DH, g * width : (g + 1) * width]


def cut_columns(values, groups):
    rows, width = values.shape
    return pl.pallas_call(
        functools.partial(cut_kernel, groups),
        grid=(rows // HP,),
        in_specs=[pl.BlockSpec((HP, width), lambda i: (i, 0))],
        out_specs=pl.BlockSpec((groups, DH, width // groups), lambda i: (0, i, 0)),
        out_shape=jax.ShapeDtypeStruct((groups, rows // HP * DH, width // groups), values.dtype),
        compiler_params=pltpu.CompilerParams(vmem_limit_bytes=VMEM),
        name="cut_columns",
    )(values).reshape(-1, width // groups)


def pad_base(step):
    return pl.multiple_of(8 + SUB * step + jnp.where(step >= LONG_SUBS, 8, 0), 8)


def load_padded(offs, chunk, src_ref, pad_ref):
    zero = jnp.zeros((8, HP), F32)
    pad_ref[0:8, :] = zero
    pad_ref[8 + SLOT : 16 + SLOT, :] = zero
    pad_ref[16 + LIVE : 24 + LIVE, :] = zero
    piece = 32
    for q in range(LIVE // chunk):
        start = q * chunk
        for first in range(0, chunk, piece):
            row = start + first
            pad_ref[pl.ds(8 + row + (8 if row >= SLOT else 0), piece), :] = src_ref[
                pl.ds(pl.multiple_of(offs[q] + first, piece), piece), :
            ].astype(F32)


def load_natural(offs, chunk, src_ref, dst_ref):
    for q in range(LIVE // chunk):
        dst_ref[pl.ds(q * chunk, chunk), :] = src_ref[
            pl.ds(pl.multiple_of(offs[q], 32), chunk), :
        ].astype(dst_ref.dtype)


def store_rel(offs, chunk, src_ref, dst_ref):
    for q in range(LIVE // chunk):
        dst_ref[pl.ds(pl.multiple_of(offs[q], 32), chunk), :] = src_ref[
            pl.ds(q * chunk, chunk), :
        ].astype(dst_ref.dtype)


def conv_rows(pad_ref, taps, base):
    window = pad_ref[pl.ds(pl.multiple_of(base - 8, 8), SUB + 8), :]
    total = taps[0:1, :] * window[8:, :]
    for j in range(1, KC):
        total = total + taps[j : j + 1, :] * window[8 - j : 8 - j + SUB, :]
    return total


def inv_head(values):
    return lax.rsqrt(jnp.sum(values * values, axis=-1, keepdims=True) * (1.0 / DH) + EPS)


def lane_sums(values):
    ones = jnp.ones((HP, HP), BF16)
    high, low = split2(values)
    return dot_nn(high, ones) + dot_nn(low, ones)


def inv_lanes(values):
    return lax.rsqrt(lane_sums(values * values) * (1.0 / DH) + EPS)


def head_back(normed, inv, grad):
    return inv * (grad - normed * (lane_sums(grad * normed) * (1.0 / DH)))


def with_ones(values):
    lane = lax.broadcasted_iota(jnp.int32, values.shape, 1)
    return jnp.where(lane == DH, 1.0, values.astype(F32)).astype(BF16)


def causal(shape):
    return lax.broadcasted_iota(jnp.int32, shape, 1) <= lax.broadcasted_iota(jnp.int32, shape, 0)


def split2(values):
    high = values.astype(BF16)
    return high, (values - high.astype(F32)).astype(BF16)


def forward_kernel(
    chunk,
    offs,
    mom_ref,
    step_ref,
    decay_ref,
    qp_ref,
    kp_ref,
    vp_ref,
    gp_ref,
    cq_ref,
    ck_ref,
    cv_ref,
    pk_ref,
    pv_ref,
    o_ref,
    a_ref,
    state_ref,
    q_s,
    k_s,
    v_s,
    qpad,
    kpad,
    vpad,
    iq_s,
    ik_s,
    r_s,
    g_s,
):
    head = pl.program_id(0)
    load_padded(offs, chunk, qp_ref, qpad)
    load_padded(offs, chunk, kp_ref, kpad)
    load_padded(offs, chunk, vp_ref, vpad)
    load_natural(offs, chunk, gp_ref, g_s)
    taps_q, taps_k, taps_v = cq_ref[...], ck_ref[...], cv_ref[...]

    def prepare(step, carry):
        base = pad_base(step)
        rows = pl.ds(pl.multiple_of(step * SUB, SUB), SUB)
        qc = conv_rows(qpad, taps_q, base)
        inv = inv_lanes(qc)
        q_s[rows, :] = (qc * inv).astype(BF16)
        iq_s[rows, :] = inv
        kc = conv_rows(kpad, taps_k, base)
        inv = inv_lanes(kc)
        k_s[rows, :] = (kc * inv).astype(BF16)
        ik_s[rows, :] = inv
        v_s[rows, :] = conv_rows(vpad, taps_v, base).astype(BF16)
        return carry

    lax.fori_loop(0, NSUB, prepare, 0)
    pkv = pk_ref[...]
    pk = (pkv * inv_head(pkv)).astype(BF16)
    pv1 = with_ones(pv_ref[...])

    mom, eta, decay = mom_ref[head], step_ref[head], decay_ref[head]

    def span(first, size=CH):
        return slice(first, first + size)

    def read(memory, rows):
        high, low = split2(memory * KAPPA)
        return dot_nt(q_s[rows, :], high) + dot_nt(q_s[rows, :], low)

    long0, long1, long2 = span(0), span(CH), span(2 * CH)
    short0, short1 = span(SLOT), span(SLOT + CH, SHORT - CH)
    update0 = dot_tn(v_s[long0, :], k_s[long0, :]) * (-KAPPA)
    mem1 = update0 * (-eta)
    high, low = split2(mem1 * KAPPA)
    err1 = dot_nt(k_s[long1, :], high) + dot_nt(k_s[long1, :], low) - v_s[long1, :].astype(F32)
    err_high, err_low = split2(err1)
    update1 = (dot_tn(err_high, k_s[long1, :]) + dot_tn(err_low, k_s[long1, :])) * KAPPA
    sur2 = mom * mem1 - eta * update1
    mem2 = (1.0 - decay) * mem1 + sur2
    update_s = dot_tn(v_s[short0, :], k_s[short0, :]) * (-KAPPA)
    mem_s = update_s * (-eta)
    state_ref[0, 0] = mem1
    state_ref[0, 1] = mem2
    state_ref[0, 2] = mem_s
    state_ref[0, 3] = update0
    state_ref[0, 4] = update1
    state_ref[0, 5] = update_s
    r_s[long0, :] = jnp.zeros((CH, HP), F32)
    r_s[long1, :] = read(mem1, long1)
    r_s[long2, :] = read(mem2, long2)
    r_s[short0, :] = jnp.zeros((CH, HP), F32)
    r_s[short1, :] = read(mem_s, short1)

    lane = lax.broadcasted_iota(jnp.int32, (SUB, HP), 1)

    def finish(rows, acc):
        inv = 1.0 / acc[:, DH : DH + 1]
        att = acc * inv
        kept = jnp.where(lane == DH + 1, iq_s[rows, :], ik_s[rows, :])
        a_ref[rows, :] = jnp.where(lane < DH, att, jnp.where(lane == DH, inv, kept))
        comb = jnp.where(lane >= DH, 0.0, att) + r_s[rows, :]
        g_s[rows, :] = comb * jax.nn.sigmoid(g_s[rows, :])

    def own_part(q, rows):
        e_d = jnp.where(causal((SUB, SUB)), jnp.exp(dot_nt(q, k_s[rows, :]) * KAPPA), 0.0)
        e_p = jnp.exp(dot_nt(q, pk) * KAPPA)
        return dot_nn(e_d.astype(BF16), with_ones(v_s[rows, :])) + dot_nn(e_p.astype(BF16), pv1)

    def pair(step, carry):
        rows0 = pl.ds(pl.multiple_of(step * CH, SUB), SUB)
        rows1 = pl.ds(pl.multiple_of(step * CH + SUB, SUB), SUB)
        finish(rows0, own_part(q_s[rows0, :], rows0))
        q = q_s[rows1, :]
        e_o = jnp.exp(dot_nt(q, k_s[rows0, :]) * KAPPA)
        finish(rows1, own_part(q, rows1) + dot_nn(e_o.astype(BF16), with_ones(v_s[rows0, :])))
        return carry

    lax.fori_loop(0, LIVE // CH, pair, 0)
    tail = pl.ds(LIVE - SUB, SUB)
    finish(tail, own_part(q_s[tail, :], tail))
    store_rel(offs, chunk, g_s, o_ref)


def head_col(part, heads, first=0):
    return pl.BlockSpec((LIVE, HP), lambda h, offs: (0, part * heads + first + h))


def attention_forward(offs, rates, wide, convs, persists, heads, chunk):
    smem = pl.BlockSpec(memory_space=pltpu.SMEM)
    col = lambda rows: pl.BlockSpec((rows, HP), lambda h, offs: (0, h))
    return pl.pallas_call(
        functools.partial(forward_kernel, chunk),
        grid_spec=pltpu.PrefetchScalarGridSpec(
            num_scalar_prefetch=1,
            grid=(heads,),
            in_specs=[smem] * 3
            + [head_col(i, heads) for i in range(4)]
            + [col(KC)] * 3
            + [col(NP)] * 2,
            out_specs=[
                col(LIVE),
                col(LIVE),
                pl.BlockSpec((1, 6, HP, HP), lambda h, offs: (h, 0, 0, 0)),
            ]
            + [col(LIVE)] * 3,
            scratch_shapes=[pltpu.VMEM((PAD_ROWS, HP), F32)] * 3
            + [pltpu.VMEM((LIVE, HP), F32)] * 4,
        ),
        out_shape=[
            jax.ShapeDtypeStruct((LIVE, heads * HP), BF16),
            jax.ShapeDtypeStruct((LIVE, heads * HP), F32),
            jax.ShapeDtypeStruct((heads, 6, HP, HP), F32),
        ]
        + [jax.ShapeDtypeStruct((LIVE, heads * HP), BF16)] * 3,
        compiler_params=pltpu.CompilerParams(vmem_limit_bytes=VMEM),
        name="attention_forward",
    )(offs, *rates, wide, wide, wide, wide, *convs, *persists)


def backward_kernel(
    chunk,
    first_head,
    heads,
    aliased,
    offs,
    mom_ref,
    step_ref,
    decay_ref,
    qp_ref,
    kp_ref,
    vp_ref,
    gp_ref,
    do_ref,
    a_ref,
    q_s,
    k_s,
    v_s,
    state_ref,
    cq_ref,
    ck_ref,
    cv_ref,
    pk_ref,
    pv_ref,
    *refs,
):
    (
        wide_ref,
        gcq_ref,
        gck_ref,
        gcv_ref,
        gpk_ref,
        gpv_ref,
        rate_ref,
        qpad,
        kpad,
        vpad,
        gq_s,
        gk_s,
        gv_s,
        da_s,
        dr_s,
        d_s,
        out_s,
        gpk_s,
        gpv_s,
        sem,
    ) = refs[1:] if aliased else refs

    head = pl.program_id(0) + first_head

    def copies(part):
        column = pl.multiple_of((part * heads + head) * HP, HP)
        return [
            pltpu.make_async_copy(
                out_s.at[part, pl.ds(q * chunk, chunk), :],
                wide_ref.at[pl.ds(pl.multiple_of(offs[q], 32), chunk), pl.ds(column, HP)],
                sem.at[part, q],
            )
            for q in range(LIVE // chunk)
        ]

    def send(part):
        for copy in copies(part):
            copy.start()

    load_padded(offs, chunk, qp_ref, qpad)
    load_padded(offs, chunk, kp_ref, kpad)
    load_padded(offs, chunk, vp_ref, vpad)
    load_natural(offs, chunk, do_ref, dr_s)
    load_natural(offs, chunk, gp_ref, d_s)
    taps_q, taps_k, taps_v = cq_ref[...], ck_ref[...], cv_ref[...]
    zero8 = jnp.zeros((8, HP), F32)
    for pad in (gq_s, gk_s, gv_s):
        pad[0:8, :] = zero8
        pad[8 + SLOT : 16 + SLOT, :] = zero8
        pad[16 + LIVE : 24 + LIVE, :] = zero8
    lane = lax.broadcasted_iota(jnp.int32, (SUB, HP), 1)

    pkv = pk_ref[...]
    pk_inv = inv_head(pkv)
    pk = (pkv * pk_inv).astype(BF16)
    pv = pv_ref[...].astype(BF16)
    mom, eta, decay = mom_ref[head], step_ref[head], decay_ref[head]
    mem1, mem2, mem_s = state_ref[0, 0], state_ref[0, 1], state_ref[0, 2]
    update0, update1, update_s = state_ref[0, 3], state_ref[0, 4], state_ref[0, 5]

    def scaled(memory):
        return split2(memory * KAPPA)

    def two_nt(x, pieces):
        return dot_nt(x, pieces[0]) + dot_nt(x, pieces[1])

    def two_nn(x, pieces):
        return dot_nn(x, pieces[0]) + dot_nn(x, pieces[1])

    km1, km2, kms = scaled(mem1), scaled(mem2), scaled(mem_s)

    def gates(first, size, memory):
        for start in range(first, first + size, SUB):
            rows = slice(start, start + SUB)
            grad = dr_s[rows, :]
            sig = jax.nn.sigmoid(d_s[rows, :])
            att = a_ref[rows, :]
            comb = jnp.where(lane >= DH, 0.0, att)
            if memory is not None:
                comb = comb + two_nt(q_s[rows, :], memory)
            through = grad * sig
            out_s[3, rows, :] = (through * comb * (1.0 - sig)).astype(BF16)
            dr_s[rows, :] = through
            low = through.astype(BF16)
            da_s[rows, :] = low
            row_dot = lane_sums(low.astype(F32) * att)
            d_s[rows, :] = jnp.where(lane == 0, att[:, DH : DH + 1], row_dot)

    gates(0, CH, None)
    gates(CH, CH, km1)
    gates(2 * CH, CH, km2)
    gates(SLOT, CH, None)
    gates(SLOT + CH, SHORT - CH, kms)
    send(3)

    def span(first, size=CH):
        return slice(first, first + size)

    long0, long1, long2 = span(0), span(CH), span(2 * CH)
    short0, short1 = span(SLOT), span(SLOT + CH, SHORT - CH)

    def padded(rows):
        shift = 16 if rows.start >= SLOT else 8
        return slice(rows.start + shift, rows.stop + shift)

    def outer(left, right):
        high, low = split2(left)
        return dot_tn(high, right) + dot_tn(low, right)

    zero_span = jnp.zeros((CH, HP), F32)

    def reads_back(rows, pieces):
        gq_s[padded(rows), :] = two_nn(dr_s[rows, :].astype(BF16), pieces)

    def zero_out(pad, rows):
        pad[padded(rows), :] = jnp.zeros((rows.stop - rows.start, HP), F32)

    def row_sum(values):
        return jnp.sum(values, axis=0, keepdims=True)

    grad_mem2 = outer(dr_s[long2, :], q_s[long2, :]) * KAPPA
    reads_back(long2, km2)
    zero_out(gk_s, long2)
    zero_out(gv_s, long2)
    total2 = grad_mem2
    rate_decay = -row_sum(grad_mem2 * mem1)
    rate_mom = row_sum(total2 * mem1)
    rate_step = -row_sum(total2 * update1)
    grad_up = total2 * (-eta)
    k1 = k_s[long1, :]
    de1 = two_nt(k1, scaled(grad_up))
    err1 = two_nt(k1, km1) - v_s[long1, :].astype(F32)
    gk_s[padded(long1), :] = two_nn(err1.astype(BF16), scaled(grad_up)) + two_nn(
        de1.astype(BF16), km1
    )
    gv_s[padded(long1), :] = -de1
    grad_mem1 = (
        outer(dr_s[long1, :], q_s[long1, :]) * KAPPA
        + (1.0 - decay) * grad_mem2
        + outer(de1, k1) * KAPPA
    )
    reads_back(long1, km1)
    total1 = grad_mem1 + mom * total2
    rate_step = rate_step - row_sum(total1 * update0)

    def first_span(rows, total):
        pieces = scaled(total * (-eta))
        gv_s[padded(rows), :] = -two_nt(k_s[rows, :], pieces)
        gk_s[padded(rows), :] = -two_nn(v_s[rows, :], pieces)
        gq_s[padded(rows), :] = zero_span

    first_span(long0, total1)
    grad_mem_s = outer(dr_s[short1, :], q_s[short1, :]) * KAPPA
    reads_back(short1, kms)
    zero_out(gk_s, short1)
    zero_out(gv_s, short1)
    rate_step = rate_step - row_sum(grad_mem_s * update_s)
    first_span(short0, grad_mem_s)
    rate_ref[...] = jnp.concatenate(
        [rate_mom, rate_step, rate_decay, jnp.zeros((5, HP), F32)], axis=0
    )

    gpk_s[...] = jnp.zeros((NP, HP), F32)
    gpv_s[...] = jnp.zeros((NP, HP), F32)

    def block(q, da, inv, row_dot, keys, vals, masked):
        prob = jnp.exp(dot_nt(q, keys) * KAPPA) * inv
        if masked:
            prob = jnp.where(causal(prob.shape), prob, 0.0)
        grad = dot_nt(da, vals)
        ds = (prob * (grad - row_dot) * KAPPA).astype(BF16)
        return dot_nn(ds, keys), dot_tn(ds, q), dot_tn(prob.astype(BF16), da)

    def one(rows, base, before=None, base_before=None):
        q, da = q_s[rows, :], da_s[rows, :]
        inv, row_dot = d_s[rows, 0:1], d_s[rows, 1:2]
        here = pl.ds(base, SUB)
        gq, gk, gv = block(q, da, inv, row_dot, k_s[rows, :], v_s[rows, :], True)
        gk_s[here, :] += gk
        gv_s[here, :] += gv
        pq, gpk, gpv = block(q, da, inv, row_dot, pk, pv, False)
        gpk_s[...] += gpk
        gpv_s[...] += gpv
        gq = gq + pq
        if before is not None:
            oq, ok, ov = block(q, da, inv, row_dot, k_s[before, :], v_s[before, :], False)
            there = pl.ds(base_before, SUB)
            gk_s[there, :] += ok
            gv_s[there, :] += ov
            gq = gq + oq
        gq_s[here, :] += gq

    def pair(step, carry):
        rows0 = pl.ds(pl.multiple_of(step * CH, SUB), SUB)
        rows1 = pl.ds(pl.multiple_of(step * CH + SUB, SUB), SUB)
        base0, base1 = pad_base(2 * step), pad_base(2 * step + 1)
        one(rows0, base0)
        one(rows1, base1, rows0, base0)
        return carry

    lax.fori_loop(0, LIVE // CH, pair, 0)
    one(pl.ds(LIVE - SUB, SUB), 16 + LIVE - SUB)
    gpv_ref[...] = gpv_s[...]
    gpk_ref[...] = head_back(pkv * pk_inv, pk_inv, gpk_s[...])

    def norms(step, carry):
        here = pl.ds(pad_base(step), SUB)
        rows = pl.ds(pl.multiple_of(step * SUB, SUB), SUB)
        inv_q, inv_k = a_ref[rows, DH + 1 : DH + 2], a_ref[rows, DH + 2 : DH + 3]
        gq_s[here, :] = head_back(q_s[rows, :].astype(F32), inv_q, gq_s[here, :])
        gk_s[here, :] = head_back(k_s[rows, :].astype(F32), inv_k, gk_s[here, :])
        return carry

    lax.fori_loop(0, NSUB, norms, 0)

    def conv_back(pre_ref, grad_ref, taps, part, taps_ref):
        def body(step, carry):
            base = pad_base(step)
            rows = pl.ds(pl.multiple_of(step * SUB, SUB), SUB)
            after = grad_ref[pl.ds(base, SUB + 8), :]
            before = pre_ref[pl.ds(pl.multiple_of(base - 8, 8), SUB + 8), :]
            grad = after[:SUB, :]
            total = taps[0:1, :] * grad
            sums = [row_sum(grad * before[8:, :])]
            for j in range(1, KC):
                total = total + taps[j : j + 1, :] * after[j : j + SUB, :]
                sums.append(row_sum(grad * before[8 - j : 8 - j + SUB, :]))
            out_s[part, rows, :] = total.astype(BF16)
            return tuple(c + s for c, s in zip(carry, sums))

        sums = lax.fori_loop(0, NSUB, body, (jnp.zeros((1, HP), F32),) * KC)
        taps_ref[...] = jnp.concatenate(sums, axis=0)
        send(part)

    conv_back(qpad, gq_s, taps_q, 0, gcq_ref)
    conv_back(kpad, gk_s, taps_k, 1, gck_ref)
    conv_back(vpad, gv_s, taps_v, 2, gcv_ref)
    for part in range(4):
        for copy in copies(part):
            copy.wait()


def attention_backward(
    offs, rates, wide, grad_out, kept, states, convs, persists, heads, chunk, first, some, into=None
):
    smem = pl.BlockSpec(memory_space=pltpu.SMEM)
    anywhere = pl.BlockSpec(memory_space=pl.ANY)
    args = [*rates, wide, wide, wide, wide, grad_out, *kept, states, *convs, *persists]
    args += [] if into is None else [into]
    col = lambda rows: pl.BlockSpec((rows, HP), lambda h, offs: (0, h + first))
    out = lambda rows: pl.BlockSpec((rows, HP), lambda h, offs: (0, h))
    shape = lambda rows, dtype: jax.ShapeDtypeStruct((rows, some * HP), dtype)
    return pl.pallas_call(
        functools.partial(backward_kernel, chunk, first, heads, into is not None),
        grid_spec=pltpu.PrefetchScalarGridSpec(
            num_scalar_prefetch=1,
            grid=(some,),
            in_specs=[smem] * 3
            + [head_col(i, heads, first) for i in range(4)]
            + [col(LIVE)] * 5
            + [pl.BlockSpec((1, 6, HP, HP), lambda h, offs: (h + first, 0, 0, 0))]
            + [col(KC)] * 3
            + [col(NP)] * 2
            + ([] if into is None else [anywhere]),
            out_specs=[anywhere] + [out(KC)] * 3 + [out(NP)] * 2 + [out(8)],
            scratch_shapes=[pltpu.VMEM((PAD_ROWS, HP), F32)] * 6
            + [pltpu.VMEM((LIVE, HP), BF16)]
            + [pltpu.VMEM((LIVE, HP), F32)] * 2
            + [pltpu.VMEM((4, LIVE, HP), BF16)]
            + [pltpu.VMEM((NP, HP), F32)] * 2
            + [pltpu.SemaphoreType.DMA((4, LIVE // chunk))],
        ),
        out_shape=[jax.ShapeDtypeStruct((LIVE, 4 * heads * HP), BF16)]
        + [shape(KC, F32)] * 3
        + [shape(NP, F32)] * 2
        + [shape(8, F32)],
        compiler_params=pltpu.CompilerParams(vmem_limit_bytes=VMEM),
        input_output_aliases={} if into is None else {len(args): 0},
        name="attention_backward",
    )(offs, *args)


def silu_grad(values):
    sigmoid_v = jax.nn.sigmoid(values)
    return sigmoid_v * (1.0 + values * (1.0 - sigmoid_v))


def rms_backward(values, inv_rms, gain, grad_out):
    scaled = grad_out * gain
    grad_in = inv_rms * (
        scaled - values * inv_rms * inv_rms * jnp.mean(scaled * values, axis=-1, keepdims=True)
    )
    return grad_in, jnp.sum(grad_out * values * inv_rms, axis=0)


def pad_heads(values):
    rows, cols = values.shape
    split = values.reshape(rows, cols // DH, DH)
    return jnp.pad(split, ((0, 0), (0, 0), (0, HP - DH))).reshape(rows, -1)


def cut_heads(values):
    rows, cols = values.shape
    return values.reshape(rows, cols // HP, HP)[:, :, :DH].reshape(rows, -1)


def after(value, token):
    return lax.optimization_barrier((value, token))[0]


def plain(values):
    return with_layout_constraint(values, Layout(tuple(range(values.ndim))))


def tie(*values):
    return lax.optimization_barrier(values)


def interleave(first, second):
    return [v for pair in zip(first, second) for v in pair]


class Team:
    def __init__(self, n_dp, n_tensor):
        self.n_dp, self.n_tensor = n_dp, n_tensor
        self.half = half = n_tensor // 2
        p, t = lax.axis_index("dp"), lax.axis_index("tensor")
        self.t = t
        self.core = p % 2
        self.side = t // half
        self.place = t % half
        self.same = self.core == self.side
        self.core_swap = [(i, i ^ 1) for i in range(n_dp)]
        self.flips = [(t, (t + half) % n_tensor) for t in range(n_tensor)]
        self.parity = [list(range(c, n_dp, 2)) for c in range(2)]
        self.chunk = LIVE // n_tensor

    def swap(self, values):
        return lax.ppermute(values, "dp", self.core_swap)

    def flip(self, values):
        return lax.ppermute(values, "tensor", self.flips)

    def rotate(self, values, by):
        half = self.half
        return lax.ppermute(
            values,
            "tensor",
            [(t, (t // half) * half + (t + by) % half) for t in range(self.n_tensor)],
        )

    def sum_bits(self, values, axis, size, first=1):
        step = first
        while step < size:
            pairs = [(i, i ^ step) for i in range(size)]
            values = values + lax.ppermute(values, axis, pairs)
            step *= 2
        return values

    def by_core(self, mine, other):
        return jnp.concatenate(
            [jnp.where(self.core == 0, mine, other), jnp.where(self.core == 0, other, mine)], axis=0
        )

    def halves(self, values):
        size = values.shape[0] // 2
        low, high = values[:size], values[size:]
        return jnp.where(self.core == 0, low, high), jnp.where(self.core == 0, high, low)

    def share_out(self, rows):
        mine, give = self.halves(rows)
        got = self.swap(give)
        return jnp.where(self.same, mine, got), jnp.where(self.same, got, mine)

    def finish_home(self, own_side, back):
        mine = jnp.where(self.same, own_side, back)
        got = self.swap(jnp.where(self.same, back, own_side))
        return self.by_core(mine, got)

    def sort_blocks(self, block, flipped):
        return jnp.where(self.same, block, flipped), jnp.where(self.same, flipped, block)

    def gather_weights(self, mine, got):
        return lax.all_gather(
            self.by_core(mine, got), "dp", axis=0, tiled=True, axis_index_groups=self.parity
        )

    def scatter_weights(self, grad):
        return lax.psum_scatter(
            grad, "dp", scatter_dimension=0, tiled=True, axis_index_groups=self.parity
        )

    def scatter_first(self, partial):
        size = partial.shape[0] // (self.n_tensor - 2)
        out = []
        for s in range(1, self.half):
            keep = partial[(2 * s - 2) * size : (2 * s - 1) * size]
            send = partial[(2 * s - 1) * size : 2 * s * size]
            out.append((keep.astype(F32) + self.swap(send).astype(F32)).astype(BF16))
        return out

    def scatter_turn(self, sums):
        return [self.rotate(v, self.half - 1 - i) for i, v in enumerate(sums)]

    def scatter_last(self, partial, turned):
        size = partial.shape[0] // 2
        total = partial[:size].astype(F32) + self.swap(partial[size:]).astype(F32)
        for v in turned:
            total = total + v.astype(F32)
        return total

    def reduce_first(self, both, axis=0):
        low, high = jnp.split(both, 2, axis=axis)
        mine = jnp.where(self.core == 0, low, high)
        got = self.swap(jnp.where(self.core == 0, high, low))
        return jnp.where(self.same, mine, got), jnp.where(self.same, got, mine)


def per_device(
    n_dp,
    n_tensor,
    tokens,
    query_weight,
    key_weight,
    value_weight,
    gate_weight,
    output_weight,
    memory_in,
    memory_out,
    swiglu_gate,
    swiglu_up,
    swiglu_down,
    conv_query,
    conv_key,
    conv_value,
    persist_key,
    persist_value,
    momentum,
    step_size,
    decay_rate,
    norm_attn,
    norm_swiglu,
    seq_lengths,
    deal_order,
    cotangent,
):
    team = Team(n_dp, n_tensor)
    half, core, side, place, same, chunk = (
        team.half,
        team.core,
        team.side,
        team.place,
        team.same,
        team.chunk,
    )
    own_rows = tokens.shape[0]
    own_blks = own_rows // BLK
    half_rows = own_rows // 2
    head_feats = query_weight.shape[1]
    heads = head_feats // DH
    grain = next(g for g in (128, 64, 32) if chunk % g == 0)
    per_blk, per_chunk = BLK // grain, chunk // grain
    per_half = half_rows // grain

    tables = jnp.concatenate([deal_order[0], seq_lengths[0]])
    other_tables = team.swap(tables)
    group_tables = jnp.where(same, tables, other_tables)
    n_blks = deal_order.shape[1]
    deal = group_tables[:n_blks]
    long_slot = jnp.where(group_tables[n_blks] == SLOT, 0, 1)

    small = jnp.concatenate(
        [
            conv_query,
            conv_key,
            conv_value,
            persist_key,
            persist_value,
            jnp.pad(
                jnp.stack([momentum, step_size, decay_rate]), ((0, 0), (0, head_feats - heads))
            ),
        ],
        axis=0,
    )
    x_near, x_give = team.share_out(tokens)
    heads_block = jnp.concatenate(
        [query_weight, key_weight, value_weight, gate_weight, output_weight.T], axis=1
    )
    heads_sent = team.flip(heads_block)
    x_near, x_give, heads_sent, small = tie(x_near, x_give, heads_sent, small)
    taps_end, persist_end = 3 * KC, 3 * KC + 2 * NP
    def chunk_of(natural):
        return 2 * ((place - natural % half) % half) + (natural // half != core).astype(jnp.int32)

    def compact_of(rel):
        part, within = rel // per_chunk, rel % per_chunk
        natural = (place - part // 2) % half + ((core + part) % 2) * half
        return natural * per_chunk + within

    def dealt_of(rel):
        compact = compact_of(rel)
        blk, sub = compact // per_blk, compact % per_blk
        nat_blk = jnp.where(
            blk < SLOT_BLKS,
            long_slot * SLOT_BLKS + blk,
            (1 - long_slot) * SLOT_BLKS + blk - SLOT_BLKS,
        )
        match = (deal[None, :] == nat_blk[:, None]).astype(jnp.int32)
        dealt = jnp.sum(match * jnp.arange(n_blks, dtype=jnp.int32)[None, :], axis=1)
        shard, row = dealt // own_blks, (dealt % own_blks) * per_blk + sub
        which, within = row // per_half, row % per_half
        piece = (
            (shard // half != side).astype(jnp.int32) * 2 * half
            + 2 * ((place - shard % half) % half)
            + (which != core).astype(jnp.int32)
        )
        return (piece * per_half + within).astype(jnp.int32)

    def rel_of(shard, row):
        nat_blk = deal[shard * own_blks + row // per_blk]
        in_long = nat_blk // SLOT_BLKS == long_slot
        live_here = in_long | (nat_blk % SLOT_BLKS < SHORT_BLKS)
        blk = jnp.where(in_long, nat_blk % SLOT_BLKS, SLOT_BLKS + nat_blk % SLOT_BLKS)
        compact = jnp.minimum(blk, LIVE // BLK - 1) * per_blk + row % per_blk
        rel = chunk_of(compact // per_chunk) * per_chunk + compact % per_chunk
        return rel.astype(jnp.int32), live_here

    def half_index(side_of):
        steps = jnp.arange(n_tensor * per_half, dtype=jnp.int32)
        part, within = steps // per_half, steps % per_half
        shard = (place - part // 2) % half + side_of * half
        return rel_of(shard, ((core + part) % 2) * per_half + within)

    n_sub = LIVE // grain
    gather_index = dealt_of(jnp.arange(n_sub, dtype=jnp.int32))
    near_index, near_live = half_index(side)
    far_index, far_live = half_index(1 - side)
    offs = (chunk_of(jnp.arange(n_tensor, dtype=jnp.int32)) * chunk).astype(jnp.int32)

    def row_mask(live_sub):
        return jnp.broadcast_to(live_sub[:per_half, None], (per_half, grain)).reshape(half_rows, 1)

    near_mask, far_mask = row_mask(near_live), row_mask(far_live)

    near_rows = 2 * chunk
    turns = range(1, half)
    heads_mine, heads_give = team.sort_blocks(heads_block, heads_sent)
    heads_w = team.gather_weights(heads_mine, team.swap(heads_give))
    x_far = team.flip(x_give)
    near_turns = [team.rotate(x_near, s) for s in turns]
    x_near_other = team.swap(x_near)
    x_far, near_turns, x_near_other = tie(x_far, near_turns, x_near_other)

    far_turns = [team.rotate(x_far, s) for s in turns]
    x_far_other = team.swap(x_far)
    near_turns_other = [team.swap(v) for v in near_turns]
    min_sent = team.flip(after(memory_in, x_far))
    c_near, c_give = team.share_out(after(cotangent, x_far))
    small_other = team.flip(after(small, x_far))
    far_turns, x_far_other, near_turns_other, min_sent, c_near, c_give, small_other = tie(
        far_turns, x_far_other, near_turns_other, min_sent, c_near, c_give, small_other
    )

    far_turns_other = [team.swap(v) for v in far_turns]
    min_mine, min_give = team.sort_blocks(memory_in, min_sent)
    min_got = team.swap(min_give)
    min_w = team.gather_weights(min_mine, min_got)
    mout_block, gu_block, down_block = after(
        (
            memory_out.T,
            jnp.concatenate([swiglu_gate, swiglu_up], axis=1),
            swiglu_down.T,
        ),
        far_turns,
    )
    normed, x_own = gather_rows(
        interleave([x_near] + near_turns, [x_near_other] + near_turns_other)
        + interleave([x_far] + far_turns, [x_far_other] + far_turns_other),
        gather_index,
        grain,
        norm_attn,
        per_chunk // STEP,
    )
    mout_sent = team.flip(after(mout_block, normed))
    c_turns = [team.rotate(after(c_near, normed), s) for s in turns]
    heads_w = pad_heads(heads_w)
    wide_feats = 4 * heads * HP
    qkvg_w, out_w = heads_w[:, :wide_feats], heads_w[:, wide_feats:]
    wide = dot_nn(normed, qkvg_w).astype(BF16)
    wide, normed, x_own, mout_sent = tie(wide, normed, x_own, mout_sent)
    small = jnp.where(same, small, small_other)
    rates = [small[persist_end + i, :heads] for i in range(3)]
    small = pad_heads(small[:persist_end])
    convs = [small[KC * i : KC * (i + 1)] for i in range(3)]
    persists = [small[taps_end + NP * i : taps_end + NP * (i + 1)] for i in range(2)]

    mout_mine, mout_give = team.sort_blocks(mout_block, mout_sent)
    mout_got = team.swap(mout_give)
    mout_w = team.gather_weights(mout_mine, mout_got)
    gu_sent = team.flip(after(gu_block, wide))
    o_low, att, states, *heads_kept = attention_forward(
        offs, rates, wide, convs, persists, heads, chunk
    )
    o_low, gu_sent, c_turns = tie(o_low, gu_sent, c_turns)

    near, far = slice(0, near_rows), slice(near_rows, None)

    def memory_of(rows, token):
        pre = dot_nn(after(normed, token)[rows], min_w).astype(BF16)
        return pre, jax.nn.silu(pre.astype(F32)).astype(BF16)

    def branch_of(rows, mem):
        return (dot_nt(o_low[rows], out_w) + dot_nt(mem, mout_w)).astype(BF16)

    gu_mine, gu_give = team.sort_blocks(gu_block, gu_sent)
    gu_got = team.swap(gu_give)
    gu_w = team.gather_weights(gu_mine, gu_got)
    c_far = team.flip(after(c_give, o_low))
    mem_pre_far, mem_far = memory_of(far, o_low)
    branch_far = branch_of(far, mem_far)
    branch_far = team.scatter_first(branch_far)
    branch_far, mem_far, gu_got = tie(branch_far, mem_far, gu_got)

    branch_turned = team.scatter_turn(branch_far)
    mem_pre_near, mem_near = memory_of(near, branch_far)
    branch_near = branch_of(near, mem_near)
    branch_turned, branch_near, c_far = tie(branch_turned, branch_near, c_far)
    down_sent = team.flip(after(down_block, c_far))
    x_own = x_own.astype(F32)
    mid_own = x_own + team.scatter_last(branch_near, branch_turned)
    inv_second = lax.rsqrt(jnp.mean(mid_own * mid_own, axis=-1, keepdims=True) + EPS)
    sw_own = (mid_own * inv_second * norm_swiglu).astype(BF16)

    ff = swiglu_gate.shape[1]

    def gates_of(gate_up):
        return gate_up[:, :ff].astype(F32), gate_up[:, ff:].astype(F32)

    def hidden_of(gate_up):
        gate_pre, up_pre = gates_of(gate_up)
        return (jax.nn.silu(gate_pre) * up_pre).astype(BF16)

    def hidden_back(gate_up, grad_hidden):
        gate_pre, up_pre = gates_of(gate_up)
        return jnp.concatenate(
            [
                (grad_hidden * up_pre * silu_grad(gate_pre)).astype(BF16),
                (grad_hidden * jax.nn.silu(gate_pre)).astype(BF16),
            ],
            axis=1,
        )

    sw_turns = [team.rotate(sw_own, s) for s in turns]
    sw_near = jnp.concatenate([sw_own, team.swap(sw_own)], axis=0)
    pre_near = dot_nn(sw_near, gu_w).astype(BF16)
    hidden_near = hidden_of(pre_near)
    sw_turns, pre_near, hidden_near, mid_own, down_sent = tie(
        sw_turns, pre_near, hidden_near, mid_own, down_sent
    )

    down_mine, down_give = team.sort_blocks(down_block, down_sent)
    down_w = team.gather_weights(down_mine, team.swap(down_give))
    c_far_turns = [team.rotate(after(c_far, sw_own), s) for s in turns]
    c_others = [team.swap(after(v, sw_own)) for v in [c_near] + c_turns + [c_far]]
    sw_far = jnp.concatenate(interleave(sw_turns, [team.swap(v) for v in sw_turns]), axis=0)
    pre_far = dot_nn(sw_far, gu_w).astype(BF16)
    hidden_far = hidden_of(pre_far)
    sw_far, pre_far, hidden_far, c_far_turns, c_others = tie(
        sw_far, pre_far, hidden_far, c_far_turns, c_others
    )

    c_others += [team.swap(v) for v in c_far_turns]
    cot_low = gather_rows(
        interleave([c_near] + c_turns + [c_far] + c_far_turns, c_others), gather_index, grain
    )
    cot_parts = [cot_low[:near_rows], cot_low[near_rows:]]
    gu_far = hidden_back(pre_far, dot_nn(cot_parts[1], down_w))
    rows_far = dot_nt(gu_far, gu_w).astype(BF16)
    rows_far, gu_far, hidden_far, sw_far, cot_parts = tie(
        rows_far, gu_far, hidden_far, sw_far, cot_parts
    )

    gu_near = hidden_back(pre_near, dot_nn(cot_parts[0], down_w))
    rows_far = team.scatter_first(rows_far)
    rows_far, gu_near = tie(rows_far, gu_near)
    rows_turned = team.scatter_turn(rows_far)
    rows_near = dot_nt(gu_near, gu_w).astype(BF16)
    grad_gu = (dot_tn(sw_near, gu_near) + dot_tn(sw_far, gu_far)).astype(BF16)
    rows_turned, rows_near, grad_gu, cot_parts, hidden_near, hidden_far = tie(
        rows_turned, rows_near, grad_gu, cot_parts, hidden_near, hidden_far
    )

    grad_gu = team.scatter_weights(grad_gu)
    grad_mid_norm = team.scatter_last(rows_near, rows_turned)
    grad_second, gain_second = rms_backward(mid_own, inv_second, norm_swiglu, grad_mid_norm)
    dz_own = (cot_low[:chunk].astype(F32) + grad_second).astype(BF16)

    def mem_back(cot, pre):
        return (dot_nn(cot, mout_w) * silu_grad(pre.astype(F32))).astype(BF16)

    dz_turns = [team.rotate(dz_own, s) for s in turns]
    dz_near = jnp.concatenate([dz_own, team.swap(dz_own)], axis=0)
    back_near = mem_back(dz_near, mem_pre_near)
    out_near = dot_nn(dz_near, out_w).astype(BF16)
    feed_far = dot_nt(after(hidden_far, dz_own), down_w).astype(BF16)
    feed_near = dot_nt(after(hidden_near, dz_own), down_w).astype(BF16)
    grad_down = (
        dot_tn(cot_parts[0], after(hidden_near, dz_own)) + dot_tn(cot_parts[1], hidden_far)
    ).astype(BF16)
    dz_turns, back_near, out_near, feed_far, feed_near, grad_down, dz_near = tie(
        dz_turns, back_near, out_near, feed_far, feed_near, grad_down, dz_near
    )

    dz_far = jnp.concatenate(interleave(dz_turns, [team.swap(v) for v in dz_turns]), axis=0)
    feed_far = team.scatter_first(feed_far)
    dz_far, feed_far = tie(dz_far, feed_far)

    feed_turned = team.scatter_turn(feed_far)
    grad_down = team.scatter_weights(grad_down)
    dz_all = jnp.concatenate([dz_near, dz_far], axis=0)
    grad_out = jnp.concatenate([out_near, dot_nn(dz_far, out_w).astype(BF16)], axis=0)
    grad_mem = jnp.concatenate([back_near, mem_back(dz_far, mem_pre_far)], axis=0)
    grad_mout = (dot_tn(dz_near, mem_near) + dot_tn(dz_far, mem_far)).astype(BF16)
    grad_min = dot_tn(normed, grad_mem).astype(BF16)
    grad_owt = cut_columns(dot_tn(o_low, dz_all).astype(BF16), n_dp // 2)
    feed_turned, dz_all, grad_out, grad_mem, grad_mout, grad_min, grad_owt, grad_gu = tie(
        feed_turned, dz_all, grad_out, grad_mem, grad_mout, grad_min, grad_owt, grad_gu
    )

    half_heads = heads // 2

    def heads_back(first, token, into=None):
        return attention_backward(
            after(offs, token),
            rates,
            wide,
            grad_out,
            [att] + heads_kept,
            states,
            convs,
            persists,
            heads,
            chunk,
            first,
            half_heads,
            into,
        )

    gu_keep, gu_back = team.reduce_first(grad_gu)
    gu_back = team.flip(gu_back)
    grad_mout = team.scatter_weights(grad_mout)
    grad_min = team.scatter_weights(grad_min)
    y_own = (mid_own + team.scatter_last(feed_near, feed_turned)).astype(BF16)
    y_turns = [team.rotate(y_own, s) for s in turns]
    y_other = team.swap(y_own)
    back_low = heads_back(0, y_own)
    back_low, y_turns, y_other, gu_back, grad_down = tie(
        back_low, y_turns, y_other, gu_back, grad_down
    )

    down_keep, down_back = team.reduce_first(grad_down)
    down_back = team.flip(down_back)
    y_pieces = [y_own, y_other] + interleave(y_turns, [team.swap(v) for v in y_turns])
    y_near = gather_rows(y_pieces, near_index[:per_half], grain)
    y_far = gather_rows(y_pieces, far_index[:per_half], grain)
    y_back = team.flip(y_far)
    back_high = heads_back(half_heads, y_far, back_low[0])
    back_high, down_back, grad_mout = tie(back_high, down_back, grad_mout)

    grad_owt = team.scatter_weights(after(grad_owt, down_back))
    mout_keep, mout_back = team.reduce_first(grad_mout)
    mout_back = team.flip(mout_back)
    small_back = jnp.concatenate(
        [jnp.concatenate(pair, axis=1) for pair in zip(back_low[1:], back_high[1:])], axis=0
    )
    small_x = team.sum_bits(small_back, "dp", n_dp, 2)
    grad_wide = back_high[0]
    grad_normed = (dot_nt(grad_wide, qkvg_w) + dot_nt(grad_mem, min_w)).astype(BF16)
    far_part = gather_rows([grad_normed], far_index, grain)
    far_part, grad_normed, grad_wide, small_x, y_back, grad_min = tie(
        far_part, grad_normed, grad_wide, small_x, y_back, grad_min
    )

    def rows_grad(index, mask, x_half, summed):
        x_rows = x_half.astype(F32)
        inv_first = lax.rsqrt(jnp.mean(x_rows * x_rows, axis=-1, keepdims=True) + EPS)
        grad_first, gain_first = rms_backward(
            x_rows, inv_first, norm_attn, jnp.where(mask, summed, 0.0)
        )
        mid = gather_rows([dz_all], index[:per_half], grain).astype(F32)
        return (mid + grad_first).astype(BF16), gain_first

    split = 2 * half_rows
    far_sums = team.scatter_first(far_part[split:])
    min_keep, min_back = team.reduce_first(grad_min)
    near_part = gather_rows([grad_normed], near_index, grain)
    near_sums = team.scatter_first(near_part[split:])
    far_sums, near_sums, min_keep, min_back, near_part = tie(
        far_sums, near_sums, min_keep, min_back, near_part
    )

    far_turned = team.scatter_turn(far_sums)
    min_back = team.flip(min_back)
    small_flipped = team.flip(small_x)
    grad_heads = dot_tn(after(grad_wide, far_sums), normed).astype(BF16)
    grad_heads = cut_columns(grad_heads, n_dp // 2)
    y_rows = team.finish_home(y_near, y_back)
    far_turned, grad_heads, small_flipped, y_rows, mout_back, min_back = tie(
        far_turned, grad_heads, small_flipped, y_rows, mout_back, min_back
    )

    grad_heads = plain(team.scatter_weights(plain(grad_heads)))
    near_turned = team.scatter_turn(after(near_sums, far_turned))
    grad_far, gain_far = rows_grad(
        far_index, far_mask, x_far, team.scatter_last(far_part[:split], far_turned)
    )
    far_back = team.flip(grad_far)
    near_part = after(near_part, grad_far)
    grad_near, gain_near = rows_grad(
        near_index, near_mask, x_near, team.scatter_last(near_part[:split], near_turned)
    )
    owt_keep, owt_back = team.reduce_first(after(grad_owt, grad_near), -1)
    gains = team.sum_bits(jnp.stack([gain_far + gain_near, gain_second]), "dp", n_dp)
    summed = small_x + small_flipped
    summed = jnp.where(same, summed, team.swap(after(summed, grad_far)))
    total = lambda keep, back: keep.astype(F32) + back.astype(F32)
    grad_gu = total(gu_keep, gu_back)
    grad_down = total(down_keep, down_back)
    grad_mout = total(mout_keep, mout_back)
    grad_min = total(min_keep, min_back)
    grad_heads, grad_near, gains, summed, grad_gu, grad_down, grad_mout, grad_min = tie(
        grad_heads, grad_near, gains, summed, grad_gu, grad_down, grad_mout, grad_min
    )
    heads_keep, heads_other = team.reduce_first(grad_heads, -1)
    heads_other = team.flip(plain(heads_other))
    gains = team.sum_bits(gains, "tensor", n_tensor)
    owt_back = team.flip(owt_back)
    row_grads = team.finish_home(grad_near, far_back)
    grad_heads = total(heads_keep, heads_other)
    grad_owt = total(owt_keep, owt_back)

    own_deal = lax.dynamic_slice_in_dim(deal_order[0], team.t * own_blks, own_blks)
    own_len = jnp.where(own_deal // SLOT_BLKS == 0, seq_lengths[0, 0], seq_lengths[0, 1])
    live_blk = (own_deal % SLOT_BLKS) * BLK < own_len
    live = jnp.broadcast_to(live_blk[:, None], (own_blks, BLK)).reshape(own_rows, 1)

    layer_out = jnp.where(live, y_rows, tokens)
    grad_tokens = jnp.where(live, row_grads, cotangent).astype(F32)

    taps = cut_heads(summed[:persist_end])
    rate_rows = jnp.sum(summed[persist_end : persist_end + 3].reshape(3, heads, HP), axis=-1)

    f = head_feats
    return (
        layer_out,
        grad_tokens,
        grad_heads[:f].T,
        grad_heads[f : 2 * f].T,
        grad_heads[2 * f : 3 * f].T,
        grad_heads[3 * f : 4 * f].T,
        grad_owt,
        grad_min,
        grad_mout.T,
        grad_gu[:, :ff],
        grad_gu[:, ff:],
        grad_down.T,
        taps[:KC],
        taps[KC : 2 * KC],
        taps[2 * KC : 3 * KC],
        taps[3 * KC : 3 * KC + NP],
        taps[3 * KC + NP :],
        rate_rows[0],
        rate_rows[1],
        rate_rows[2],
        gains[0],
        gains[1],
    )


def solution(mesh):
    rows = P(("dp", "tensor"), None)
    cols_w, rows_w = P("dp", "tensor"), P("tensor", "dp")
    feats, rate = P(None, "tensor"), P("tensor")
    weights = (cols_w,) * 4 + (rows_w, cols_w, rows_w, cols_w, cols_w, rows_w)
    smalls = (feats,) * 5 + (rate,) * 3
    return jax.shard_map(
        functools.partial(per_device, mesh.shape["dp"], mesh.shape["tensor"]),
        mesh=mesh,
        in_specs=(rows,) + weights + smalls + (P(), P(), P("dp", None), P("dp", None), rows),
        out_specs=(rows, rows) + weights + smalls + (P(), P()),
        check_vma=False,
    )
```

```python
import functools

import jax
import jax.numpy as jnp
from jax import lax
from jax.experimental import pallas as pl
from jax.experimental.layout import Layout, with_layout_constraint
from jax.experimental.pallas import tpu as pltpu
from jax.sharding import PartitionSpec as P

DH = 96
HP = 128
NP = 64
CH = 512
KC = 4
SLOT = 1536
SHORT = 768
LIVE = SLOT + SHORT
BLK = 128
SUB = 256
NSUB = LIVE // SUB
LONG_SUBS = SLOT // SUB
SLOT_BLKS = SLOT // BLK
SHORT_BLKS = SHORT // BLK
PAD_ROWS = LIVE + 24
EPS = 1e-06
KAPPA = DH ** (-0.5)
VMEM = 56 * 1024 * 1024

F32 = jnp.float32
BF16 = jnp.bfloat16


def dot_nn(a, b):
    return lax.dot_general(a, b, (((1,), (0,)), ((), ())), preferred_element_type=F32)


def dot_nt(a, b):
    return lax.dot_general(a, b, (((1,), (1,)), ((), ())), preferred_element_type=F32)


def dot_tn(a, b):
    return lax.dot_general(a, b, (((0,), (0,)), ((), ())), preferred_element_type=F32)


STEP = 3


def gather_kernel(sources, rows, own_steps, normed, idx_ref, *refs):
    ins, refs = refs[:sources], refs[sources:]
    if normed:
        gain_ref, refs = refs[0], refs[1:]
    out_ref, buf, sem = refs[0], refs[-2], refs[-1]
    step, steps = pl.program_id(0), pl.num_programs(0)
    per_source = ins[0].shape[0] // rows

    def copy(source, first, slot, j):
        return pltpu.make_async_copy(
            source.at[pl.ds(first, rows)], buf.at[slot, pl.ds(j * rows, rows)], sem.at[slot, j]
        )

    def fetch(at, slot):
        for j in range(STEP):
            block = idx_ref[at * STEP + j]
            first = pl.multiple_of((block % per_source) * rows, rows)
            for i in range(sources):

                @pl.when(block // per_source == i)
                def _(i=i, first=first, j=j):
                    copy(ins[i], first, slot, j).start()

    slot = step % 2

    @pl.when(step == 0)
    def _():
        fetch(0, 0)

    @pl.when(step + 1 < steps)
    def _():
        fetch(step + 1, 1 - slot)

    for j in range(STEP):
        copy(ins[0], 0, slot, j).wait()
    block = buf[slot]
    if own_steps:

        @pl.when(step < own_steps)
        def _():
            refs[1][...] = block

    if normed:
        wide = block.astype(F32)
        inv = lax.rsqrt(jnp.mean(wide * wide, axis=-1, keepdims=True) + EPS)
        block = (wide * inv * gain_ref[...]).astype(BF16)
    out_ref[...] = block


def gather_rows(sources, index, rows, gain=None, own_steps=0):
    width, dtype = sources[0].shape[1], sources[0].dtype
    in_specs = [pl.BlockSpec(memory_space=pl.ANY)] * len(sources)
    args = list(sources)
    size = STEP * rows
    if gain is not None:
        in_specs.append(pl.BlockSpec((1, width), lambda i, idx: (0, 0)))
        args.append(gain[None, :])
    out_specs = [pl.BlockSpec((size, width), lambda i, idx: (i, 0))]
    out_shape = [jax.ShapeDtypeStruct((index.shape[0] * rows, width), dtype)]
    if own_steps:
        out_specs.append(
            pl.BlockSpec((size, width), lambda i, idx: (jnp.minimum(i, own_steps - 1), 0))
        )
        out_shape.append(jax.ShapeDtypeStruct((own_steps * size, width), dtype))
    out = pl.pallas_call(
        functools.partial(gather_kernel, len(sources), rows, own_steps, gain is not None),
        grid_spec=pltpu.PrefetchScalarGridSpec(
            num_scalar_prefetch=1,
            grid=(index.shape[0] // STEP,),
            in_specs=in_specs,
            out_specs=out_specs,
            scratch_shapes=[
                pltpu.VMEM((2, size, width), dtype),
                pltpu.SemaphoreType.DMA((2, STEP)),
            ],
        ),
        out_shape=out_shape,
        compiler_params=pltpu.CompilerParams(vmem_limit_bytes=VMEM),
        name="gather_rows",
    )(index, *args)
    return out if own_steps else out[0]


def cut_kernel(groups, in_ref, out_ref):
    width = out_ref.shape[2]
    for g in range(groups):
        out_ref[g, :, :] = in_ref[:DH, g * width : (g + 1) * width]


def cut_columns(values, groups):
    rows, width = values.shape
    return pl.pallas_call(
        functools.partial(cut_kernel, groups),
        grid=(rows // HP,),
        in_specs=[pl.BlockSpec((HP, width), lambda i: (i, 0))],
        out_specs=pl.BlockSpec((groups, DH, width // groups), lambda i: (0, i, 0)),
        out_shape=jax.ShapeDtypeStruct((groups, rows // HP * DH, width // groups), values.dtype),
        compiler_params=pltpu.CompilerParams(vmem_limit_bytes=VMEM),
        name="cut_columns",
    )(values).reshape(-1, width // groups)


def pad_base(step):
    return pl.multiple_of(8 + SUB * step + jnp.where(step >= LONG_SUBS, 8, 0), 8)


def load_padded(offs, chunk, src_ref, pad_ref):
    zero = jnp.zeros((8, HP), F32)
    pad_ref[0:8, :] = zero
    pad_ref[8 + SLOT : 16 + SLOT, :] = zero
    pad_ref[16 + LIVE : 24 + LIVE, :] = zero
    piece = 32
    for q in range(LIVE // chunk):
        start = q * chunk
        for first in range(0, chunk, piece):
            row = start + first
            pad_ref[pl.ds(8 + row + (8 if row >= SLOT else 0), piece), :] = src_ref[
                pl.ds(pl.multiple_of(offs[q] + first, piece), piece), :
            ].astype(F32)


def load_natural(offs, chunk, src_ref, dst_ref):
    for q in range(LIVE // chunk):
        dst_ref[pl.ds(q * chunk, chunk), :] = src_ref[
            pl.ds(pl.multiple_of(offs[q], 32), chunk), :
        ].astype(dst_ref.dtype)


def store_rel(offs, chunk, src_ref, dst_ref):
    for q in range(LIVE // chunk):
        dst_ref[pl.ds(pl.multiple_of(offs[q], 32), chunk), :] = src_ref[
            pl.ds(q * chunk, chunk), :
        ].astype(dst_ref.dtype)


def conv_rows(pad_ref, taps, base):
    window = pad_ref[pl.ds(pl.multiple_of(base - 8, 8), SUB + 8), :]
    total = taps[0:1, :] * window[8:, :]
    for j in range(1, KC):
        total = total + taps[j : j + 1, :] * window[8 - j : 8 - j + SUB, :]
    return total


def inv_head(values):
    return lax.rsqrt(jnp.sum(values * values, axis=-1, keepdims=True) * (1.0 / DH) + EPS)


def lane_sums(values):
    ones = jnp.ones((HP, HP), BF16)
    return dot_nn(values.astype(BF16), ones)


def inv_lanes(values):
    return lax.rsqrt(lane_sums(values * values) * (1.0 / DH) + EPS)


def head_back(normed, inv, grad):
    return inv * (grad - normed * (lane_sums(grad * normed) * (1.0 / DH)))


def with_ones(values):
    lane = lax.broadcasted_iota(jnp.int32, values.shape, 1)
    return jnp.where(lane == DH, 1.0, values.astype(F32)).astype(BF16)


def causal(shape):
    return lax.broadcasted_iota(jnp.int32, shape, 1) <= lax.broadcasted_iota(jnp.int32, shape, 0)


def split2(values):
    high = values.astype(BF16)
    return high, (values - high.astype(F32)).astype(BF16)


def forward_kernel(
    chunk,
    offs,
    mom_ref,
    step_ref,
    decay_ref,
    qp_ref,
    kp_ref,
    vp_ref,
    gp_ref,
    cq_ref,
    ck_ref,
    cv_ref,
    pk_ref,
    pv_ref,
    o_ref,
    a_ref,
    state_ref,
    q_s,
    k_s,
    v_s,
    qpad,
    kpad,
    vpad,
    iq_s,
    ik_s,
    r_s,
    g_s,
):
    head = pl.program_id(0)
    load_padded(offs, chunk, qp_ref, qpad)
    load_padded(offs, chunk, kp_ref, kpad)
    load_padded(offs, chunk, vp_ref, vpad)
    load_natural(offs, chunk, gp_ref, g_s)
    taps_q, taps_k, taps_v = cq_ref[...], ck_ref[...], cv_ref[...]

    def prepare(step, carry):
        base = pad_base(step)
        rows = pl.ds(pl.multiple_of(step * SUB, SUB), SUB)
        qc = conv_rows(qpad, taps_q, base)
        inv = inv_lanes(qc)
        q_s[rows, :] = (qc * inv).astype(BF16)
        iq_s[rows, :] = inv
        kc = conv_rows(kpad, taps_k, base)
        inv = inv_lanes(kc)
        k_s[rows, :] = (kc * inv).astype(BF16)
        ik_s[rows, :] = inv
        v_s[rows, :] = conv_rows(vpad, taps_v, base).astype(BF16)
        return carry

    lax.fori_loop(0, NSUB, prepare, 0)
    pkv = pk_ref[...]
    pk = (pkv * inv_head(pkv)).astype(BF16)
    pv1 = with_ones(pv_ref[...])

    mom, eta, decay = mom_ref[head], step_ref[head], decay_ref[head]

    def span(first, size=CH):
        return slice(first, first + size)

    def read(memory, rows):
        high, low = split2(memory * KAPPA)
        return dot_nt(q_s[rows, :], high) + dot_nt(q_s[rows, :], low)

    long0, long1, long2 = span(0), span(CH), span(2 * CH)
    short0, short1 = span(SLOT), span(SLOT + CH, SHORT - CH)
    update0 = dot_tn(v_s[long0, :], k_s[long0, :]) * (-KAPPA)
    mem1 = update0 * (-eta)
    high, low = split2(mem1 * KAPPA)
    err1 = dot_nt(k_s[long1, :], high) + dot_nt(k_s[long1, :], low) - v_s[long1, :].astype(F32)
    err_high, err_low = split2(err1)
    update1 = (dot_tn(err_high, k_s[long1, :]) + dot_tn(err_low, k_s[long1, :])) * KAPPA
    sur2 = mom * mem1 - eta * update1
    mem2 = (1.0 - decay) * mem1 + sur2
    update_s = dot_tn(v_s[short0, :], k_s[short0, :]) * (-KAPPA)
    mem_s = update_s * (-eta)
    state_ref[0, 0] = mem1
    state_ref[0, 1] = mem2
    state_ref[0, 2] = mem_s
    state_ref[0, 3] = update0
    state_ref[0, 4] = update1
    state_ref[0, 5] = update_s
    r_s[long0, :] = jnp.zeros((CH, HP), F32)
    r_s[long1, :] = read(mem1, long1)
    r_s[long2, :] = read(mem2, long2)
    r_s[short0, :] = jnp.zeros((CH, HP), F32)
    r_s[short1, :] = read(mem_s, short1)

    lane = lax.broadcasted_iota(jnp.int32, (SUB, HP), 1)

    def finish(rows, acc):
        inv = 1.0 / acc[:, DH : DH + 1]
        att = acc * inv
        kept = jnp.where(lane == DH + 1, iq_s[rows, :], ik_s[rows, :])
        a_ref[rows, :] = jnp.where(lane < DH, att, jnp.where(lane == DH, inv, kept))
        comb = jnp.where(lane >= DH, 0.0, att) + r_s[rows, :]
        g_s[rows, :] = comb * jax.nn.sigmoid(g_s[rows, :])

    def own_part(q, rows):
        e_d = jnp.where(causal((SUB, SUB)), jnp.exp(dot_nt(q, k_s[rows, :]) * KAPPA), 0.0)
        e_p = jnp.exp(dot_nt(q, pk) * KAPPA)
        return dot_nn(e_d.astype(BF16), with_ones(v_s[rows, :])) + dot_nn(e_p.astype(BF16), pv1)

    def pair(step, carry):
        rows0 = pl.ds(pl.multiple_of(step * CH, SUB), SUB)
        rows1 = pl.ds(pl.multiple_of(step * CH + SUB, SUB), SUB)
        finish(rows0, own_part(q_s[rows0, :], rows0))
        q = q_s[rows1, :]
        e_o = jnp.exp(dot_nt(q, k_s[rows0, :]) * KAPPA)
        finish(rows1, own_part(q, rows1) + dot_nn(e_o.astype(BF16), with_ones(v_s[rows0, :])))
        return carry

    lax.fori_loop(0, LIVE // CH, pair, 0)
    tail = pl.ds(LIVE - SUB, SUB)
    finish(tail, own_part(q_s[tail, :], tail))
    store_rel(offs, chunk, g_s, o_ref)


def head_col(part, heads, first=0):
    return pl.BlockSpec((LIVE, HP), lambda h, offs: (0, part * heads + first + h))


def attention_forward(offs, rates, wide, convs, persists, heads, chunk):
    smem = pl.BlockSpec(memory_space=pltpu.SMEM)
    col = lambda rows: pl.BlockSpec((rows, HP), lambda h, offs: (0, h))
    return pl.pallas_call(
        functools.partial(forward_kernel, chunk),
        grid_spec=pltpu.PrefetchScalarGridSpec(
            num_scalar_prefetch=1,
            grid=(heads,),
            in_specs=[smem] * 3
            + [head_col(i, heads) for i in range(4)]
            + [col(KC)] * 3
            + [col(NP)] * 2,
            out_specs=[
                col(LIVE),
                col(LIVE),
                pl.BlockSpec((1, 6, HP, HP), lambda h, offs: (h, 0, 0, 0)),
            ]
            + [col(LIVE)] * 3,
            scratch_shapes=[pltpu.VMEM((PAD_ROWS, HP), F32)] * 3
            + [pltpu.VMEM((LIVE, HP), F32)] * 4,
        ),
        out_shape=[
            jax.ShapeDtypeStruct((LIVE, heads * HP), BF16),
            jax.ShapeDtypeStruct((LIVE, heads * HP), F32),
            jax.ShapeDtypeStruct((heads, 6, HP, HP), F32),
        ]
        + [jax.ShapeDtypeStruct((LIVE, heads * HP), BF16)] * 3,
        compiler_params=pltpu.CompilerParams(vmem_limit_bytes=VMEM),
        name="attention_forward",
    )(offs, *rates, wide, wide, wide, wide, *convs, *persists)


def backward_kernel(
    chunk,
    first_head,
    heads,
    aliased,
    offs,
    mom_ref,
    step_ref,
    decay_ref,
    qp_ref,
    kp_ref,
    vp_ref,
    gp_ref,
    do_ref,
    a_ref,
    q_s,
    k_s,
    v_s,
    state_ref,
    cq_ref,
    ck_ref,
    cv_ref,
    pk_ref,
    pv_ref,
    *refs,
):
    (
        wide_ref,
        gcq_ref,
        gck_ref,
        gcv_ref,
        gpk_ref,
        gpv_ref,
        rate_ref,
        qpad,
        kpad,
        vpad,
        gq_s,
        gk_s,
        gv_s,
        da_s,
        dr_s,
        d_s,
        out_s,
        gpk_s,
        gpv_s,
        sem,
    ) = refs[1:] if aliased else refs

    head = pl.program_id(0) + first_head

    def copies(part):
        column = pl.multiple_of((part * heads + head) * HP, HP)
        return [
            pltpu.make_async_copy(
                out_s.at[part, pl.ds(q * chunk, chunk), :],
                wide_ref.at[pl.ds(pl.multiple_of(offs[q], 32), chunk), pl.ds(column, HP)],
                sem.at[part, q],
            )
            for q in range(LIVE // chunk)
        ]

    def send(part):
        for copy in copies(part):
            copy.start()

    load_padded(offs, chunk, qp_ref, qpad)
    load_padded(offs, chunk, kp_ref, kpad)
    load_padded(offs, chunk, vp_ref, vpad)
    load_natural(offs, chunk, do_ref, dr_s)
    load_natural(offs, chunk, gp_ref, d_s)
    taps_q, taps_k, taps_v = cq_ref[...], ck_ref[...], cv_ref[...]
    zero8 = jnp.zeros((8, HP), F32)
    for pad in (gq_s, gk_s, gv_s):
        pad[0:8, :] = zero8
        pad[8 + SLOT : 16 + SLOT, :] = zero8
        pad[16 + LIVE : 24 + LIVE, :] = zero8
    lane = lax.broadcasted_iota(jnp.int32, (SUB, HP), 1)

    pkv = pk_ref[...]
    pk_inv = inv_head(pkv)
    pk = (pkv * pk_inv).astype(BF16)
    pv = pv_ref[...].astype(BF16)
    mom, eta, decay = mom_ref[head], step_ref[head], decay_ref[head]
    mem1, mem2, mem_s = state_ref[0, 0], state_ref[0, 1], state_ref[0, 2]
    update0, update1, update_s = state_ref[0, 3], state_ref[0, 4], state_ref[0, 5]

    def scaled(memory):
        return (memory * KAPPA).astype(BF16)

    two_nt, two_nn = dot_nt, dot_nn

    km1, km2, kms = scaled(mem1), scaled(mem2), scaled(mem_s)

    def gates(first, size, memory):
        for start in range(first, first + size, SUB):
            rows = slice(start, start + SUB)
            grad = dr_s[rows, :]
            sig = jax.nn.sigmoid(d_s[rows, :])
            att = a_ref[rows, :]
            comb = jnp.where(lane >= DH, 0.0, att)
            if memory is not None:
                comb = comb + two_nt(q_s[rows, :], memory)
            through = grad * sig
            out_s[3, rows, :] = (through * comb * (1.0 - sig)).astype(BF16)
            dr_s[rows, :] = through
            low = through.astype(BF16)
            da_s[rows, :] = low
            row_dot = lane_sums(low.astype(F32) * att)
            d_s[rows, :] = jnp.where(lane == 0, att[:, DH : DH + 1], row_dot)

    gates(0, CH, None)
    gates(CH, CH, km1)
    gates(2 * CH, CH, km2)
    gates(SLOT, CH, None)
    gates(SLOT + CH, SHORT - CH, kms)
    send(3)

    def span(first, size=CH):
        return slice(first, first + size)

    long0, long1, long2 = span(0), span(CH), span(2 * CH)
    short0, short1 = span(SLOT), span(SLOT + CH, SHORT - CH)

    def padded(rows):
        shift = 16 if rows.start >= SLOT else 8
        return slice(rows.start + shift, rows.stop + shift)

    def outer(left, right):
        high, low = split2(left)
        return dot_tn(high, right) + dot_tn(low, right)

    zero_span = jnp.zeros((CH, HP), F32)

    def reads_back(rows, pieces):
        gq_s[padded(rows), :] = two_nn(dr_s[rows, :].astype(BF16), pieces)

    def zero_out(pad, rows):
        pad[padded(rows), :] = jnp.zeros((rows.stop - rows.start, HP), F32)

    def row_sum(values):
        return jnp.sum(values, axis=0, keepdims=True)

    grad_mem2 = outer(dr_s[long2, :], q_s[long2, :]) * KAPPA
    reads_back(long2, km2)
    zero_out(gk_s, long2)
    zero_out(gv_s, long2)
    total2 = grad_mem2
    rate_decay = -row_sum(grad_mem2 * mem1)
    rate_mom = row_sum(total2 * mem1)
    rate_step = -row_sum(total2 * update1)
    grad_up = total2 * (-eta)
    k1 = k_s[long1, :]
    de1 = two_nt(k1, scaled(grad_up))
    err1 = two_nt(k1, km1) - v_s[long1, :].astype(F32)
    gk_s[padded(long1), :] = two_nn(err1.astype(BF16), scaled(grad_up)) + two_nn(
        de1.astype(BF16), km1
    )
    gv_s[padded(long1), :] = -de1
    grad_mem1 = (
        outer(dr_s[long1, :], q_s[long1, :]) * KAPPA
        + (1.0 - decay) * grad_mem2
        + outer(de1, k1) * KAPPA
    )
    reads_back(long1, km1)
    total1 = grad_mem1 + mom * total2
    rate_step = rate_step - row_sum(total1 * update0)

    def first_span(rows, total):
        pieces = scaled(total * (-eta))
        gv_s[padded(rows), :] = -two_nt(k_s[rows, :], pieces)
        gk_s[padded(rows), :] = -two_nn(v_s[rows, :], pieces)
        gq_s[padded(rows), :] = zero_span

    first_span(long0, total1)
    grad_mem_s = outer(dr_s[short1, :], q_s[short1, :]) * KAPPA
    reads_back(short1, kms)
    zero_out(gk_s, short1)
    zero_out(gv_s, short1)
    rate_step = rate_step - row_sum(grad_mem_s * update_s)
    first_span(short0, grad_mem_s)
    rate_ref[...] = jnp.concatenate(
        [rate_mom, rate_step, rate_decay, jnp.zeros((5, HP), F32)], axis=0
    )

    gpk_s[...] = jnp.zeros((NP, HP), F32)
    gpv_s[...] = jnp.zeros((NP, HP), F32)

    def block(q, da, inv, row_dot, keys, vals, masked):
        prob = jnp.exp(dot_nt(q, keys) * KAPPA) * inv
        if masked:
            prob = jnp.where(causal(prob.shape), prob, 0.0)
        grad = dot_nt(da, vals)
        ds = (prob * (grad - row_dot) * KAPPA).astype(BF16)
        return dot_nn(ds, keys), dot_tn(ds, q), dot_tn(prob.astype(BF16), da)

    def one(rows, base, before=None, base_before=None):
        q, da = q_s[rows, :], da_s[rows, :]
        inv, row_dot = d_s[rows, 0:1], d_s[rows, 1:2]
        here = pl.ds(base, SUB)
        gq, gk, gv = block(q, da, inv, row_dot, k_s[rows, :], v_s[rows, :], True)
        gk_s[here, :] += gk
        gv_s[here, :] += gv
        pq, gpk, gpv = block(q, da, inv, row_dot, pk, pv, False)
        gpk_s[...] += gpk
        gpv_s[...] += gpv
        gq = gq + pq
        if before is not None:
            oq, ok, ov = block(q, da, inv, row_dot, k_s[before, :], v_s[before, :], False)
            there = pl.ds(base_before, SUB)
            gk_s[there, :] += ok
            gv_s[there, :] += ov
            gq = gq + oq
        gq_s[here, :] += gq

    def pair(step, carry):
        rows0 = pl.ds(pl.multiple_of(step * CH, SUB), SUB)
        rows1 = pl.ds(pl.multiple_of(step * CH + SUB, SUB), SUB)
        base0, base1 = pad_base(2 * step), pad_base(2 * step + 1)
        one(rows0, base0)
        one(rows1, base1, rows0, base0)
        return carry

    lax.fori_loop(0, LIVE // CH, pair, 0)
    one(pl.ds(LIVE - SUB, SUB), 16 + LIVE - SUB)
    gpv_ref[...] = gpv_s[...]
    gpk_ref[...] = head_back(pkv * pk_inv, pk_inv, gpk_s[...])

    def norms(step, carry):
        here = pl.ds(pad_base(step), SUB)
        rows = pl.ds(pl.multiple_of(step * SUB, SUB), SUB)
        inv_q, inv_k = a_ref[rows, DH + 1 : DH + 2], a_ref[rows, DH + 2 : DH + 3]
        gq_s[here, :] = head_back(q_s[rows, :].astype(F32), inv_q, gq_s[here, :])
        gk_s[here, :] = head_back(k_s[rows, :].astype(F32), inv_k, gk_s[here, :])
        return carry

    lax.fori_loop(0, NSUB, norms, 0)

    def conv_back(pre_ref, grad_ref, taps, part, taps_ref):
        def body(step, carry):
            base = pad_base(step)
            rows = pl.ds(pl.multiple_of(step * SUB, SUB), SUB)
            after = grad_ref[pl.ds(base, SUB + 8), :]
            before = pre_ref[pl.ds(pl.multiple_of(base - 8, 8), SUB + 8), :]
            grad = after[:SUB, :]
            total = taps[0:1, :] * grad
            sums = [row_sum(grad * before[8:, :])]
            for j in range(1, KC):
                total = total + taps[j : j + 1, :] * after[j : j + SUB, :]
                sums.append(row_sum(grad * before[8 - j : 8 - j + SUB, :]))
            out_s[part, rows, :] = total.astype(BF16)
            return tuple(c + s for c, s in zip(carry, sums))

        sums = lax.fori_loop(0, NSUB, body, (jnp.zeros((1, HP), F32),) * KC)
        taps_ref[...] = jnp.concatenate(sums, axis=0)
        send(part)

    conv_back(qpad, gq_s, taps_q, 0, gcq_ref)
    conv_back(kpad, gk_s, taps_k, 1, gck_ref)
    conv_back(vpad, gv_s, taps_v, 2, gcv_ref)
    for part in range(4):
        for copy in copies(part):
            copy.wait()


def attention_backward(
    offs, rates, wide, grad_out, kept, states, convs, persists, heads, chunk, first, some, into=None
):
    smem = pl.BlockSpec(memory_space=pltpu.SMEM)
    anywhere = pl.BlockSpec(memory_space=pl.ANY)
    args = [*rates, wide, wide, wide, wide, grad_out, *kept, states, *convs, *persists]
    args += [] if into is None else [into]
    col = lambda rows: pl.BlockSpec((rows, HP), lambda h, offs: (0, h + first))
    out = lambda rows: pl.BlockSpec((rows, HP), lambda h, offs: (0, h))
    shape = lambda rows, dtype: jax.ShapeDtypeStruct((rows, some * HP), dtype)
    return pl.pallas_call(
        functools.partial(backward_kernel, chunk, first, heads, into is not None),
        grid_spec=pltpu.PrefetchScalarGridSpec(
            num_scalar_prefetch=1,
            grid=(some,),
            in_specs=[smem] * 3
            + [head_col(i, heads, first) for i in range(4)]
            + [col(LIVE)] * 5
            + [pl.BlockSpec((1, 6, HP, HP), lambda h, offs: (h + first, 0, 0, 0))]
            + [col(KC)] * 3
            + [col(NP)] * 2
            + ([] if into is None else [anywhere]),
            out_specs=[anywhere] + [out(KC)] * 3 + [out(NP)] * 2 + [out(8)],
            scratch_shapes=[pltpu.VMEM((PAD_ROWS, HP), F32)] * 6
            + [pltpu.VMEM((LIVE, HP), BF16)]
            + [pltpu.VMEM((LIVE, HP), F32)] * 2
            + [pltpu.VMEM((4, LIVE, HP), BF16)]
            + [pltpu.VMEM((NP, HP), F32)] * 2
            + [pltpu.SemaphoreType.DMA((4, LIVE // chunk))],
        ),
        out_shape=[jax.ShapeDtypeStruct((LIVE, 4 * heads * HP), BF16)]
        + [shape(KC, F32)] * 3
        + [shape(NP, F32)] * 2
        + [shape(8, F32)],
        compiler_params=pltpu.CompilerParams(vmem_limit_bytes=VMEM),
        input_output_aliases={} if into is None else {len(args): 0},
        name="attention_backward",
    )(offs, *args)


def silu_grad(values):
    sigmoid_v = jax.nn.sigmoid(values)
    return sigmoid_v * (1.0 + values * (1.0 - sigmoid_v))


def rms_backward(values, inv_rms, gain, grad_out):
    scaled = grad_out * gain
    grad_in = inv_rms * (
        scaled - values * inv_rms * inv_rms * jnp.mean(scaled * values, axis=-1, keepdims=True)
    )
    return grad_in, jnp.sum(grad_out * values * inv_rms, axis=0)


def pad_heads(values):
    rows, cols = values.shape
    split = values.reshape(rows, cols // DH, DH)
    return jnp.pad(split, ((0, 0), (0, 0), (0, HP - DH))).reshape(rows, -1)


def cut_heads(values):
    rows, cols = values.shape
    return values.reshape(rows, cols // HP, HP)[:, :, :DH].reshape(rows, -1)


def after(value, token):
    return lax.optimization_barrier((value, token))[0]


def plain(values):
    return with_layout_constraint(values, Layout(tuple(range(values.ndim))))


def tie(*values):
    return lax.optimization_barrier(values)


def interleave(first, second):
    return [v for pair in zip(first, second) for v in pair]


class Team:
    def __init__(self, n_dp, n_tensor):
        self.n_dp, self.n_tensor = n_dp, n_tensor
        self.half = half = n_tensor // 2
        p, t = lax.axis_index("dp"), lax.axis_index("tensor")
        self.t = t
        self.core = p % 2
        self.side = t // half
        self.place = t % half
        self.same = self.core == self.side
        self.core_swap = [(i, i ^ 1) for i in range(n_dp)]
        self.flips = [(t, (t + half) % n_tensor) for t in range(n_tensor)]
        self.parity = [list(range(c, n_dp, 2)) for c in range(2)]
        self.chunk = LIVE // n_tensor

    def swap(self, values):
        return lax.ppermute(values, "dp", self.core_swap)

    def flip(self, values):
        return lax.ppermute(values, "tensor", self.flips)

    def rotate(self, values, by):
        half = self.half
        return lax.ppermute(
            values,
            "tensor",
            [(t, (t // half) * half + (t + by) % half) for t in range(self.n_tensor)],
        )

    def sum_bits(self, values, axis, size, first=1):
        step = first
        while step < size:
            pairs = [(i, i ^ step) for i in range(size)]
            values = values + lax.ppermute(values, axis, pairs)
            step *= 2
        return values

    def by_core(self, mine, other):
        return jnp.concatenate(
            [jnp.where(self.core == 0, mine, other), jnp.where(self.core == 0, other, mine)], axis=0
        )

    def halves(self, values):
        size = values.shape[0] // 2
        low, high = values[:size], values[size:]
        return jnp.where(self.core == 0, low, high), jnp.where(self.core == 0, high, low)

    def share_out(self, rows):
        mine, give = self.halves(rows)
        got = self.swap(give)
        return jnp.where(self.same, mine, got), jnp.where(self.same, got, mine)

    def finish_home(self, own_side, back):
        mine = jnp.where(self.same, own_side, back)
        got = self.swap(jnp.where(self.same, back, own_side))
        return self.by_core(mine, got)

    def sort_blocks(self, block, flipped):
        return jnp.where(self.same, block, flipped), jnp.where(self.same, flipped, block)

    def gather_weights(self, mine, got):
        return lax.all_gather(
            self.by_core(mine, got), "dp", axis=0, tiled=True, axis_index_groups=self.parity
        )

    def scatter_weights(self, grad):
        return lax.psum_scatter(
            grad, "dp", scatter_dimension=0, tiled=True, axis_index_groups=self.parity
        )

    def scatter_first(self, partial):
        size = partial.shape[0] // (self.n_tensor - 2)
        out = []
        for s in range(1, self.half):
            keep = partial[(2 * s - 2) * size : (2 * s - 1) * size]
            send = partial[(2 * s - 1) * size : 2 * s * size]
            out.append((keep.astype(F32) + self.swap(send).astype(F32)).astype(BF16))
        return out

    def scatter_turn(self, sums):
        return [self.rotate(v, self.half - 1 - i) for i, v in enumerate(sums)]

    def scatter_last(self, partial, turned):
        size = partial.shape[0] // 2
        total = partial[:size].astype(F32) + self.swap(partial[size:]).astype(F32)
        for v in turned:
            total = total + v.astype(F32)
        return total

    def reduce_first(self, both, axis=0):
        low, high = jnp.split(both, 2, axis=axis)
        mine = jnp.where(self.core == 0, low, high)
        got = self.swap(jnp.where(self.core == 0, high, low))
        return jnp.where(self.same, mine, got), jnp.where(self.same, got, mine)


def per_device(
    n_dp,
    n_tensor,
    tokens,
    query_weight,
    key_weight,
    value_weight,
    gate_weight,
    output_weight,
    memory_in,
    memory_out,
    swiglu_gate,
    swiglu_up,
    swiglu_down,
    conv_query,
    conv_key,
    conv_value,
    persist_key,
    persist_value,
    momentum,
    step_size,
    decay_rate,
    norm_attn,
    norm_swiglu,
    seq_lengths,
    deal_order,
    cotangent,
):
    team = Team(n_dp, n_tensor)
    half, core, side, place, same, chunk = (
        team.half,
        team.core,
        team.side,
        team.place,
        team.same,
        team.chunk,
    )
    own_rows = tokens.shape[0]
    own_blks = own_rows // BLK
    half_rows = own_rows // 2
    head_feats = query_weight.shape[1]
    heads = head_feats // DH
    grain = next(g for g in (128, 64, 32) if chunk % g == 0)
    per_blk, per_chunk = BLK // grain, chunk // grain
    per_half = half_rows // grain

    tables = jnp.concatenate([deal_order[0], seq_lengths[0]])
    other_tables = team.swap(tables)
    group_tables = jnp.where(same, tables, other_tables)
    n_blks = deal_order.shape[1]
    deal = group_tables[:n_blks]
    long_slot = jnp.where(group_tables[n_blks] == SLOT, 0, 1)

    small = jnp.concatenate(
        [
            conv_query,
            conv_key,
            conv_value,
            persist_key,
            persist_value,
            jnp.pad(
                jnp.stack([momentum, step_size, decay_rate]), ((0, 0), (0, head_feats - heads))
            ),
        ],
        axis=0,
    )
    x_near, x_give = team.share_out(tokens)
    heads_block = jnp.concatenate(
        [query_weight, key_weight, value_weight, gate_weight, output_weight.T], axis=1
    )
    heads_sent = team.flip(heads_block)
    x_near, x_give, heads_sent, small = tie(x_near, x_give, heads_sent, small)
    taps_end, persist_end = 3 * KC, 3 * KC + 2 * NP
    def chunk_of(natural):
        return 2 * ((place - natural % half) % half) + (natural // half != core).astype(jnp.int32)

    def compact_of(rel):
        part, within = rel // per_chunk, rel % per_chunk
        natural = (place - part // 2) % half + ((core + part) % 2) * half
        return natural * per_chunk + within

    def dealt_of(rel):
        compact = compact_of(rel)
        blk, sub = compact // per_blk, compact % per_blk
        nat_blk = jnp.where(
            blk < SLOT_BLKS,
            long_slot * SLOT_BLKS + blk,
            (1 - long_slot) * SLOT_BLKS + blk - SLOT_BLKS,
        )
        match = (deal[None, :] == nat_blk[:, None]).astype(jnp.int32)
        dealt = jnp.sum(match * jnp.arange(n_blks, dtype=jnp.int32)[None, :], axis=1)
        shard, row = dealt // own_blks, (dealt % own_blks) * per_blk + sub
        which, within = row // per_half, row % per_half
        piece = (
            (shard // half != side).astype(jnp.int32) * 2 * half
            + 2 * ((place - shard % half) % half)
            + (which != core).astype(jnp.int32)
        )
        return (piece * per_half + within).astype(jnp.int32)

    def rel_of(shard, row):
        nat_blk = deal[shard * own_blks + row // per_blk]
        in_long = nat_blk // SLOT_BLKS == long_slot
        live_here = in_long | (nat_blk % SLOT_BLKS < SHORT_BLKS)
        blk = jnp.where(in_long, nat_blk % SLOT_BLKS, SLOT_BLKS + nat_blk % SLOT_BLKS)
        compact = jnp.minimum(blk, LIVE // BLK - 1) * per_blk + row % per_blk
        rel = chunk_of(compact // per_chunk) * per_chunk + compact % per_chunk
        return rel.astype(jnp.int32), live_here

    def half_index(side_of):
        steps = jnp.arange(n_tensor * per_half, dtype=jnp.int32)
        part, within = steps // per_half, steps % per_half
        shard = (place - part // 2) % half + side_of * half
        return rel_of(shard, ((core + part) % 2) * per_half + within)

    n_sub = LIVE // grain
    gather_index = dealt_of(jnp.arange(n_sub, dtype=jnp.int32))
    near_index, near_live = half_index(side)
    far_index, far_live = half_index(1 - side)
    offs = (chunk_of(jnp.arange(n_tensor, dtype=jnp.int32)) * chunk).astype(jnp.int32)

    def row_mask(live_sub):
        return jnp.broadcast_to(live_sub[:per_half, None], (per_half, grain)).reshape(half_rows, 1)

    near_mask, far_mask = row_mask(near_live), row_mask(far_live)

    near_rows = 2 * chunk
    turns = range(1, half)
    heads_mine, heads_give = team.sort_blocks(heads_block, heads_sent)
    heads_w = team.gather_weights(heads_mine, team.swap(heads_give))
    x_far = team.flip(x_give)
    near_turns = [team.rotate(x_near, s) for s in turns]
    x_near_other = team.swap(x_near)
    x_far, near_turns, x_near_other = tie(x_far, near_turns, x_near_other)

    far_turns = [team.rotate(x_far, s) for s in turns]
    x_far_other = team.swap(x_far)
    near_turns_other = [team.swap(v) for v in near_turns]
    min_sent = team.flip(after(memory_in, x_far))
    c_near, c_give = team.share_out(after(cotangent, x_far))
    small_other = team.flip(after(small, x_far))
    far_turns, x_far_other, near_turns_other, min_sent, c_near, c_give, small_other = tie(
        far_turns, x_far_other, near_turns_other, min_sent, c_near, c_give, small_other
    )

    far_turns_other = [team.swap(v) for v in far_turns]
    min_mine, min_give = team.sort_blocks(memory_in, min_sent)
    min_got = team.swap(min_give)
    min_w = team.gather_weights(min_mine, min_got)
    mout_block, gu_block, down_block = after(
        (
            memory_out.T,
            jnp.concatenate([swiglu_gate, swiglu_up], axis=1),
            swiglu_down.T,
        ),
        far_turns,
    )
    normed, x_own = gather_rows(
        interleave([x_near] + near_turns, [x_near_other] + near_turns_other)
        + interleave([x_far] + far_turns, [x_far_other] + far_turns_other),
        gather_index,
        grain,
        norm_attn,
        per_chunk // STEP,
    )
    mout_sent = team.flip(after(mout_block, normed))
    c_turns = [team.rotate(after(c_near, normed), s) for s in turns]
    heads_w = pad_heads(heads_w)
    wide_feats = 4 * heads * HP
    qkvg_w, out_w = heads_w[:, :wide_feats], heads_w[:, wide_feats:]
    wide = dot_nn(normed, qkvg_w).astype(BF16)
    wide, normed, x_own, mout_sent = tie(wide, normed, x_own, mout_sent)
    small = jnp.where(same, small, small_other)
    rates = [small[persist_end + i, :heads] for i in range(3)]
    small = pad_heads(small[:persist_end])
    convs = [small[KC * i : KC * (i + 1)] for i in range(3)]
    persists = [small[taps_end + NP * i : taps_end + NP * (i + 1)] for i in range(2)]

    mout_mine, mout_give = team.sort_blocks(mout_block, mout_sent)
    mout_got = team.swap(mout_give)
    mout_w = team.gather_weights(mout_mine, mout_got)
    gu_sent = team.flip(after(gu_block, wide))
    o_low, att, states, *heads_kept = attention_forward(
        offs, rates, wide, convs, persists, heads, chunk
    )
    o_low, gu_sent, c_turns = tie(o_low, gu_sent, c_turns)

    near, far = slice(0, near_rows), slice(near_rows, None)

    def memory_of(rows, token):
        pre = dot_nn(after(normed, token)[rows], min_w).astype(BF16)
        return pre, jax.nn.silu(pre.astype(F32)).astype(BF16)

    def branch_of(rows, mem):
        return (dot_nt(o_low[rows], out_w) + dot_nt(mem, mout_w)).astype(BF16)

    gu_mine, gu_give = team.sort_blocks(gu_block, gu_sent)
    gu_got = team.swap(gu_give)
    gu_w = team.gather_weights(gu_mine, gu_got)
    c_far = team.flip(after(c_give, o_low))
    mem_pre_far, mem_far = memory_of(far, o_low)
    branch_far = branch_of(far, mem_far)
    branch_far = team.scatter_first(branch_far)
    branch_far, mem_far, gu_got = tie(branch_far, mem_far, gu_got)

    branch_turned = team.scatter_turn(branch_far)
    mem_pre_near, mem_near = memory_of(near, branch_far)
    branch_near = branch_of(near, mem_near)
    branch_turned, branch_near, c_far = tie(branch_turned, branch_near, c_far)
    down_sent = team.flip(after(down_block, c_far))
    x_own = x_own.astype(F32)
    mid_own = x_own + team.scatter_last(branch_near, branch_turned)
    inv_second = lax.rsqrt(jnp.mean(mid_own * mid_own, axis=-1, keepdims=True) + EPS)
    sw_own = (mid_own * inv_second * norm_swiglu).astype(BF16)

    ff = swiglu_gate.shape[1]

    def gates_of(gate_up):
        return gate_up[:, :ff].astype(F32), gate_up[:, ff:].astype(F32)

    def hidden_of(gate_up):
        gate_pre, up_pre = gates_of(gate_up)
        return (jax.nn.silu(gate_pre) * up_pre).astype(BF16)

    def hidden_back(gate_up, grad_hidden):
        gate_pre, up_pre = gates_of(gate_up)
        return jnp.concatenate(
            [
                (grad_hidden * up_pre * silu_grad(gate_pre)).astype(BF16),
                (grad_hidden * jax.nn.silu(gate_pre)).astype(BF16),
            ],
            axis=1,
        )

    sw_turns = [team.rotate(sw_own, s) for s in turns]
    sw_near = jnp.concatenate([sw_own, team.swap(sw_own)], axis=0)
    pre_near = dot_nn(sw_near, gu_w).astype(BF16)
    hidden_near = hidden_of(pre_near)
    sw_turns, pre_near, hidden_near, mid_own, down_sent = tie(
        sw_turns, pre_near, hidden_near, mid_own, down_sent
    )

    down_mine, down_give = team.sort_blocks(down_block, down_sent)
    down_w = team.gather_weights(down_mine, team.swap(down_give))
    c_far_turns = [team.rotate(after(c_far, sw_own), s) for s in turns]
    c_others = [team.swap(after(v, sw_own)) for v in [c_near] + c_turns + [c_far]]
    sw_far = jnp.concatenate(interleave(sw_turns, [team.swap(v) for v in sw_turns]), axis=0)
    pre_far = dot_nn(sw_far, gu_w).astype(BF16)
    hidden_far = hidden_of(pre_far)
    sw_far, pre_far, hidden_far, c_far_turns, c_others = tie(
        sw_far, pre_far, hidden_far, c_far_turns, c_others
    )

    c_others += [team.swap(v) for v in c_far_turns]
    cot_low = gather_rows(
        interleave([c_near] + c_turns + [c_far] + c_far_turns, c_others), gather_index, grain
    )
    cot_parts = [cot_low[:near_rows], cot_low[near_rows:]]
    gu_far = hidden_back(pre_far, dot_nn(cot_parts[1], down_w))
    rows_far = dot_nt(gu_far, gu_w).astype(BF16)
    rows_far, gu_far, hidden_far, sw_far, cot_parts = tie(
        rows_far, gu_far, hidden_far, sw_far, cot_parts
    )

    gu_near = hidden_back(pre_near, dot_nn(cot_parts[0], down_w))
    rows_far = team.scatter_first(rows_far)
    rows_far, gu_near = tie(rows_far, gu_near)
    rows_turned = team.scatter_turn(rows_far)
    rows_near = dot_nt(gu_near, gu_w).astype(BF16)
    grad_gu = (dot_tn(sw_near, gu_near) + dot_tn(sw_far, gu_far)).astype(BF16)
    rows_turned, rows_near, grad_gu, cot_parts, hidden_near, hidden_far = tie(
        rows_turned, rows_near, grad_gu, cot_parts, hidden_near, hidden_far
    )

    grad_gu = team.scatter_weights(grad_gu)
    grad_mid_norm = team.scatter_last(rows_near, rows_turned)
    grad_second, gain_second = rms_backward(mid_own, inv_second, norm_swiglu, grad_mid_norm)
    dz_own = (cot_low[:chunk].astype(F32) + grad_second).astype(BF16)

    def mem_back(cot, pre):
        return (dot_nn(cot, mout_w) * silu_grad(pre.astype(F32))).astype(BF16)

    dz_turns = [team.rotate(dz_own, s) for s in turns]
    dz_near = jnp.concatenate([dz_own, team.swap(dz_own)], axis=0)
    back_near = mem_back(dz_near, mem_pre_near)
    out_near = dot_nn(dz_near, out_w).astype(BF16)
    feed_far = dot_nt(after(hidden_far, dz_own), down_w).astype(BF16)
    feed_near = dot_nt(after(hidden_near, dz_own), down_w).astype(BF16)
    grad_down = (
        dot_tn(cot_parts[0], after(hidden_near, dz_own)) + dot_tn(cot_parts[1], hidden_far)
    ).astype(BF16)
    dz_turns, back_near, out_near, feed_far, feed_near, grad_down, dz_near = tie(
        dz_turns, back_near, out_near, feed_far, feed_near, grad_down, dz_near
    )

    dz_far = jnp.concatenate(interleave(dz_turns, [team.swap(v) for v in dz_turns]), axis=0)
    feed_far = team.scatter_first(feed_far)
    dz_far, feed_far = tie(dz_far, feed_far)

    feed_turned = team.scatter_turn(feed_far)
    grad_down = team.scatter_weights(grad_down)
    dz_all = jnp.concatenate([dz_near, dz_far], axis=0)
    grad_out = jnp.concatenate([out_near, dot_nn(dz_far, out_w).astype(BF16)], axis=0)
    grad_mem = jnp.concatenate([back_near, mem_back(dz_far, mem_pre_far)], axis=0)
    grad_mout = (dot_tn(dz_near, mem_near) + dot_tn(dz_far, mem_far)).astype(BF16)
    grad_min = dot_tn(normed, grad_mem).astype(BF16)
    grad_owt = cut_columns(dot_tn(o_low, dz_all).astype(BF16), n_dp // 2)
    feed_turned, dz_all, grad_out, grad_mem, grad_mout, grad_min, grad_owt, grad_gu = tie(
        feed_turned, dz_all, grad_out, grad_mem, grad_mout, grad_min, grad_owt, grad_gu
    )

    half_heads = heads // 2

    def heads_back(first, token, into=None):
        return attention_backward(
            after(offs, token),
            rates,
            wide,
            grad_out,
            [att] + heads_kept,
            states,
            convs,
            persists,
            heads,
            chunk,
            first,
            half_heads,
            into,
        )

    gu_keep, gu_back = team.reduce_first(grad_gu)
    gu_back = team.flip(gu_back)
    grad_mout = team.scatter_weights(grad_mout)
    grad_min = team.scatter_weights(grad_min)
    y_own = (mid_own + team.scatter_last(feed_near, feed_turned)).astype(BF16)
    y_turns = [team.rotate(y_own, s) for s in turns]
    y_other = team.swap(y_own)
    back_low = heads_back(0, y_own)
    back_low, y_turns, y_other, gu_back, grad_down = tie(
        back_low, y_turns, y_other, gu_back, grad_down
    )

    down_keep, down_back = team.reduce_first(grad_down)
    down_back = team.flip(down_back)
    y_pieces = [y_own, y_other] + interleave(y_turns, [team.swap(v) for v in y_turns])
    y_near = gather_rows(y_pieces, near_index[:per_half], grain)
    y_far = gather_rows(y_pieces, far_index[:per_half], grain)
    y_back = team.flip(y_far)
    back_high = heads_back(half_heads, y_far, back_low[0])
    back_high, down_back, grad_mout = tie(back_high, down_back, grad_mout)

    grad_owt = team.scatter_weights(after(grad_owt, down_back))
    mout_keep, mout_back = team.reduce_first(grad_mout)
    mout_back = team.flip(mout_back)
    small_back = jnp.concatenate(
        [jnp.concatenate(pair, axis=1) for pair in zip(back_low[1:], back_high[1:])], axis=0
    )
    small_x = team.sum_bits(small_back, "dp", n_dp, 2)
    grad_wide = back_high[0]
    grad_normed = (dot_nt(grad_wide, qkvg_w) + dot_nt(grad_mem, min_w)).astype(BF16)
    far_part = gather_rows([grad_normed], far_index, grain)
    far_part, grad_normed, grad_wide, small_x, y_back, grad_min = tie(
        far_part, grad_normed, grad_wide, small_x, y_back, grad_min
    )

    def rows_grad(index, mask, x_half, summed):
        x_rows = x_half.astype(F32)
        inv_first = lax.rsqrt(jnp.mean(x_rows * x_rows, axis=-1, keepdims=True) + EPS)
        grad_first, gain_first = rms_backward(
            x_rows, inv_first, norm_attn, jnp.where(mask, summed, 0.0)
        )
        mid = gather_rows([dz_all], index[:per_half], grain).astype(F32)
        return (mid + grad_first).astype(BF16), gain_first

    split = 2 * half_rows
    far_sums = team.scatter_first(far_part[split:])
    min_keep, min_back = team.reduce_first(grad_min)
    near_part = gather_rows([grad_normed], near_index, grain)
    near_sums = team.scatter_first(near_part[split:])
    far_sums, near_sums, min_keep, min_back, near_part = tie(
        far_sums, near_sums, min_keep, min_back, near_part
    )

    far_turned = team.scatter_turn(far_sums)
    min_back = team.flip(min_back)
    small_flipped = team.flip(small_x)
    grad_heads = dot_tn(after(grad_wide, far_sums), normed).astype(BF16)
    grad_heads = cut_columns(grad_heads, n_dp // 2)
    y_rows = team.finish_home(y_near, y_back)
    far_turned, grad_heads, small_flipped, y_rows, mout_back, min_back = tie(
        far_turned, grad_heads, small_flipped, y_rows, mout_back, min_back
    )

    grad_heads = plain(team.scatter_weights(plain(grad_heads)))
    near_turned = team.scatter_turn(after(near_sums, far_turned))
    grad_far, gain_far = rows_grad(
        far_index, far_mask, x_far, team.scatter_last(far_part[:split], far_turned)
    )
    far_back = team.flip(grad_far)
    near_part = after(near_part, grad_far)
    grad_near, gain_near = rows_grad(
        near_index, near_mask, x_near, team.scatter_last(near_part[:split], near_turned)
    )
    owt_keep, owt_back = team.reduce_first(after(grad_owt, grad_near), -1)
    gains = team.sum_bits(jnp.stack([gain_far + gain_near, gain_second]), "dp", n_dp)
    summed = small_x + small_flipped
    summed = jnp.where(same, summed, team.swap(after(summed, grad_far)))
    total = lambda keep, back: keep.astype(F32) + back.astype(F32)
    grad_gu = total(gu_keep, gu_back)
    grad_down = total(down_keep, down_back)
    grad_mout = total(mout_keep, mout_back)
    grad_min = total(min_keep, min_back)
    grad_heads, grad_near, gains, summed, grad_gu, grad_down, grad_mout, grad_min = tie(
        grad_heads, grad_near, gains, summed, grad_gu, grad_down, grad_mout, grad_min
    )
    heads_keep, heads_other = team.reduce_first(grad_heads, -1)
    heads_other = team.flip(plain(heads_other))
    gains = team.sum_bits(gains, "tensor", n_tensor)
    owt_back = team.flip(owt_back)
    row_grads = team.finish_home(grad_near, far_back)
    grad_heads = total(heads_keep, heads_other)
    grad_owt = total(owt_keep, owt_back)

    own_deal = lax.dynamic_slice_in_dim(deal_order[0], team.t * own_blks, own_blks)
    own_len = jnp.where(own_deal // SLOT_BLKS == 0, seq_lengths[0, 0], seq_lengths[0, 1])
    live_blk = (own_deal % SLOT_BLKS) * BLK < own_len
    live = jnp.broadcast_to(live_blk[:, None], (own_blks, BLK)).reshape(own_rows, 1)

    layer_out = jnp.where(live, y_rows, tokens)
    grad_tokens = jnp.where(live, row_grads, cotangent).astype(F32)

    taps = cut_heads(summed[:persist_end])
    rate_rows = jnp.sum(summed[persist_end : persist_end + 3].reshape(3, heads, HP), axis=-1)

    f = head_feats
    return (
        layer_out,
        grad_tokens,
        grad_heads[:f].T,
        grad_heads[f : 2 * f].T,
        grad_heads[2 * f : 3 * f].T,
        grad_heads[3 * f : 4 * f].T,
        grad_owt,
        grad_min,
        grad_mout.T,
        grad_gu[:, :ff],
        grad_gu[:, ff:],
        grad_down.T,
        taps[:KC],
        taps[KC : 2 * KC],
        taps[2 * KC : 3 * KC],
        taps[3 * KC : 3 * KC + NP],
        taps[3 * KC + NP :],
        rate_rows[0],
        rate_rows[1],
        rate_rows[2],
        gains[0],
        gains[1],
    )


def solution(mesh):
    rows = P(("dp", "tensor"), None)
    cols_w, rows_w = P("dp", "tensor"), P("tensor", "dp")
    feats, rate = P(None, "tensor"), P("tensor")
    weights = (cols_w,) * 4 + (rows_w, cols_w, rows_w, cols_w, cols_w, rows_w)
    smalls = (feats,) * 5 + (rate,) * 3
    return jax.shard_map(
        functools.partial(per_device, mesh.shape["dp"], mesh.shape["tensor"]),
        mesh=mesh,
        in_specs=(rows,) + weights + smalls + (P(), P(), P("dp", None), P("dp", None), rows),
        out_specs=(rows, rows) + weights + smalls + (P(), P()),
        check_vma=False,
    )
```
